32 devices in a mesh: groups: 2 (over y), tile: 4 (over z), slab: 2 (over x), batch: 2 (over core).
Axes of the slice: x: 2, y: 2, z: 4, core: 2. Of those that a mesh axis runs over, the one named last changes fastest.
Arguments:
- phase_shift: float32 [4, 1024, 4096], P(('groups', 'slab'), 'tile'), parts along dimension 0, may hold values from -1.5 to 1.5
- absorption: float32 [4, 1024, 4096], P(('groups', 'slab'), 'tile'), parts along dimension 0, may hold values from 0.02 to 0.6
- probe_wave: float32 [2, 256, 256], replicated, may hold values from -6 to 6
- measured: float32 [64, 256, 256], P(('groups', 'tile', 'batch')), parts along dimension 0, may hold values from 0 to 3
- offsets: int32 [64, 2], P(('groups', 'tile', 'batch')), parts along dimension 0, may hold values from 0 to 3840, as said below
Outputs:
- object_gradient: float32 [2, 4, 1024, 4096], P(None, ('groups', 'slab'), 'tile'), parts along dimension 1
The draws below stay inside these ranges and needn't reach their ends.
There are 2 independent parts, one for each index of `groups`. The reference program is written for one: setup_inputs(seed, part) draws one part's arguments, and reference() takes and returns one part's arrays. A program takes and returns all parts, laid end to end along the dimension named above; an argument that names none is the same for every part. Nothing has to cross between parts.
Inputs may be any that keep to these rules, and one draw needn't show every extreme that they name: `offsets`: A position's patch covers rows r to r + 255 and columns c to c + 255 of the object and lies inside it. Positions are listed by row block: the 8 positions of block b (positions b * (8) onward) have b * 256 <= r < (b + 1) * 256.
All inputs are finite; a program needn't handle non-finite values.
Results may differ from the reference program's by a relative error of at most 0.0003.
Values sent between devices are 32-bit elements; how exact they have to be, the bound alone decides.
No kernel may reach another device: no remote copies, remote signals or barrier semaphores. Data moves between devices by JAX's collectives and lax.ppermute only.
A program may use at most 128 MiB of HBM per device.

```python
import math
import jax
import jax.numpy as jnp
from jax import lax

P_SIZE = 256
TR = 256
COLS = 4096
SLICES = 2
ROWS = 1024
POSITIONS = 32


def draw_offsets(key, part):
    blocks = ROWS // TR
    per_block = POSITIONS // blocks
    indices = jnp.arange(POSITIONS, dtype=jnp.int32)
    owner = indices // per_block
    limit = jnp.where(owner == blocks - 1, TR - P_SIZE + 1, TR).astype(jnp.int32)
    key_row, key_col = jax.random.split(key)
    local_row = jax.random.randint(key_row, (POSITIONS,), 0, 1 << 30, dtype=jnp.int32) % limit
    local_row = jnp.where(indices == POSITIONS - 1, TR - P_SIZE, local_row)
    row_offset = owner * TR + local_row
    col_offset = jax.random.randint(key_col, (POSITIONS,), 0, COLS - P_SIZE + 1, dtype=jnp.int32)
    col_offset = jnp.where(indices == 0, COLS - P_SIZE, col_offset)
    col_offset = jnp.where(indices == 1, 0, col_offset)
    return jnp.stack([row_offset, col_offset], axis=1).astype(jnp.int32)


def levels(stream_key, dims, shards, least, largest):
    def one(axis_at, blocks):
        steps = jax.random.uniform(jax.random.fold_in(jax.random.fold_in(stream_key, 6), axis_at), (blocks,), jnp.float32, least / len(shards), largest / len(shards))
        return jnp.repeat(jnp.exp(steps), dims[axis_at] // blocks).reshape((-1,) + (1,) * (len(dims) - axis_at - 1))

    gain = one(*shards[0])
    for cut in shards[1:]:
        gain = gain * one(*cut)
    return gain


def normal_values(own_key, extent, spread, reach, kind=jnp.bfloat16):
    array = jax.random.normal(own_key, extent, jnp.float32) * spread
    return jnp.minimum(jnp.maximum(array, -reach), reach).astype(kind)


def setup_inputs(seed: int = 0, part: int = 0) -> dict:
    arg_keys = jax.random.split(jax.random.key(seed), 6)
    part_splits = jax.random.split(jax.random.fold_in(arg_keys[5], part), 6)
    phase_shift = jnp.clip(jax.random.uniform(part_splits[0], (SLICES, ROWS, COLS), jnp.float32, -1.5, 1.5) * levels(part_splits[0], (SLICES, ROWS, COLS), ((0, 2), (1, 4)), -0.4, 0.0), -1.5, 1.5)
    absorption = jnp.clip(jnp.exp(math.log(0.6) - 3.4011974 * jax.random.uniform(part_splits[1], (SLICES, ROWS, COLS), jnp.float32) ** levels(part_splits[1], (SLICES, ROWS, COLS), ((0, 2), (1, 4)), -0.2, 0.2)), 0.02, 0.6)
    probe_wave = normal_values(arg_keys[2], (2, P_SIZE, P_SIZE), 1.0, 6.0, jnp.float32)
    measured = jnp.clip(3.0 * jax.random.uniform(part_splits[3], (POSITIONS, P_SIZE, P_SIZE), jnp.float32) ** levels(part_splits[3], (POSITIONS, P_SIZE, P_SIZE), ((0, 8),), -0.2, 0.2), 0.0, 3.0)
    offsets = draw_offsets(jax.random.fold_in(jax.random.fold_in(arg_keys[5], part), 71), part)
    return dict(phase_shift=phase_shift, absorption=absorption, probe_wave=probe_wave, measured=measured, offsets=offsets)


def kernel_table(patch_side):
    indices = jnp.arange(patch_side, dtype=jnp.int32)
    wavenumber = jnp.where(indices < patch_side // 2, indices, indices - patch_side)
    quadratic = ((wavenumber * wavenumber) % (8 * patch_side)).astype(jnp.float32)
    angles = (-math.pi / (4.0 * patch_side)) * quadratic
    kernel_line = jnp.cos(angles) + 1j * jnp.sin(angles)
    return kernel_line[:, None] * kernel_line[None, :]


def reference(phase_shift, absorption, probe_wave, measured, offsets):
    kernel = kernel_table(P_SIZE)
    probe_complex = probe_wave[0] + 1j * probe_wave[1]

    def add_position(gradient, inputs):
        offset_pair, amplitude = inputs
        row_start = offset_pair[0].astype(jnp.int32)
        col_start = offset_pair[1].astype(jnp.int32)
        zero_index = jnp.int32(0)
        phase_patch = lax.dynamic_slice(phase_shift, (zero_index, row_start, col_start), (SLICES, P_SIZE, P_SIZE))
        absorb_patch = lax.dynamic_slice(absorption, (zero_index, row_start, col_start), (SLICES, P_SIZE, P_SIZE))
        transmit = jnp.exp(-absorb_patch) * (jnp.cos(phase_patch) + 1j * jnp.sin(phase_patch))
        incoming = []
        wave_now = probe_complex
        for slice_idx in range(SLICES):
            incoming.append(wave_now)
            wave_now = jnp.fft.ifft2(jnp.fft.fft2(wave_now * transmit[slice_idx]) * kernel)
        far_field = jnp.fft.fft2(wave_now) / P_SIZE
        magnitude = jnp.abs(far_field)
        seed_wave = far_field * (1.0 - amplitude / jnp.maximum(magnitude, 0.5))
        adjoint = jnp.fft.ifft2(seed_wave) * P_SIZE
        terms = [None] * SLICES
        for slice_idx in range(SLICES - 1, -1, -1):
            back_wave = jnp.fft.ifft2(jnp.fft.fft2(adjoint) * jnp.conj(kernel))
            terms[slice_idx] = jnp.conj(incoming[slice_idx]) * back_wave
            adjoint = jnp.conj(transmit[slice_idx]) * back_wave
        stacked = jnp.stack(terms)
        parts = jnp.stack([jnp.real(stacked), jnp.imag(stacked)])
        starts = (zero_index, zero_index, row_start, col_start)
        current = lax.dynamic_slice(gradient, starts, (2, SLICES, P_SIZE, P_SIZE))
        gradient = lax.dynamic_update_slice(gradient, current + parts, starts)
        return gradient, None

    initial = jnp.zeros((2, SLICES, ROWS, COLS), jnp.float32)
    gradient, unused = lax.scan(add_position, initial, (offsets, measured))
    return gradient
```

```python
import math

import numpy as np
import jax
import jax.numpy as jnp
from jax import lax
from jax.experimental import pallas as pl
from jax.experimental.pallas import tpu as pltpu
from jax.sharding import PartitionSpec as P

SIN = [(-1.0) ** k / math.factorial(2 * k + 1) for k in range(8)]
COS = [(-1.0) ** k / math.factorial(2 * k) for k in range(8)]


def move(block, axis, distance):
    size = lax.axis_size(axis)
    route = [(i, i + distance) for i in range(size) if 0 <= i + distance < size]
    return lax.ppermute(block, axis, route)


def rotate(block, axis, distance):
    size = lax.axis_size(axis)
    return lax.ppermute(block, axis, [(i, (i + distance) % size) for i in range(size)])


def halves(matrix):
    high = matrix.astype(np.float32).astype(jnp.bfloat16)
    low = (matrix - high.astype(np.float64)).astype(np.float32).astype(jnp.bfloat16)
    return high, low


def right_table(matrix):
    real, imag = halves(matrix.real), halves(matrix.imag)
    minus = halves(-matrix.imag)
    order = lambda pair: [pair[0], pair[1], pair[0]]
    first = np.concatenate(order(real) + order(minus), axis=0)
    second = np.concatenate(order(imag) + order(real), axis=0)
    return np.concatenate([first, second], axis=1)


def left_table(matrix):
    return np.ascontiguousarray(right_table(matrix.T).T)


def tables(side):
    index = np.arange(side)
    fourier = np.exp(-2j * np.pi * (index[:, None] * index[None, :] % side) / side)
    wavenumber = np.where(index < side // 2, index, index - side)
    kernel = np.exp(-1j * np.pi * (wavenumber * wavenumber % (8 * side)) / (4 * side))
    fresnel = (fourier.conj() * kernel[None, :]) @ fourier / side
    scaled = fourier / math.sqrt(side)
    out = []
    for matrix in (fresnel, fresnel.conj(), scaled, scaled.conj()):
        out += [left_table(matrix), right_table(matrix)]
    return out


def split(value):
    high = value.astype(jnp.bfloat16)
    low = (value - high.astype(jnp.float32)).astype(jnp.bfloat16)
    return high, low


def two_sided(left, right, real, imag):
    side = real.shape[-1]
    real_high, real_low = split(real)
    imag_high, imag_low = split(imag)
    wide = jnp.concatenate([real_high, real_high, real_low, imag_high, imag_high, imag_low], axis=1)
    inner = jnp.dot(wide, right[...], preferred_element_type=jnp.float32)
    real_high, real_low = split(inner[:, :side])
    imag_high, imag_low = split(inner[:, side:])
    tall = jnp.concatenate([real_high, real_high, real_low, imag_high, imag_high, imag_low], axis=0)
    outer = jnp.dot(left[...], tall, preferred_element_type=jnp.float32)
    return outer[:side], outer[side:]


def transmission(phase, absorption):
    square = phase * phase
    sine = jnp.full_like(phase, SIN[-1])
    cosine = jnp.full_like(phase, COS[-1])
    for a, b in zip(SIN[-2::-1], COS[-2::-1]):
        sine = sine * square + a
        cosine = cosine * square + b
    damping = jnp.exp(-absorption)
    return damping * cosine, damping * sine * phase


def slot_kernel(sections, scalars, probe, measured, *refs):
    patches = refs[:sections]
    tables_in = refs[sections : sections + 8]
    outs = refs[sections + 8 : 2 * sections + 8]
    wave, trans = refs[2 * sections + 8 :]
    slab, row, col = scalars[0], scalars[1], scalars[2]
    forward_left, forward_right, adjoint_left, adjoint_right = tables_in[:4]
    fourier_left, fourier_right, inverse_left, inverse_right = tables_in[4:]
    for distance in range(sections):
        owner = lax.rem(slab + (sections - distance), sections)
        real, imag = transmission(patches[distance][0], patches[distance][1])
        trans[owner, 0] = real
        trans[owner, 1] = imag
    for part in range(2):
        wave[0, part] = pltpu.roll(pltpu.roll(probe[part], row, 0), col, 1)
    for step in range(sections):
        a, b, c, d = wave[step, 0], wave[step, 1], trans[step, 0], trans[step, 1]
        real, imag = a * c - b * d, a * d + b * c
        if step < sections - 1:
            real, imag = two_sided(forward_left, forward_right, real, imag)
            wave[step + 1, 0] = real
            wave[step + 1, 1] = imag
    real, imag = two_sided(fourier_left, fourier_right, real, imag)
    factor = 1.0 - measured[0] * lax.rsqrt(jnp.maximum(real * real + imag * imag, 0.25))
    real, imag = two_sided(inverse_left, inverse_right, real * factor, imag * factor)
    for step in range(sections - 1, -1, -1):
        a, b = wave[step, 0], wave[step, 1]
        wave[step, 0] = a * real + b * imag
        wave[step, 1] = a * imag - b * real
        if step > 0:
            c, d = trans[step, 0], trans[step, 1]
            real, imag = c * real + d * imag, c * imag - d * real
            real, imag = two_sided(adjoint_left, adjoint_right, real, imag)
    for distance in range(sections):
        outs[distance][...] = wave[lax.rem(slab + distance, sections)]


def run_slot(scalars, probe, measured, index, patches, constants):
    sections = len(patches)
    side = probe.shape[-1]
    whole = pl.BlockSpec(memory_space=pltpu.VMEM)
    shape = jax.ShapeDtypeStruct((2, side, side), jnp.float32)
    return pl.pallas_call(
        lambda scalars, *refs: slot_kernel(sections, scalars, *refs),
        grid_spec=pltpu.PrefetchScalarGridSpec(
            num_scalar_prefetch=1,
            grid=(1,),
            in_specs=[whole, pl.BlockSpec((1, side, side), lambda i, s: (s[3], 0, 0))]
            + [whole] * (sections + 8),
            out_specs=[whole] * sections,
            scratch_shapes=[pltpu.VMEM((sections, 2, side, side), jnp.float32)] * 2,
        ),
        out_shape=[shape] * sections,
        compiler_params=pltpu.CompilerParams(vmem_limit_bytes=50 << 20),
    )(jnp.concatenate([scalars, index[None]]), probe, measured, *patches, *constants)


def cut_kernel(count, side, scalars, phase, absorption, *refs):
    outs = refs[:count]
    buffer, sems = refs[count:]
    copies = []
    for k in range(count):
        for which, source in enumerate((phase, absorption)):
            for half in range(2):
                start = pl.multiple_of(scalars[3 * k + half] * side, side)
                copies.append(
                    pltpu.make_async_copy(
                        source.at[0, :, pl.ds(start, side)],
                        buffer.at[k, which, half],
                        sems.at[k, which, half],
                    )
                )
    for copy in copies:
        copy.start()
    lane = lax.broadcasted_iota(jnp.int32, (side, side), 1)
    for k in range(count):
        own = lane >= scalars[3 * k + 2]
        for which in range(2):
            for half in range(2):
                copies[4 * k + 2 * which + half].wait()
            outs[k][which] = jnp.where(own, buffer[k, which, 0], buffer[k, which, 1])


def cut(cols, phase, absorption, side):
    count = cols.shape[0]
    blocks = phase.shape[-1] // side
    first = cols // side
    scalars = jnp.stack([first, jnp.minimum(first + 1, blocks - 1), cols % side], axis=1)
    shape = jax.ShapeDtypeStruct((2, side, side), jnp.float32)
    return pl.pallas_call(
        lambda *refs: cut_kernel(count, side, *refs),
        in_specs=[
            pl.BlockSpec(memory_space=pltpu.SMEM),
            pl.BlockSpec(memory_space=pl.ANY),
            pl.BlockSpec(memory_space=pl.ANY),
        ],
        out_specs=[pl.BlockSpec(memory_space=pltpu.VMEM)] * count,
        out_shape=[shape] * count,
        scratch_shapes=[
            pltpu.VMEM((count, 2, 2, side, side), jnp.float32),
            pltpu.SemaphoreType.DMA((count, 2, 2)),
        ],
        compiler_params=pltpu.CompilerParams(vmem_limit_bytes=50 << 20),
    )(scalars.reshape(-1), phase, absorption)


def gather_kernel(count, side, blocks, scalars, *refs):
    terms, out = refs[:count], refs[count]
    block = pl.program_id(0)
    out[...] = jnp.zeros_like(out)
    rows = lax.broadcasted_iota(jnp.int32, (side, side), 0)
    lane = lax.broadcasted_iota(jnp.int32, (side, side), 1)
    for k in range(count):
        first, col = scalars[4 * k], scalars[4 * k + 1]
        low, high = scalars[4 * k + 2], scalars[4 * k + 3]
        for half in range(2):

            @pl.when((first + half == block) & (high > low))
            def _():
                keep = (rows >= low) & (rows < high)
                keep = keep & ((lane < col) if half else (lane >= col))
                for part in range(2):
                    out[part, 0] += jnp.where(keep, terms[k][part], 0.0)


def gather_terms(terms, scalars, cols_total):
    count = len(terms)
    side = terms[0].shape[-1]
    blocks = cols_total // side
    return pl.pallas_call(
        lambda *refs: gather_kernel(count, side, blocks, *refs),
        grid_spec=pltpu.PrefetchScalarGridSpec(
            num_scalar_prefetch=1,
            grid=(blocks,),
            in_specs=[pl.BlockSpec(memory_space=pltpu.VMEM)] * count,
            out_specs=pl.BlockSpec((2, 1, side, side), lambda i, s: (0, 0, 0, i)),
        ),
        out_shape=jax.ShapeDtypeStruct((2, 1, side, cols_total), jnp.float32),
        compiler_params=pltpu.CompilerParams(vmem_limit_bytes=50 << 20),
    )(scalars.reshape(-1), *terms)


def local(phase, absorption, probe, measured, offsets):
    side = probe.shape[-1]
    cols_total = phase.shape[2]
    sections = lax.axis_size("slab")
    slab = lax.axis_index("slab")
    tile = lax.axis_index("tile")
    last = tile == lax.axis_size("tile") - 1
    each = offsets.shape[0] // sections
    n_up = each // 2
    n_here = each - n_up
    constants = [jnp.asarray(table) for table in tables(side)]

    below = move(offsets, "tile", 1)

    def here_index(k, owner):
        return owner * n_here + k

    def up_index(k, owner):
        return sections * n_here + owner * n_up + k

    def peer(distance):
        return (slab + distance) % sections

    def shifts(pair):
        return pair[0] % side, pair[1] % side

    def pick(table, index):
        return lax.dynamic_index_in_dim(table, index, 0, keepdims=False)

    distances = list(range(sections))
    here_ids = [[here_index(k, peer(d)) for d in distances] for k in range(n_here)]
    up_ids = [[up_index(k, peer(d)) for d in distances] for k in range(n_up)]
    flat = lambda lists: [i for row in lists for i in row]
    own_ids = flat(here_ids) + flat(up_ids)
    own_pairs = offsets[jnp.stack(own_ids)]
    low_pairs = below[jnp.stack(own_ids)]
    own_cut = cut(own_pairs[:, 1], phase, absorption, side)
    low_cut = cut(low_pairs[:, 1], phase, absorption, side)
    rows = lax.broadcasted_iota(jnp.int32, (1, side, 1), 1)

    def exchange(items):
        return [items[0]] + [rotate(items[d], "slab", d) for d in distances[1:]]

    terms, spans = [], []

    def add(term, pair, low, high):
        terms.append(term)
        spans.append(jnp.stack([pair[1] // side, pair[1] % side, low, high]))

    full = jnp.int32(side)
    none = jnp.int32(0)

    def slot(patches, pair, measured_in, index):
        row, col = shifts(pair)
        got = exchange(patches)
        outs = run_slot(jnp.stack([slab, row, col]), probe, measured_in, index, got, constants)
        return exchange(outs)

    for k in range(n_here):
        patches = []
        for d in distances:
            position = k * sections + d
            upper = move(low_cut[position], "tile", -1)
            row = own_pairs[position, 0] % side
            patches.append(jnp.where(rows >= row, own_cut[position], upper))
        done = slot(patches, own_pairs[k * sections], measured, here_ids[k][0])
        for d in distances:
            position = k * sections + (sections - d) % sections
            row = own_pairs[position, 0] % side
            add(done[d], own_pairs[position], row, full)
            low_row = low_pairs[position, 0] % side
            add(move(done[d], "tile", 1), low_pairs[position], none, low_row)
    for k in range(n_up):
        patches = []
        base = n_here * sections + k * sections
        for d in distances:
            lower = move(own_cut[base + d], "tile", 1)
            row = low_pairs[base + d, 0] % side
            patches.append(jnp.where(rows >= row, lower, low_cut[base + d]))
        sent = move(pick(measured, up_ids[k][0]), "tile", 1)
        done = slot(patches, low_pairs[base], sent[None], none)
        for d in distances:
            position = base + (sections - d) % sections
            add(done[d], low_pairs[position], none, low_pairs[position, 0] % side)
            row = jnp.where(last, full, own_pairs[position, 0] % side)
            add(move(done[d], "tile", -1), own_pairs[position], row, full)
        done = slot([own_cut[base + d] for d in distances], own_pairs[base], measured, up_ids[k][0])
        for d in distances:
            position = base + (sections - d) % sections
            row = jnp.where(last, own_pairs[position, 0] % side, full)
            add(done[d], own_pairs[position], row, full)

    spans = jnp.stack(spans)
    other_spans = rotate(spans, "batch", 1)
    other_terms = [rotate(term, "batch", 1) for term in terms]
    return gather_terms(terms + other_terms, jnp.concatenate([spans, other_spans]), cols_total)


def solution(mesh):
    in_specs = (
        P(("groups", "slab"), "tile", None),
        P(("groups", "slab"), "tile", None),
        P(),
        P(("groups", "tile", "batch"), None, None),
        P(("groups", "tile", "batch"), None),
    )
    out_specs = P(None, ("groups", "slab"), "tile", None)
    return jax.shard_map(local, mesh=mesh, in_specs=in_specs, out_specs=out_specs, check_vma=False)
```

```python
import math

import numpy as np
import jax
import jax.numpy as jnp
from jax import lax
from jax.experimental import pallas as pl
from jax.experimental.pallas import tpu as pltpu
from jax.sharding import PartitionSpec as P

SIN = [(-1.0) ** k / math.factorial(2 * k + 1) for k in range(8)]
COS = [(-1.0) ** k / math.factorial(2 * k) for k in range(8)]
VMEM = pl.BlockSpec(memory_space=pltpu.VMEM)
SMEM = pl.BlockSpec(memory_space=pltpu.SMEM)
ANY = pl.BlockSpec(memory_space=pl.ANY)


def params(mib):
    return pltpu.CompilerParams(vmem_limit_bytes=mib << 20)


def move(block, axis, distance):
    size = lax.axis_size(axis)
    route = [(i, i + distance) for i in range(size) if 0 <= i + distance < size]
    return lax.ppermute(block, axis, route)


def rotate(block, axis, distance):
    size = lax.axis_size(axis)
    return lax.ppermute(block, axis, [(i, (i + distance) % size) for i in range(size)])


def rotate_last(block, distance):
    tiles, size = lax.axis_size("tile"), lax.axis_size("slab")
    base = (tiles - 1) * size
    route = [(base + i, base + (i + distance) % size) for i in range(size)]
    return lax.ppermute(block, ("tile", "slab"), route)


def halves(matrix):
    high = matrix.astype(np.float32).astype(jnp.bfloat16)
    low = (matrix - high.astype(np.float64)).astype(np.float32).astype(jnp.bfloat16)
    return [high, low]


def compact_tables(side):
    index = np.arange(side)
    fourier = np.exp(-2j * np.pi * (index[:, None] * index[None, :] % side) / side)
    wavenumber = np.where(index < side // 2, index, index - side)
    kernel = np.exp(-1j * np.pi * (wavenumber * wavenumber % (8 * side)) / (4 * side))
    line = np.fft.ifft(kernel)
    line = (line + line[-index % side]) / 2
    fresnel = line[(index[:, None] - index[None, :]) % side]
    scaled = fourier / math.sqrt(side)
    pieces = []
    for matrix in (fresnel, scaled):
        pieces += halves(matrix.real) + halves(matrix.imag)
    return np.stack(pieces)


def expand_kernel(pieces, *outs):
    side = pieces.shape[-1]
    for which in range(2):
        left, right = outs[2 * which], outs[2 * which + 1]
        real_high, real_low, imag_high, imag_low = [pieces[4 * which + k] for k in range(4)]
        real = [real_high, real_low, real_high]
        imag = [imag_high, imag_low, imag_high]
        minus = [-imag_high, -imag_low, -imag_high]
        for column, blocks in enumerate((real + minus, imag + real)):
            for row, block in enumerate(blocks):
                rows, cols = pl.ds(row * side, side), pl.ds(column * side, side)
                right[rows, cols] = block
                left[cols, rows] = block


def expand(side):
    pieces = jnp.asarray(compact_tables(side))
    left = jax.ShapeDtypeStruct((2 * side, 6 * side), jnp.bfloat16)
    right = jax.ShapeDtypeStruct((6 * side, 2 * side), jnp.bfloat16)
    return pl.pallas_call(
        expand_kernel,
        in_specs=[VMEM],
        out_specs=[VMEM] * 4,
        out_shape=[left, right, left, right],
        compiler_params=params(16),
        name="expand",
    )(pieces)


def split(value):
    high = value.astype(jnp.bfloat16)
    low = (value - high.astype(jnp.float32)).astype(jnp.bfloat16)
    return high, low


def two_sided(left, right, real, imag):
    side = real.shape[-1]
    real_high, real_low = split(real)
    imag_high, imag_low = split(imag)
    wide = jnp.concatenate([real_high, real_high, real_low, imag_high, imag_high, imag_low], axis=1)
    inner = jnp.dot(wide, right[...], preferred_element_type=jnp.float32)
    real_high, real_low = split(inner[:, :side])
    imag_high, imag_low = split(inner[:, side:])
    tall = jnp.concatenate([real_high, real_high, real_low, imag_high, imag_high, imag_low], axis=0)
    outer = jnp.dot(left[...], tall, preferred_element_type=jnp.float32)
    return outer[:side], outer[side:]


def transmission(phase, absorption):
    square = phase * phase
    sine = jnp.full_like(phase, SIN[-1])
    cosine = jnp.full_like(phase, COS[-1])
    for a, b in zip(SIN[-2::-1], COS[-2::-1]):
        sine = sine * square + a
        cosine = cosine * square + b
    damping = jnp.exp(-absorption)
    return damping * cosine, damping * sine * phase


def slot_kernel(kind, base, each, sections, pairs, probe, measured, *refs):
    pieces = 1 if kind == "last" else 2
    own = refs[:pieces]
    others = refs[pieces : pieces + sections - 1]
    refs = refs[pieces + sections - 1 :]
    prop_left, prop_right, dft_left, dft_right = refs[:4]
    outs = refs[4 : 4 + sections]
    wave, trans = refs[4 + sections : 6 + sections]
    side = probe.shape[-1]
    slab = lax.axis_index("slab")
    index = base + slab * each
    row = lax.rem(pairs[0, index], side)
    col = lax.rem(pairs[1, index], side)
    if kind == "up":
        amplitude = measured
        fetch = None
    else:
        amplitude, sem = refs[6 + sections :]
        fetch = pltpu.make_async_copy(measured.at[index], amplitude, sem)
        fetch.start()
    rows = lax.broadcasted_iota(jnp.int32, (side, side), 0)
    patch = [own[0][0], own[0][1]]
    if pieces == 2:
        patch = [jnp.where(rows >= row, own[0][k], own[1][k]) for k in range(2)]
    trans[slab, 0], trans[slab, 1] = transmission(patch[0], patch[1])
    for distance in range(1, sections):
        owner = lax.rem(slab + (sections - distance), sections)
        real, imag = transmission(others[distance - 1][0], others[distance - 1][1])
        trans[owner, 0] = real
        trans[owner, 1] = imag
    for part in range(2):
        wave[0, part] = pltpu.roll(pltpu.roll(probe[part], row, 0), col, 1)
    for step in range(sections):
        a, b, c, d = wave[step, 0], wave[step, 1], trans[step, 0], trans[step, 1]
        real, imag = a * c - b * d, a * d + b * c
        if step < sections - 1:
            real, imag = two_sided(prop_left, prop_right, real, imag)
            wave[step + 1, 0] = real
            wave[step + 1, 1] = imag
    real, imag = two_sided(dft_left, dft_right, real, imag)
    if fetch is not None:
        fetch.wait()
    factor = 1.0 - amplitude[...] * lax.rsqrt(jnp.maximum(real * real + imag * imag, 0.25))
    real, minus = two_sided(dft_left, dft_right, real * factor, -imag * factor)
    for step in range(sections - 1, -1, -1):
        a, b = wave[step, 0], wave[step, 1]
        wave[step, 0] = a * real - b * minus
        wave[step, 1] = -(a * minus + b * real)
        if step > 0:
            c, d = trans[step, 0], trans[step, 1]
            real, minus = c * real - d * minus, c * minus + d * real
            real, minus = two_sided(prop_left, prop_right, real, minus)
    for distance in range(sections):
        outs[distance][...] = wave[lax.rem(slab + distance, sections)]


def run_slot(kind, base, each, pairs, probe, measured, own, others, constants):
    sections = len(others) + 1
    side = probe.shape[-1]
    shape = jax.ShapeDtypeStruct((2, side, side), jnp.float32)
    scratch = [pltpu.VMEM((sections, 2, side, side), jnp.float32)] * 2
    if kind != "up":
        scratch += [pltpu.VMEM((side, side), jnp.float32), pltpu.SemaphoreType.DMA(())]
    return pl.pallas_call(
        lambda *refs: slot_kernel(kind, base, each, sections, *refs),
        in_specs=[SMEM, VMEM, VMEM if kind == "up" else ANY]
        + [VMEM] * (len(own) + len(others) + 4),
        out_specs=[VMEM] * sections,
        out_shape=[shape] * sections,
        scratch_shapes=scratch,
        compiler_params=params(32),
        name="slot_" + kind,
    )(pairs, probe, measured, *own, *others, *constants)


def position(k, bases, slab, sections):
    base, each, distance = bases[k]
    return base + lax.rem(slab + distance, sections) * each


def cut_kernel(bases, sections, send, pairs, phase, absorption, *refs):
    count = len(bases)
    side = phase.shape[1]
    blocks = phase.shape[2] // side
    slab = lax.axis_index("slab")
    if send is not None:
        measured, refs = refs[0], refs[1:]
    outs = refs[:count]
    buffer, sems = refs[-2], refs[-1]
    copies, columns = [], []
    for k in range(count):
        column = pairs[1, position(k, bases, slab, sections)]
        first = lax.div(column, side)
        columns.append(lax.rem(column, side))
        for which, source in enumerate((phase, absorption)):
            for half in range(2):
                block = first if half == 0 else jnp.minimum(first + 1, blocks - 1)
                copies.append(
                    pltpu.make_async_copy(
                        source.at[0, :, pl.ds(pl.multiple_of(block * side, side), side)],
                        buffer.at[k, which, half],
                        sems.at[k, which, half],
                    )
                )
    for copy in copies:
        copy.start()
    if send is not None:
        index = send[0] + slab * send[1]
        extra = pltpu.make_async_copy(measured.at[index], refs[count], refs[-3])
        extra.start()
    lane = lax.broadcasted_iota(jnp.int32, (side, side), 1)
    for k in range(count):
        own = lane >= columns[k]
        for which in range(2):
            for half in range(2):
                copies[4 * k + 2 * which + half].wait()
            outs[k][which] = jnp.where(own, buffer[k, which, 0], buffer[k, which, 1])
    if send is not None:
        extra.wait()


def cut(bases, pairs, phase, absorption, measured=None, send=None):
    side = phase.shape[1]
    count = len(bases)
    sections = lax.axis_size("slab")
    shape = jax.ShapeDtypeStruct((2, side, side), jnp.float32)
    shapes = [shape] * count
    scratch = [
        pltpu.VMEM((count, 2, 2, side, side), jnp.float32),
        pltpu.SemaphoreType.DMA((count, 2, 2)),
    ]
    inputs = [pairs, phase, absorption]
    if send is not None:
        shapes = shapes + [jax.ShapeDtypeStruct((side, side), jnp.float32)]
        scratch = [pltpu.SemaphoreType.DMA(())] + scratch
        inputs.append(measured)
    return pl.pallas_call(
        lambda *refs: cut_kernel(bases, sections, send, *refs),
        in_specs=[SMEM] + [ANY] * (len(inputs) - 1),
        out_specs=[VMEM] * len(shapes),
        out_shape=shapes,
        scratch_shapes=scratch,
        compiler_params=params(16),
        name="cut",
    )(*inputs)


def join_kernel(bases, sections, pairs, here, there, out):
    side = out.shape[-1]
    slab = lax.axis_index("slab")
    row = lax.rem(pairs[0, position(0, bases, slab, sections)], side)
    rows = lax.broadcasted_iota(jnp.int32, (side, side), 0)
    for part in range(2):
        out[part] = jnp.where(rows >= row, here[part], there[part])


def join(base, pairs, here, there):
    sections = lax.axis_size("slab")
    return pl.pallas_call(
        lambda *refs: join_kernel([base], sections, *refs),
        in_specs=[SMEM, VMEM, VMEM],
        out_specs=VMEM,
        out_shape=jax.ShapeDtypeStruct(here.shape, jnp.float32),
        compiler_params=params(8),
        name="join",
    )(pairs, here, there)


def spans(metas, tables, side, sections):
    slab = lax.axis_index("slab")
    last = lax.axis_index("tile") == lax.axis_size("tile") - 1
    out = []
    for source, base, mode in metas:
        index = position(0, [base], slab, sections)
        row, col = tables[source][0, index], tables[source][1, index]
        row = lax.rem(row, side)
        low, high = row, jnp.int32(side)
        if mode == "below":
            low, high = jnp.int32(0), row
        elif mode == "last":
            low = jnp.where(last, row, side)
        elif mode == "inner":
            low = jnp.where(last, side, row)
        out.append((lax.div(col, side), lax.rem(col, side), low, high))
    return out


def early_kernel(metas, sections, *refs):
    count = len(metas)
    tables, terms, out = refs[:4], refs[4 : 4 + count], refs[4 + count]
    side = terms[0].shape[-1]
    blocks = out.shape[-1] // side
    rows = lax.broadcasted_iota(jnp.int32, (side, side), 0)
    lane = lax.broadcasted_iota(jnp.int32, (side, side), 1)

    @pl.loop(0, blocks)
    def _(block):
        out[:, :, pl.ds(pl.multiple_of(block * side, side), side)] = jnp.zeros((2, side, side), jnp.float32)

    for k, (first, col, low, high) in enumerate(spans(metas, tables, side, sections)):
        for half in range(2):
            block = first + half

            @pl.when((block < blocks) & (high > low))
            def _():
                keep = (rows >= low) & (rows < high)
                keep = keep & ((lane < col) if half else (lane >= col))
                place = pl.ds(pl.multiple_of(block * side, side), side)
                for part in range(2):
                    out[part, :, place] += jnp.where(keep, terms[k][part], 0.0)


def early(metas, tables, terms, cols_total):
    side = terms[0].shape[-1]
    sections = lax.axis_size("slab")
    return pl.pallas_call(
        lambda *refs: early_kernel(metas, sections, *refs),
        in_specs=[SMEM] * 4 + [VMEM] * len(terms),
        out_specs=VMEM,
        out_shape=jax.ShapeDtypeStruct((2, side, cols_total), jnp.float32),
        compiler_params=params(20),
        name="early",
    )(*tables, *terms)


def late_kernel(metas, sections, *refs):
    count = len(metas)
    tables, total, terms = refs[:4], refs[4], refs[5 : 5 + count]
    out, stage, sems = refs[5 + count :]
    side = terms[0].shape[-1]
    blocks = out.shape[-1] // side
    rows = lax.broadcasted_iota(jnp.int32, (side, side), 0)
    lane = lax.broadcasted_iota(jnp.int32, (side, side), 1)
    ranges = spans(metas, tables, side, sections)

    def send(block):
        place = pl.ds(pl.multiple_of(block * side, side), side)
        return pltpu.make_async_copy(stage.at[:, :, place], out.at[:, 0, :, place], sems.at[block])

    @pl.loop(0, blocks)
    def _(block):
        place = pl.ds(pl.multiple_of(block * side, side), side)
        stage[:, :, place] = total[:, :, place]
        for k, (first, col, low, high) in enumerate(ranges):
            for half in range(2):

                @pl.when((first + half == block) & (high > low))
                def _():
                    keep = (rows >= low) & (rows < high)
                    keep = keep & ((lane < col) if half else (lane >= col))
                    for part in range(2):
                        stage[part, :, place] += jnp.where(keep, terms[k][part], 0.0)

        send(block).start()

    @pl.loop(0, blocks)
    def _(block):
        send(block).wait()


def late(metas, tables, total, terms):
    side = terms[0].shape[-1]
    cols_total = total.shape[-1]
    sections = lax.axis_size("slab")
    return pl.pallas_call(
        lambda *refs: late_kernel(metas, sections, *refs),
        in_specs=[SMEM] * 4 + [VMEM] * (1 + len(terms)),
        out_specs=ANY,
        out_shape=jax.ShapeDtypeStruct((2, 1, side, cols_total), jnp.float32),
        scratch_shapes=[
            pltpu.VMEM((2, side, cols_total), jnp.float32),
            pltpu.SemaphoreType.DMA((cols_total // side,)),
        ],
        compiler_params=params(28),
        name="late",
    )(*tables, total, *terms)


def local(phase, absorption, probe, measured, offsets):
    side = probe.shape[-1]
    cols_total = phase.shape[2]
    sections = lax.axis_size("slab")
    each = offsets.shape[0] // sections
    n_up = each // 2
    n_here = each - n_up
    distances = list(range(sections))

    pairs = offsets.T
    below = move(pairs, "tile", 1)
    here = lambda k, d: (k, n_here, d)
    up = lambda k, d: (sections * n_here + k, n_up, d)
    back = lambda d: (sections - d) % sections

    lower, amplitude = [], []
    for k in range(n_up):
        *cuts, send = cut(
            [up(k, d) for d in distances], pairs, phase, absorption, measured, (up(k, 0)[0], n_up)
        )
        lower.append(cuts)
        amplitude.append(send)
    raised = [[None] * sections for k in range(n_up)]
    extra = [[None] * sections for k in range(n_up)]
    for k in range(n_up):
        for d in distances[1:] + [0]:
            raised[k][d] = move(lower[k][d], "tile", 1)
            extra[k][d] = rotate_last(lower[k][d], d) if d else None
    amplitude = [move(value, "tile", 1) for value in amplitude]
    low_cuts = [cut([here(k, d) for d in distances], below, phase, absorption) for k in range(n_here)]
    lowered = [[None] * sections for k in range(n_here)]
    for k in range(n_here):
        for d in distances[1:] + [0]:
            lowered[k][d] = move(low_cuts[k][d], "tile", -1)
    constants = expand(side)
    up_cuts = [cut([up(k, d) for d in distances], below, phase, absorption) for k in range(n_up)]
    own_cuts = [cut([here(k, d) for d in distances], pairs, phase, absorption) for k in range(n_here)]

    mine, metas = [], []
    final, final_metas = [], []
    tables = [pairs, below, rotate(pairs, "batch", 1), rotate(below, "batch", 1)]

    def add(term, source, base, mode, is_final=False):
        for other in range(2):
            value = rotate(term, "batch", 1) if other else term
            (final if is_final else mine).append(value)
            (final_metas if is_final else metas).append((source + 2 * other, base, mode))

    for k in range(n_up):
        others = extra[k][1:]
        done = run_slot(
            "last", up(k, 0)[0], n_up, pairs, probe, measured, [lower[k][0]], others, constants
        )
        for d in distances:
            value = rotate_last(done[d], d) if d else done[d]
            add(value, 0, up(k, back(d)), "last")
    for k in range(n_up):
        others = [
            rotate(join(up(k, d), below, raised[k][d], up_cuts[k][d]), "slab", d)
            for d in distances[1:]
        ]
        done = run_slot(
            "up", up(k, 0)[0], n_up, below, probe, amplitude[k],
            [raised[k][0], up_cuts[k][0]], others, constants,
        )
        for d in distances:
            value = rotate(done[d], "slab", d) if d else done[d]
            add(value, 1, up(k, back(d)), "below")
            add(move(value, "tile", -1), 0, up(k, back(d)), "inner", d > 0)
    for k in range(n_here):
        others = [
            rotate(join(here(k, d), pairs, own_cuts[k][d], lowered[k][d]), "slab", d)
            for d in distances[1:]
        ]
        done = run_slot(
            "here", here(k, 0)[0], n_here, pairs, probe, measured,
            [own_cuts[k][0], lowered[k][0]], others, constants,
        )
        for d in distances:
            value = rotate(done[d], "slab", d) if d else done[d]
            add(value, 0, here(k, back(d)), "above", d > 0)
            add(move(value, "tile", 1), 1, here(k, back(d)), "below", True)
    total = early(metas, tables, mine, cols_total)
    return late(final_metas, tables, total, final)


def solution(mesh):
    in_specs = (
        P(("groups", "slab"), "tile", None),
        P(("groups", "slab"), "tile", None),
        P(),
        P(("groups", "tile", "batch"), None, None),
        P(("groups", "tile", "batch"), None),
    )
    out_specs = P(None, ("groups", "slab"), "tile", None)
    return jax.shard_map(local, mesh=mesh, in_specs=in_specs, out_specs=out_specs, check_vma=False)
```

```python
import math

import numpy as np
import jax
import jax.numpy as jnp
from jax import lax
from jax.experimental import pallas as pl
from jax.experimental.pallas import tpu as pltpu
from jax.sharding import PartitionSpec as P

SIN = [(-1.0) ** k / math.factorial(2 * k + 1) for k in range(8)]
COS = [(-1.0) ** k / math.factorial(2 * k) for k in range(8)]
VMEM = pl.BlockSpec(memory_space=pltpu.VMEM)
SMEM = pl.BlockSpec(memory_space=pltpu.SMEM)
HBM = pl.BlockSpec(memory_space=pltpu.HBM)


def params(mib):
    return pltpu.CompilerParams(vmem_limit_bytes=mib << 20)


def cost(microseconds):
    return pl.CostEstimate(flops=int(microseconds * 1e9), transcendentals=0, bytes_accessed=0)


def after(value, *others):
    return lax.optimization_barrier((value, *others))[0]


def move(block, axis, distance):
    size = lax.axis_size(axis)
    route = [(i, i + distance) for i in range(size) if 0 <= i + distance < size]
    return lax.ppermute(block, axis, route)


def rotate(block, axis, distance):
    size = lax.axis_size(axis)
    return lax.ppermute(block, axis, [(i, (i + distance) % size) for i in range(size)])


def rotate_last(block, distance):
    tiles, size = lax.axis_size("tile"), lax.axis_size("slab")
    base = (tiles - 1) * size
    route = [(base + i, base + (i + distance) % size) for i in range(size)]
    return lax.ppermute(block, ("tile", "slab"), route)


def halves(matrix):
    high = matrix.astype(np.float32).astype(jnp.bfloat16)
    low = (matrix - high.astype(np.float64)).astype(np.float32).astype(jnp.bfloat16)
    return [high, low]


def compact_tables(side):
    index = np.arange(side)
    fourier = np.exp(-2j * np.pi * (index[:, None] * index[None, :] % side) / side)
    wavenumber = np.where(index < side // 2, index, index - side)
    kernel = np.exp(-1j * np.pi * (wavenumber * wavenumber % (8 * side)) / (4 * side))
    line = np.fft.ifft(kernel)
    line = (line + line[-index % side]) / 2
    fresnel = line[(index[:, None] - index[None, :]) % side]
    scaled = fourier / math.sqrt(side)
    pieces = []
    for matrix in (fresnel, scaled):
        pieces += halves(matrix.real) + halves(matrix.imag)
    return np.stack(pieces)


def expand_kernel(pieces, *outs):
    side = pieces.shape[-1]
    for which in range(2):
        left, right = outs[2 * which], outs[2 * which + 1]
        real_high, real_low, imag_high, imag_low = [pieces[4 * which + k] for k in range(4)]
        real = [real_high, real_low, real_high]
        imag = [imag_high, imag_low, imag_high]
        minus = [-imag_high, -imag_low, -imag_high]
        for column, blocks in enumerate((real + minus, imag + real)):
            for row, block in enumerate(blocks):
                rows, cols = pl.ds(row * side, side), pl.ds(column * side, side)
                right[rows, cols] = block
                left[cols, rows] = block


def expand(side):
    pieces = jnp.asarray(compact_tables(side))
    left = jax.ShapeDtypeStruct((2 * side, 6 * side), jnp.bfloat16)
    right = jax.ShapeDtypeStruct((6 * side, 2 * side), jnp.bfloat16)
    return pl.pallas_call(
        expand_kernel,
        in_specs=[VMEM],
        out_specs=[VMEM] * 4,
        out_shape=[left, right, left, right],
        compiler_params=params(16),
        name="expand",
    )(pieces)


def split(value):
    high = value.astype(jnp.bfloat16)
    low = (value - high.astype(jnp.float32)).astype(jnp.bfloat16)
    return high, low


def two_sided(left, right, real, imag):
    side = real.shape[-1]
    real_high, real_low = split(real)
    imag_high, imag_low = split(imag)
    wide = jnp.concatenate([real_high, real_high, real_low, imag_high, imag_high, imag_low], axis=1)
    inner = jnp.dot(wide, right[...], preferred_element_type=jnp.float32)
    real_high, real_low = split(inner[:, :side])
    imag_high, imag_low = split(inner[:, side:])
    tall = jnp.concatenate([real_high, real_high, real_low, imag_high, imag_high, imag_low], axis=0)
    outer = jnp.dot(left[...], tall, preferred_element_type=jnp.float32)
    return outer[:side], outer[side:]


def transmission(phase, absorption):
    square = phase * phase
    sine = jnp.full_like(phase, SIN[-1])
    cosine = jnp.full_like(phase, COS[-1])
    for a, b in zip(SIN[-2::-1], COS[-2::-1]):
        sine = sine * square + a
        cosine = cosine * square + b
    damping = jnp.exp(-absorption)
    return damping * cosine, damping * sine * phase


def slot_kernel(kind, *args):
    if kind == "last":

        @pl.when(lax.axis_index("tile") == lax.axis_size("tile") - 1)
        def _():
            slot_body(kind, *args)
    else:
        slot_body(kind, *args)


def slot_body(kind, base, each, sections, pairs, probe, measured, *refs):
    pieces = 1 if kind == "last" else 2
    own = refs[:pieces]
    others = refs[pieces : pieces + sections - 1]
    refs = refs[pieces + sections - 1 :]
    prop_left, prop_right, dft_left, dft_right = refs[:4]
    outs = refs[4 : 4 + sections]
    wave, trans = refs[4 + sections : 6 + sections]
    side = probe.shape[-1]
    slab = lax.axis_index("slab")
    index = base + slab * each
    row = lax.rem(pairs[0, index], side)
    col = lax.rem(pairs[1, index], side)
    if kind == "up":
        amplitude = measured
        fetch = None
    else:
        amplitude, sem = refs[6 + sections :]
        fetch = pltpu.make_async_copy(measured.at[index], amplitude, sem)
        fetch.start()
    rows = lax.broadcasted_iota(jnp.int32, (side, side), 0)
    patch = [own[0][0], own[0][1]]
    if pieces == 2:
        patch = [jnp.where(rows >= row, own[0][k], own[1][k]) for k in range(2)]
    trans[slab, 0], trans[slab, 1] = transmission(patch[0], patch[1])
    for distance in range(1, sections):
        owner = lax.rem(slab + (sections - distance), sections)
        real, imag = transmission(others[distance - 1][0], others[distance - 1][1])
        trans[owner, 0] = real
        trans[owner, 1] = imag
    for part in range(2):
        wave[0, part] = pltpu.roll(pltpu.roll(probe[part], row, 0), col, 1)
    for step in range(sections):
        a, b, c, d = wave[step, 0], wave[step, 1], trans[step, 0], trans[step, 1]
        real, imag = a * c - b * d, a * d + b * c
        if step < sections - 1:
            real, imag = two_sided(prop_left, prop_right, real, imag)
            wave[step + 1, 0] = real
            wave[step + 1, 1] = imag
    real, imag = two_sided(dft_left, dft_right, real, imag)
    if fetch is not None:
        fetch.wait()
    factor = 1.0 - amplitude[...] * lax.rsqrt(jnp.maximum(real * real + imag * imag, 0.25))
    real, minus = two_sided(dft_left, dft_right, real * factor, -imag * factor)
    for step in range(sections - 1, -1, -1):
        a, b = wave[step, 0], wave[step, 1]
        wave[step, 0] = a * real - b * minus
        wave[step, 1] = -(a * minus + b * real)
        if step > 0:
            c, d = trans[step, 0], trans[step, 1]
            real, minus = c * real - d * minus, c * minus + d * real
            real, minus = two_sided(prop_left, prop_right, real, minus)
    for distance in range(sections):
        outs[distance][...] = wave[lax.rem(slab + distance, sections)]


def run_slot(kind, base, each, pairs, probe, measured, own, others, constants):
    sections = len(others) + 1
    side = probe.shape[-1]
    shape = jax.ShapeDtypeStruct((2, side, side), jnp.float32)
    scratch = [pltpu.VMEM((sections, 2, side, side), jnp.float32)] * 2
    if kind != "up":
        scratch += [pltpu.VMEM((side, side), jnp.float32), pltpu.SemaphoreType.DMA(())]
    return pl.pallas_call(
        lambda *refs: slot_kernel(kind, base, each, sections, *refs),
        in_specs=[SMEM, VMEM, VMEM if kind == "up" else HBM]
        + [VMEM] * (len(own) + len(others) + 4),
        out_specs=[VMEM] * sections,
        out_shape=[shape] * sections,
        scratch_shapes=scratch,
        compiler_params=params(32),
        name="slot_" + kind,
    )(pairs, probe, measured, *own, *others, *constants)


def position(k, bases, slab, sections):
    base, each, distance = bases[k]
    return base + lax.rem(slab + distance, sections) * each


def cut_kernel(bases, sections, send, pairs, phase, absorption, *refs):
    count = len(bases)
    side = phase.shape[1]
    blocks = phase.shape[2] // side
    slab = lax.axis_index("slab")
    if send is not None:
        measured, refs = refs[0], refs[1:]
    outs = refs[:count]
    buffer, sems = refs[-2], refs[-1]
    copies, columns = [], []
    for k in range(count):
        column = pairs[1, position(k, bases, slab, sections)]
        first = lax.div(column, side)
        columns.append(lax.rem(column, side))
        for which, source in enumerate((phase, absorption)):
            for half in range(2):
                block = first if half == 0 else jnp.minimum(first + 1, blocks - 1)
                copies.append(
                    pltpu.make_async_copy(
                        source.at[0, :, pl.ds(pl.multiple_of(block * side, side), side)],
                        buffer.at[k, which, half],
                        sems.at[k, which, half],
                    )
                )
    for copy in copies:
        copy.start()
    if send is not None:
        index = send[0] + slab * send[1]
        extra = pltpu.make_async_copy(measured.at[index], refs[count], refs[-3])
        extra.start()
    lane = lax.broadcasted_iota(jnp.int32, (side, side), 1)
    for k in range(count):
        own = lane >= columns[k]
        for which in range(2):
            for half in range(2):
                copies[4 * k + 2 * which + half].wait()
            outs[k][which] = jnp.where(own, buffer[k, which, 0], buffer[k, which, 1])
    if send is not None:
        extra.wait()


def cut(bases, pairs, phase, absorption, measured=None, send=None):
    side = phase.shape[1]
    count = len(bases)
    sections = lax.axis_size("slab")
    shape = jax.ShapeDtypeStruct((2, side, side), jnp.float32)
    shapes = [shape] * count
    scratch = [
        pltpu.VMEM((count, 2, 2, side, side), jnp.float32),
        pltpu.SemaphoreType.DMA((count, 2, 2)),
    ]
    inputs = [pairs, phase, absorption]
    if send is not None:
        shapes = shapes + [jax.ShapeDtypeStruct((side, side), jnp.float32)]
        scratch = [pltpu.SemaphoreType.DMA(())] + scratch
        inputs.append(measured)
    return pl.pallas_call(
        lambda *refs: cut_kernel(bases, sections, send, *refs),
        in_specs=[SMEM] + [HBM] * (len(inputs) - 1),
        out_specs=[VMEM] * len(shapes),
        out_shape=shapes,
        scratch_shapes=scratch,
        compiler_params=params(16),
        name="cut",
    )(*inputs)


def join_kernel(bases, sections, pairs, here, there, out):
    side = out.shape[-1]
    slab = lax.axis_index("slab")
    row = lax.rem(pairs[0, position(0, bases, slab, sections)], side)
    rows = lax.broadcasted_iota(jnp.int32, (side, side), 0)
    for part in range(2):
        out[part] = jnp.where(rows >= row, here[part], there[part])


def join(base, pairs, here, there):
    sections = lax.axis_size("slab")
    return pl.pallas_call(
        lambda *refs: join_kernel([base], sections, *refs),
        in_specs=[SMEM, VMEM, VMEM],
        out_specs=VMEM,
        out_shape=jax.ShapeDtypeStruct(here.shape, jnp.float32),
        compiler_params=params(8),
        name="join",
    )(pairs, here, there)


def pack_kernel(*refs):
    out = refs[-1]
    for k, term in enumerate(refs[:-1]):
        out[k] = term[...]


def pack(terms):
    if len(terms) == 1:
        return terms[0][None]
    return pl.pallas_call(
        pack_kernel,
        in_specs=[VMEM] * len(terms),
        out_specs=VMEM,
        out_shape=jax.ShapeDtypeStruct((len(terms), *terms[0].shape), jnp.float32),
        compiler_params=params(8),
        name="pack",
    )(*terms)


def spread(metas, terms):
    views, kinds = [], []
    for kind, term in zip(metas, terms):
        if isinstance(kind, list):
            views += [term.at[i] for i in range(len(kind))]
            kinds += kind
        else:
            views.append(term)
            kinds.append(kind)
    return views, kinds


def spans(metas, tables, side, sections):
    slab = lax.axis_index("slab")
    last = lax.axis_index("tile") == lax.axis_size("tile") - 1
    out = []
    for source, base, mode in metas:
        index = position(0, [base], slab, sections)
        row, col = tables[source][0, index], tables[source][1, index]
        row = lax.rem(row, side)
        low, high = row, jnp.int32(side)
        if mode == "below":
            low, high = jnp.int32(0), row
        elif mode == "last":
            low = jnp.where(last, row, side)
        elif mode == "inner":
            low = jnp.where(last, side, row)
        out.append((lax.div(col, side), lax.rem(col, side), low, high))
    return out


def early_kernel(metas, sections, *refs):
    count = len(metas)
    tables, terms, out = refs[:4], refs[4 : 4 + count], refs[4 + count]
    terms, metas = spread(metas, terms)
    side = terms[0].shape[-1]
    blocks = out.shape[-1] // side
    rows = lax.broadcasted_iota(jnp.int32, (side, side), 0)
    lane = lax.broadcasted_iota(jnp.int32, (side, side), 1)

    @pl.loop(0, blocks)
    def _(block):
        out[:, :, pl.ds(pl.multiple_of(block * side, side), side)] = jnp.zeros((2, side, side), jnp.float32)

    for k, (first, col, low, high) in enumerate(spans(metas, tables, side, sections)):
        for half in range(2):
            block = first + half

            @pl.when((block < blocks) & (high > low))
            def _():
                keep = (rows >= low) & (rows < high)
                keep = keep & ((lane < col) if half else (lane >= col))
                place = pl.ds(pl.multiple_of(block * side, side), side)
                for part in range(2):
                    out[part, :, place] += jnp.where(keep, terms[k][part], 0.0)


def early(metas, tables, terms, cols_total):
    side = terms[0].shape[-1]
    sections = lax.axis_size("slab")
    return pl.pallas_call(
        lambda *refs: early_kernel(metas, sections, *refs),
        in_specs=[SMEM] * 4 + [VMEM] * len(terms),
        out_specs=VMEM,
        out_shape=jax.ShapeDtypeStruct((2, side, cols_total), jnp.float32),
        compiler_params=params(20),
        cost_estimate=cost(4),
        name="early",
    )(*tables, *terms)


def late_kernel(metas, sections, *refs):
    count = len(metas)
    tables, total, terms = refs[:4], refs[4], refs[5 : 5 + count]
    out, stage, sems = refs[5 + count :]
    side = terms[0].shape[-1]
    blocks = out.shape[-1] // side
    rows = lax.broadcasted_iota(jnp.int32, (side, side), 0)
    lane = lax.broadcasted_iota(jnp.int32, (side, side), 1)
    ranges = spans(metas, tables, side, sections)

    def place(block):
        return pl.ds(pl.multiple_of(block * side, side), side)

    def send(block, source):
        where = place(block)
        return pltpu.make_async_copy(source.at[:, :, where], out.at[:, 0, :, where], sems.at[block])

    def touched(block):
        hit = jnp.bool_(False)
        for first, col, low, high in ranges:
            hit = hit | (((block == first) | (block == first + 1)) & (high > low))
        return hit

    @pl.loop(0, blocks)
    def _(block):
        @pl.when(jnp.logical_not(touched(block)))
        def _():
            send(block, total).start()

    @pl.loop(0, blocks)
    def _(block):
        @pl.when(touched(block))
        def _():
            where = place(block)
            stage[:, :, where] = total[:, :, where]
            for k, (first, col, low, high) in enumerate(ranges):
                for half in range(2):

                    @pl.when((first + half == block) & (high > low))
                    def _():
                        keep = (rows >= low) & (rows < high)
                        keep = keep & ((lane < col) if half else (lane >= col))
                        for part in range(2):
                            stage[part, :, where] += jnp.where(keep, terms[k][part], 0.0)

            send(block, stage).start()

    @pl.loop(0, blocks)
    def _(block):
        send(block, stage).wait()


def late(metas, tables, total, terms):
    side = terms[0].shape[-1]
    cols_total = total.shape[-1]
    sections = lax.axis_size("slab")
    return pl.pallas_call(
        lambda *refs: late_kernel(metas, sections, *refs),
        in_specs=[SMEM] * 4 + [VMEM] * (1 + len(terms)),
        out_specs=HBM,
        out_shape=jax.ShapeDtypeStruct((2, 1, side, cols_total), jnp.float32),
        scratch_shapes=[
            pltpu.VMEM((2, side, cols_total), jnp.float32),
            pltpu.SemaphoreType.DMA((cols_total // side,)),
        ],
        compiler_params=params(28),
        name="late",
    )(*tables, total, *terms)


def local(phase, absorption, probe, measured, offsets):
    side = probe.shape[-1]
    cols_total = phase.shape[2]
    sections = lax.axis_size("slab")
    each = offsets.shape[0] // sections
    n_up = each // 2
    n_here = each - n_up
    distances = list(range(sections))

    pairs = offsets.T
    below = move(pairs, "tile", 1)
    here = lambda k, d: (k, n_here, d)
    up = lambda k, d: (sections * n_here + k, n_up, d)
    back = lambda d: (sections - d) % sections

    far = distances[1:]
    phase = pltpu.with_memory_space_constraint(phase, pltpu.HBM)
    absorption = pltpu.with_memory_space_constraint(absorption, pltpu.HBM)
    measured = pltpu.with_memory_space_constraint(measured, pltpu.HBM)
    done = [pairs]

    def step(kernel, scalars, *args):
        out = kernel(after(scalars, *done), *args)
        done[:] = [out[0] if isinstance(out, (list, tuple)) else out]
        return out

    def cutter(table, kinds, *args):
        return step(lambda p: cut(kinds, p, phase, absorption, *args), table)

    def joiner(table, kind, *args):
        return step(lambda p: join(kind, p, *args), table)

    def slotter(table, kind, base, each, *args):
        return step(lambda p: run_slot(kind, base, each, p, probe, *args, constants), table)

    lower, amplitude = [], []
    for k in range(n_up):
        *cuts, send = cutter(
            pairs, [up(k, d) for d in distances], measured, (up(k, 0)[0], n_up)
        )
        lower.append(cuts)
        amplitude.append(send)
    extra = [[rotate_last(lower[k][d], d) for d in far] for k in range(n_up)]
    raised = [[move(after(lower[k][d], below), "tile", 1) for d in far] for k in range(n_up)]
    low_cuts = [cutter(below, [here(k, d) for d in distances]) for k in range(n_here)]
    lowered = [[move(low_cuts[k][d], "tile", -1) for d in far] for k in range(n_here)]
    up_cuts = [cutter(below, [up(k, d) for d in distances]) for k in range(n_up)]
    own_cuts = [cutter(pairs, [here(k, d) for d in distances]) for k in range(n_here)]
    constants = expand(side)
    up_joined = [
        [joiner(below, up(k, d), raised[k][d - 1], up_cuts[k][d]) for d in far] for k in range(n_up)
    ]
    up_other = [[rotate(up_joined[k][d - 1], "slab", d) for d in far] for k in range(n_up)]
    for k in range(n_up):
        raised[k].insert(0, move(after(lower[k][0], *done), "tile", 1))
        amplitude[k] = move(after(amplitude[k], *done), "tile", 1)
    here_joined = [
        [joiner(pairs, here(k, d), own_cuts[k][d], lowered[k][d - 1]) for d in far]
        for k in range(n_here)
    ]
    here_other = [[rotate(here_joined[k][d - 1], "slab", d) for d in far] for k in range(n_here)]
    for k in range(n_here):
        lowered[k].insert(0, move(after(low_cuts[k][0], *done), "tile", -1))

    other_pairs, other_below = rotate(pairs, "batch", 1), rotate(below, "batch", 1)
    done += [other_pairs, other_below]
    tables = [pairs, below, other_pairs, other_below]

    last_outs = [
        slotter(pairs, "last", up(k, 0)[0], n_up, measured, [lower[k][0]], extra[k])
        for k in range(n_up)
    ]
    up_outs = [
        slotter(
            below, "up", up(k, 0)[0], n_up, amplitude[k], [raised[k][0], up_cuts[k][0]], up_other[k]
        )
        for k in range(n_up)
    ]
    up_back = [[rotate(up_outs[k][d], "slab", d) for d in far] for k in range(n_up)]
    fallen = [move(up_outs[k][0], "tile", -1) for k in range(n_up)]
    here_outs = [
        slotter(
            pairs, "here", here(k, 0)[0], n_here, measured,
            [own_cuts[k][0], lowered[k][0]], here_other[k],
        )
        for k in range(n_here)
    ]
    here_back = [[rotate(here_outs[k][d], "slab", d) for d in far] for k in range(n_here)]
    risen = [move(here_outs[k][0], "tile", 1) for k in range(n_here)]

    twin = lambda kind: (kind[0] + 2, kind[1], kind[2])
    terms, kinds = [], []

    def group(items, gate=None):
        values = [value for value, kind in items]
        if gate is not None:
            values[0] = after(values[0], gate)
        twins = rotate(pack(values), "batch", 1)
        terms.extend(values + [twins])
        kinds.extend([kind for value, kind in items] + [[twin(kind) for value, kind in items]])
        return twins

    items = []
    for k in range(n_here):
        items.append((here_outs[k][0], (0, here(k, 0), "above")))
    for k in range(n_up):
        items.append((last_outs[k][0], (0, up(k, 0), "last")))
        items.append((up_outs[k][0], (1, up(k, 0), "below")))
        items.append((fallen[k], (0, up(k, 0), "inner")))
        for d in far:
            items.append((up_back[k][d - 1], (1, up(k, back(d)), "below")))
    gate = group(items)
    falling = [[move(value, "tile", -1) for value in row] for row in up_back]
    rising = [[move(value, "tile", 1) for value in row] for row in here_back]
    ending = [
        [rotate_last(after(last_outs[k][d], *here_back[0]), d) for d in far] for k in range(n_up)
    ]
    items = []
    for k in range(n_here):
        items.append((risen[k], (1, here(k, 0), "below")))
        for d in far:
            items.append((here_back[k][d - 1], (0, here(k, back(d)), "above")))
    group(items, gate)
    total = early(kinds, tables, terms, cols_total)
    final, final_kinds = [], []

    def add(value, kind):
        final.extend([value, rotate(after(value, total), "batch", 1)])
        final_kinds.extend([kind, twin(kind)])

    for k in range(n_up):
        for d in far:
            add(falling[k][d - 1], (0, up(k, back(d)), "inner"))
            add(ending[k][d - 1], (0, up(k, back(d)), "last"))
    for k in range(n_here):
        for d in far:
            add(rising[k][d - 1], (1, here(k, back(d)), "below"))
    return late(final_kinds, tables, total, final)


def solution(mesh):
    in_specs = (
        P(("groups", "slab"), "tile", None),
        P(("groups", "slab"), "tile", None),
        P(),
        P(("groups", "tile", "batch"), None, None),
        P(("groups", "tile", "batch"), None),
    )
    out_specs = P(None, ("groups", "slab"), "tile", None)
    return jax.shard_map(local, mesh=mesh, in_specs=in_specs, out_specs=out_specs, check_vma=False)
```

```python
import math

import numpy as np
import jax
import jax.numpy as jnp
from jax import lax
from jax.experimental import pallas as pl
from jax.experimental.pallas import tpu as pltpu
from jax.sharding import PartitionSpec as P

SIN = [(-1.0) ** k / math.factorial(2 * k + 1) for k in range(8)]
COS = [(-1.0) ** k / math.factorial(2 * k) for k in range(8)]
VMEM = pl.BlockSpec(memory_space=pltpu.VMEM)
SMEM = pl.BlockSpec(memory_space=pltpu.SMEM)
HBM = pl.BlockSpec(memory_space=pltpu.HBM)


def params(mib):
    return pltpu.CompilerParams(vmem_limit_bytes=mib << 20)


def cost(microseconds):
    return pl.CostEstimate(flops=int(microseconds * 1e9), transcendentals=0, bytes_accessed=0)


def after(value, *others):
    return lax.optimization_barrier((value, *others))[0]


def move(block, axis, distance):
    size = lax.axis_size(axis)
    route = [(i, i + distance) for i in range(size) if 0 <= i + distance < size]
    return lax.ppermute(block, axis, route)


def rotate(block, axis, distance):
    size = lax.axis_size(axis)
    return lax.ppermute(block, axis, [(i, (i + distance) % size) for i in range(size)])


def rotate_last(block, distance):
    tiles, size = lax.axis_size("tile"), lax.axis_size("slab")
    base = (tiles - 1) * size
    route = [(base + i, base + (i + distance) % size) for i in range(size)]
    return lax.ppermute(block, ("tile", "slab"), route)


def halves(matrix):
    high = matrix.astype(np.float32).astype(jnp.bfloat16)
    low = (matrix - high.astype(np.float64)).astype(np.float32).astype(jnp.bfloat16)
    return [high, low]


def compact_tables(side):
    index = np.arange(side)
    fourier = np.exp(-2j * np.pi * (index[:, None] * index[None, :] % side) / side)
    wavenumber = np.where(index < side // 2, index, index - side)
    kernel = np.exp(-1j * np.pi * (wavenumber * wavenumber % (8 * side)) / (4 * side))
    line = np.fft.ifft(kernel)
    line = (line + line[-index % side]) / 2
    fresnel = line[(index[:, None] - index[None, :]) % side]
    scaled = fourier / math.sqrt(side)
    pieces = []
    for matrix in (fresnel, scaled):
        pieces += halves(matrix.real) + halves(matrix.imag)
    return np.stack(pieces)


def expand_kernel(pieces, *outs):
    side = pieces.shape[-1]
    for which in range(2):
        left, right = outs[2 * which], outs[2 * which + 1]
        real_high, real_low, imag_high, imag_low = [pieces[4 * which + k] for k in range(4)]
        real = [real_high, real_low, real_high]
        imag = [imag_high, imag_low, imag_high]
        minus = [-imag_high, -imag_low, -imag_high]
        for column, blocks in enumerate((real + minus, imag + real)):
            for row, block in enumerate(blocks):
                rows, cols = pl.ds(row * side, side), pl.ds(column * side, side)
                right[rows, cols] = block
                left[cols, rows] = block


def expand(side):
    pieces = jnp.asarray(compact_tables(side))
    left = jax.ShapeDtypeStruct((2 * side, 6 * side), jnp.bfloat16)
    right = jax.ShapeDtypeStruct((6 * side, 2 * side), jnp.bfloat16)
    return pl.pallas_call(
        expand_kernel,
        in_specs=[VMEM],
        out_specs=[VMEM] * 4,
        out_shape=[left, right, left, right],
        compiler_params=params(16),
        name="expand",
    )(pieces)


def split(value):
    high = value.astype(jnp.bfloat16)
    low = (value - high.astype(jnp.float32)).astype(jnp.bfloat16)
    return high, low


def two_sided(left, right, real, imag):
    side = real.shape[-1]
    real_high, real_low = split(real)
    imag_high, imag_low = split(imag)
    wide = jnp.concatenate([real_high, real_high, real_low, imag_high, imag_high, imag_low], axis=1)
    inner = jnp.dot(wide, right[...], preferred_element_type=jnp.float32)
    real_high, real_low = split(inner[:, :side])
    imag_high, imag_low = split(inner[:, side:])
    tall = jnp.concatenate([real_high, real_high, real_low, imag_high, imag_high, imag_low], axis=0)
    outer = jnp.dot(left[...], tall, preferred_element_type=jnp.float32)
    return outer[:side], outer[side:]


def transmission(phase, absorption):
    square = phase * phase
    sine = jnp.full_like(phase, SIN[-1])
    cosine = jnp.full_like(phase, COS[-1])
    for a, b in zip(SIN[-2::-1], COS[-2::-1]):
        sine = sine * square + a
        cosine = cosine * square + b
    damping = jnp.exp(-absorption)
    return damping * cosine, damping * sine * phase


def slot_kernel(kind, *args):
    if kind == "last":

        @pl.when(lax.axis_index("tile") == lax.axis_size("tile") - 1)
        def _():
            slot_body(kind, *args)
    else:
        slot_body(kind, *args)


def slot_body(kind, base, each, sections, pairs, probe, measured, *refs):
    pieces = 1 if kind == "last" else 2
    own = refs[:pieces]
    others = refs[pieces : pieces + sections - 1]
    refs = refs[pieces + sections - 1 :]
    prop_left, prop_right, dft_left, dft_right = refs[:4]
    outs = refs[4 : 4 + sections]
    wave, trans = refs[4 + sections : 6 + sections]
    side = probe.shape[-1]
    slab = lax.axis_index("slab")
    index = base + slab * each
    row = lax.rem(pairs[0, index], side)
    col = lax.rem(pairs[1, index], side)
    if kind == "up":
        amplitude = measured.at[pl.ds(0, side)]
        fetch = None
    else:
        amplitude, sem = refs[6 + sections :]
        fetch = pltpu.make_async_copy(measured.at[index], amplitude, sem)
        fetch.start()
    rows = lax.broadcasted_iota(jnp.int32, (side, side), 0)
    patch = [own[0][0], own[0][1]]
    if pieces == 2:
        patch = [jnp.where(rows >= row, own[0][k], own[1][k]) for k in range(2)]
    trans[slab, 0], trans[slab, 1] = transmission(patch[0], patch[1])
    for distance in range(1, sections):
        owner = lax.rem(slab + (sections - distance), sections)
        real, imag = transmission(others[distance - 1][0], others[distance - 1][1])
        trans[owner, 0] = real
        trans[owner, 1] = imag
    for part in range(2):
        wave[0, part] = pltpu.roll(pltpu.roll(probe[part], row, 0), col, 1)
    for step in range(sections):
        a, b, c, d = wave[step, 0], wave[step, 1], trans[step, 0], trans[step, 1]
        real, imag = a * c - b * d, a * d + b * c
        if step < sections - 1:
            real, imag = two_sided(prop_left, prop_right, real, imag)
            wave[step + 1, 0] = real
            wave[step + 1, 1] = imag
    real, imag = two_sided(dft_left, dft_right, real, imag)
    if fetch is not None:
        fetch.wait()
    factor = 1.0 - amplitude[...] * lax.rsqrt(jnp.maximum(real * real + imag * imag, 0.25))
    real, minus = two_sided(dft_left, dft_right, real * factor, -imag * factor)
    for step in range(sections - 1, -1, -1):
        a, b = wave[step, 0], wave[step, 1]
        wave[step, 0] = a * real - b * minus
        wave[step, 1] = -(a * minus + b * real)
        if step > 0:
            c, d = trans[step, 0], trans[step, 1]
            real, minus = c * real - d * minus, c * minus + d * real
            real, minus = two_sided(prop_left, prop_right, real, minus)
    for distance in range(sections):
        outs[distance][...] = wave[lax.rem(slab + distance, sections)]


def run_slot(kind, base, each, pairs, probe, measured, own, others, constants):
    sections = len(others) + 1
    side = probe.shape[-1]
    shape = jax.ShapeDtypeStruct((2, side, side), jnp.float32)
    scratch = [pltpu.VMEM((sections, 2, side, side), jnp.float32)] * 2
    if kind != "up":
        scratch += [pltpu.VMEM((side, side), jnp.float32), pltpu.SemaphoreType.DMA(())]
    return pl.pallas_call(
        lambda *refs: slot_kernel(kind, base, each, sections, *refs),
        in_specs=[SMEM, VMEM, VMEM if kind == "up" else HBM]
        + [VMEM] * (len(own) + len(others) + 4),
        out_specs=[VMEM] * sections,
        out_shape=[shape] * sections,
        scratch_shapes=scratch,
        compiler_params=params(32),
        name="slot_" + kind,
    )(pairs, probe, measured, *own, *others, *constants)


def position(k, bases, slab, sections):
    base, each, distance = bases[k]
    return base + lax.rem(slab + distance, sections) * each


def cut_kernel(bases, sections, pairs, phase, absorption, *refs):
    count = len(bases)
    side = phase.shape[1]
    blocks = phase.shape[2] // side
    slab = lax.axis_index("slab")
    outs = refs[:count]
    buffer, sems = refs[-2], refs[-1]
    copies, columns = [], []
    for k in range(count):
        column = pairs[1, position(k, bases, slab, sections)]
        first = lax.div(column, side)
        columns.append(lax.rem(column, side))
        for which, source in enumerate((phase, absorption)):
            for half in range(2):
                block = first if half == 0 else jnp.minimum(first + 1, blocks - 1)
                copies.append(
                    pltpu.make_async_copy(
                        source.at[0, :, pl.ds(pl.multiple_of(block * side, side), side)],
                        buffer.at[k, which, half],
                        sems.at[k, which, half],
                    )
                )
    for copy in copies:
        copy.start()
    lane = lax.broadcasted_iota(jnp.int32, (side, side), 1)
    for k in range(count):
        own = lane >= columns[k]
        for which in range(2):
            for half in range(2):
                copies[4 * k + 2 * which + half].wait()
            outs[k][which] = jnp.where(own, buffer[k, which, 0], buffer[k, which, 1])


def cut(bases, pairs, phase, absorption):
    side = phase.shape[1]
    count = len(bases)
    sections = lax.axis_size("slab")
    shape = jax.ShapeDtypeStruct((2, side, side), jnp.float32)
    scratch = [
        pltpu.VMEM((count, 2, 2, side, side), jnp.float32),
        pltpu.SemaphoreType.DMA((count, 2, 2)),
    ]
    return pl.pallas_call(
        lambda *refs: cut_kernel(bases, sections, *refs),
        in_specs=[SMEM, HBM, HBM],
        out_specs=[VMEM] * count,
        out_shape=[shape] * count,
        scratch_shapes=scratch,
        compiler_params=params(16),
        name="cut",
    )(pairs, phase, absorption)


def greet_kernel(base, each, pairs, measured, out, sem):
    side = measured.shape[-1]
    slab = lax.axis_index("slab")
    copy = pltpu.make_async_copy(measured.at[base + slab * each], out.at[pl.ds(0, side)], sem)
    copy.start()
    rows = lax.broadcasted_iota(jnp.int32, (8, side), 0)
    lane = lax.broadcasted_iota(jnp.int32, (8, side), 1)
    words = jnp.zeros((8, side), jnp.float32)
    for row in range(2):
        for col in range(pairs.shape[1]):
            value = pairs[row, col].astype(jnp.float32)
            words = jnp.where((rows == row) & (lane == col), value, words)
    out[pl.ds(side, 8)] = words
    copy.wait()


def greet(base, each, pairs, measured):
    side = measured.shape[-1]
    return pl.pallas_call(
        lambda *refs: greet_kernel(base, each, *refs),
        in_specs=[SMEM, HBM],
        out_specs=VMEM,
        out_shape=jax.ShapeDtypeStruct((side + 8, side), jnp.float32),
        scratch_shapes=[pltpu.SemaphoreType.DMA(())],
        compiler_params=params(4),
        name="greet",
    )(pairs, measured)


def join_kernel(bases, sections, pairs, here, there, out):
    side = out.shape[-1]
    slab = lax.axis_index("slab")
    row = lax.rem(pairs[0, position(0, bases, slab, sections)], side)
    rows = lax.broadcasted_iota(jnp.int32, (side, side), 0)
    for part in range(2):
        out[part] = jnp.where(rows >= row, here[part], there[part])


def join(base, pairs, here, there):
    sections = lax.axis_size("slab")
    return pl.pallas_call(
        lambda *refs: join_kernel([base], sections, *refs),
        in_specs=[SMEM, VMEM, VMEM],
        out_specs=VMEM,
        out_shape=jax.ShapeDtypeStruct(here.shape, jnp.float32),
        compiler_params=params(8),
        name="join",
    )(pairs, here, there)


def pack_kernel(*refs):
    out = refs[-1]
    for k, term in enumerate(refs[:-1]):
        out[k] = term[...]


def pack(terms):
    if len(terms) == 1:
        return terms[0][None]
    return pl.pallas_call(
        pack_kernel,
        in_specs=[VMEM] * len(terms),
        out_specs=VMEM,
        out_shape=jax.ShapeDtypeStruct((len(terms), *terms[0].shape), jnp.float32),
        compiler_params=params(8),
        name="pack",
    )(*terms)


def spread(metas, terms):
    views, kinds = [], []
    for kind, term in zip(metas, terms):
        if isinstance(kind, list):
            views += [term.at[i] for i in range(len(kind))]
            kinds += kind
        else:
            views.append(term)
            kinds.append(kind)
    return views, kinds


def spans(metas, tables, side, sections):
    slab = lax.axis_index("slab")
    last = lax.axis_index("tile") == lax.axis_size("tile") - 1
    out = []
    for source, base, mode in metas:
        index = position(0, [base], slab, sections)
        row, col = tables[source][0, index], tables[source][1, index]
        row = lax.rem(row, side)
        low, high = row, jnp.int32(side)
        if mode == "below":
            low, high = jnp.int32(0), row
        elif mode == "last":
            low = jnp.where(last, row, side)
        elif mode == "inner":
            low = jnp.where(last, side, row)
        out.append((lax.div(col, side), lax.rem(col, side), low, high))
    return out


def early_kernel(metas, sections, *refs):
    count = len(metas)
    tables, terms, out = refs[:4], refs[4 : 4 + count], refs[4 + count]
    terms, metas = spread(metas, terms)
    side = terms[0].shape[-1]
    blocks = out.shape[-1] // side
    rows = lax.broadcasted_iota(jnp.int32, (side, side), 0)
    lane = lax.broadcasted_iota(jnp.int32, (side, side), 1)

    @pl.loop(0, blocks)
    def _(block):
        out[:, :, pl.ds(pl.multiple_of(block * side, side), side)] = jnp.zeros((2, side, side), jnp.float32)

    for k, (first, col, low, high) in enumerate(spans(metas, tables, side, sections)):
        for half in range(2):
            block = first + half

            @pl.when((block < blocks) & (high > low))
            def _():
                keep = (rows >= low) & (rows < high)
                keep = keep & ((lane < col) if half else (lane >= col))
                place = pl.ds(pl.multiple_of(block * side, side), side)
                for part in range(2):
                    out[part, :, place] += jnp.where(keep, terms[k][part], 0.0)


def early(metas, tables, terms, cols_total):
    side = terms[0].shape[-1]
    sections = lax.axis_size("slab")
    return pl.pallas_call(
        lambda *refs: early_kernel(metas, sections, *refs),
        in_specs=[SMEM] * 4 + [VMEM] * len(terms),
        out_specs=VMEM,
        out_shape=jax.ShapeDtypeStruct((2, side, cols_total), jnp.float32),
        compiler_params=params(20),
        cost_estimate=cost(4),
        name="early",
    )(*tables, *terms)


def late_kernel(metas, sections, *refs):
    count = len(metas)
    tables, total, terms = refs[:4], refs[4], refs[5 : 5 + count]
    out, stage, sems = refs[5 + count :]
    side = terms[0].shape[-1]
    blocks = out.shape[-1] // side
    rows = lax.broadcasted_iota(jnp.int32, (side, side), 0)
    lane = lax.broadcasted_iota(jnp.int32, (side, side), 1)
    ranges = spans(metas, tables, side, sections)

    def place(block):
        return pl.ds(pl.multiple_of(block * side, side), side)

    def send(block, source):
        where = place(block)
        return pltpu.make_async_copy(source.at[:, :, where], out.at[:, 0, :, where], sems.at[block])

    def touched(block):
        hit = jnp.bool_(False)
        for first, col, low, high in ranges:
            hit = hit | (((block == first) | (block == first + 1)) & (high > low))
        return hit

    @pl.loop(0, blocks)
    def _(block):
        @pl.when(jnp.logical_not(touched(block)))
        def _():
            send(block, total).start()

    @pl.loop(0, blocks)
    def _(block):
        @pl.when(touched(block))
        def _():
            where = place(block)
            stage[:, :, where] = total[:, :, where]
            for k, (first, col, low, high) in enumerate(ranges):
                for half in range(2):

                    @pl.when((first + half == block) & (high > low))
                    def _():
                        keep = (rows >= low) & (rows < high)
                        keep = keep & ((lane < col) if half else (lane >= col))
                        for part in range(2):
                            stage[part, :, where] += jnp.where(keep, terms[k][part], 0.0)

            send(block, stage).start()

    @pl.loop(0, blocks)
    def _(block):
        send(block, stage).wait()


def late(metas, tables, total, terms):
    side = terms[0].shape[-1]
    cols_total = total.shape[-1]
    sections = lax.axis_size("slab")
    return pl.pallas_call(
        lambda *refs: late_kernel(metas, sections, *refs),
        in_specs=[SMEM] * 4 + [VMEM] * (1 + len(terms)),
        out_specs=HBM,
        out_shape=jax.ShapeDtypeStruct((2, 1, side, cols_total), jnp.float32),
        scratch_shapes=[
            pltpu.VMEM((2, side, cols_total), jnp.float32),
            pltpu.SemaphoreType.DMA((cols_total // side,)),
        ],
        compiler_params=params(28),
        name="late",
    )(*tables, total, *terms)


def local(phase, absorption, probe, measured, offsets):
    side = probe.shape[-1]
    cols_total = phase.shape[2]
    sections = lax.axis_size("slab")
    each = offsets.shape[0] // sections
    n_up = each // 2
    n_here = each - n_up
    distances = list(range(sections))

    pairs = offsets.T
    here = lambda k, d: (k, n_here, d)
    up = lambda k, d: (sections * n_here + k, n_up, d)
    back = lambda d: (sections - d) % sections

    far = distances[1:]
    phase = pltpu.with_memory_space_constraint(phase, pltpu.HBM)
    absorption = pltpu.with_memory_space_constraint(absorption, pltpu.HBM)
    measured = pltpu.with_memory_space_constraint(measured, pltpu.HBM)
    done = [pairs]

    def step(kernel, scalars, *args):
        out = kernel(after(scalars, *done), *args)
        done[:] = [out[0] if isinstance(out, (list, tuple)) else out]
        return out

    def cutter(table, kinds, *args):
        return step(lambda p: cut(kinds, p, phase, absorption, *args), table)

    def joiner(table, kind, *args):
        return step(lambda p: join(kind, p, *args), table)

    def slotter(table, kind, base, each, *args):
        return step(lambda p: run_slot(kind, base, each, p, probe, *args, constants), table)

    greetings = [
        move(step(lambda p: greet(up(k, 0)[0], n_up, p, measured), pairs), "tile", 1)
        for k in range(n_up)
    ]
    lower = [cutter(pairs, [up(k, d) for d in distances]) for k in range(n_up)]
    if n_up:
        below = greetings[0][side : side + 2, : pairs.shape[1]].astype(jnp.int32)
    else:
        below = move(pairs, "tile", 1)
    extra = [[rotate_last(lower[k][d], d) for d in far] for k in range(n_up)]
    raised = [[move(after(lower[k][d], below), "tile", 1) for d in far] for k in range(n_up)]
    for k in range(n_up):
        raised[k].insert(0, move(after(lower[k][0], below), "tile", 1))
    low_cuts = [cutter(below, [here(k, d) for d in distances]) for k in range(n_here)]
    lowered = [[move(low_cuts[k][d], "tile", -1) for d in far] for k in range(n_here)]
    for k in range(n_here):
        lowered[k].insert(0, move(low_cuts[k][0], "tile", -1))
    up_cuts = [cutter(below, [up(k, d) for d in distances]) for k in range(n_up)]
    own_cuts = [cutter(pairs, [here(k, d) for d in distances]) for k in range(n_here)]
    constants = expand(side)
    up_joined = [
        [joiner(below, up(k, d), raised[k][d], up_cuts[k][d]) for d in far] for k in range(n_up)
    ]
    up_other = [[rotate(up_joined[k][d - 1], "slab", d) for d in far] for k in range(n_up)]
    here_joined = [
        [joiner(pairs, here(k, d), own_cuts[k][d], lowered[k][d]) for d in far]
        for k in range(n_here)
    ]
    here_other = [[rotate(here_joined[k][d - 1], "slab", d) for d in far] for k in range(n_here)]

    other_pairs, other_below = rotate(pairs, "batch", 1), rotate(below, "batch", 1)
    done += [other_pairs, other_below]
    tables = [pairs, below, other_pairs, other_below]

    last_outs = [
        slotter(pairs, "last", up(k, 0)[0], n_up, measured, [lower[k][0]], extra[k])
        for k in range(n_up)
    ]
    up_outs = [
        slotter(
            below, "up", up(k, 0)[0], n_up, greetings[k], [raised[k][0], up_cuts[k][0]], up_other[k]
        )
        for k in range(n_up)
    ]
    up_back = [[rotate(up_outs[k][d], "slab", d) for d in far] for k in range(n_up)]
    fallen = [move(up_outs[k][0], "tile", -1) for k in range(n_up)]
    here_outs = [
        slotter(
            pairs, "here", here(k, 0)[0], n_here, measured,
            [own_cuts[k][0], lowered[k][0]], here_other[k],
        )
        for k in range(n_here)
    ]
    here_back = [[rotate(here_outs[k][d], "slab", d) for d in far] for k in range(n_here)]
    risen = [move(here_outs[k][0], "tile", 1) for k in range(n_here)]

    twin = lambda kind: (kind[0] + 2, kind[1], kind[2])
    terms, kinds = [], []

    def group(items, gate=None):
        values = [value for value, kind in items]
        if gate is not None:
            values[0] = after(values[0], gate)
        twins = rotate(pack(values), "batch", 1)
        terms.extend(values + [twins])
        kinds.extend([kind for value, kind in items] + [[twin(kind) for value, kind in items]])
        return twins

    items = []
    for k in range(n_up):
        items.append((last_outs[k][0], (0, up(k, 0), "last")))
        items.append((up_outs[k][0], (1, up(k, 0), "below")))
    gate = group(items) if items else None
    falling = [
        [move(after(value, fallen[k]), "tile", -1) for value in up_back[k]] for k in range(n_up)
    ]
    rising = [[move(value, "tile", 1) for value in row] for row in here_back]
    ending = [
        [rotate_last(after(last_outs[k][d], *here_back[0]), d) for d in far] for k in range(n_up)
    ]
    items = []
    for k in range(n_here):
        items.append((here_outs[k][0], (0, here(k, 0), "above")))
        items.append((risen[k], (1, here(k, 0), "below")))
        for d in far:
            items.append((here_back[k][d - 1], (0, here(k, back(d)), "above")))
    for k in range(n_up):
        items.append((fallen[k], (0, up(k, 0), "inner")))
        for d in far:
            items.append((up_back[k][d - 1], (1, up(k, back(d)), "below")))
            items.append((falling[k][d - 1], (0, up(k, back(d)), "inner")))
    group(items, gate)
    total = early(kinds, tables, terms, cols_total)
    final, final_kinds = [], []

    def add(value, kind):
        final.extend([value, rotate(after(value, total), "batch", 1)])
        final_kinds.extend([kind, twin(kind)])

    for k in range(n_up):
        for d in far:
            add(ending[k][d - 1], (0, up(k, back(d)), "last"))
    for k in range(n_here):
        for d in far:
            add(rising[k][d - 1], (1, here(k, back(d)), "below"))
    return late(final_kinds, tables, total, final)


def solution(mesh):
    in_specs = (
        P(("groups", "slab"), "tile", None),
        P(("groups", "slab"), "tile", None),
        P(),
        P(("groups", "tile", "batch"), None, None),
        P(("groups", "tile", "batch"), None),
    )
    out_specs = P(None, ("groups", "slab"), "tile", None)
    return jax.shard_map(local, mesh=mesh, in_specs=in_specs, out_specs=out_specs, check_vma=False)
```

```python
import math

import numpy as np
import jax
import jax.numpy as jnp
from jax import lax
from jax.experimental import pallas as pl
from jax.experimental.pallas import tpu as pltpu
from jax.sharding import PartitionSpec as P

SIN = [(-1.0) ** k / math.factorial(2 * k + 1) for k in range(8)]
COS = [(-1.0) ** k / math.factorial(2 * k) for k in range(8)]
VMEM = pl.BlockSpec(memory_space=pltpu.VMEM)
SMEM = pl.BlockSpec(memory_space=pltpu.SMEM)
HBM = pl.BlockSpec(memory_space=pltpu.HBM)


def params(mib):
    return pltpu.CompilerParams(vmem_limit_bytes=mib << 20)


def cost(microseconds):
    return pl.CostEstimate(flops=int(microseconds * 1e9), transcendentals=0, bytes_accessed=0)


def after(value, *others):
    return lax.optimization_barrier((value, *others))[0]


def move(block, axis, distance):
    size = lax.axis_size(axis)
    route = [(i, i + distance) for i in range(size) if 0 <= i + distance < size]
    return lax.ppermute(block, axis, route)


def rotate(block, axis, distance):
    size = lax.axis_size(axis)
    return lax.ppermute(block, axis, [(i, (i + distance) % size) for i in range(size)])


def rotate_last(block, distance):
    tiles, size = lax.axis_size("tile"), lax.axis_size("slab")
    base = (tiles - 1) * size
    route = [(base + i, base + (i + distance) % size) for i in range(size)]
    return lax.ppermute(block, ("tile", "slab"), route)


def halves(matrix):
    high = matrix.astype(np.float32).astype(jnp.bfloat16)
    low = (matrix - high.astype(np.float64)).astype(np.float32).astype(jnp.bfloat16)
    return [high, low]


def compact_tables(side):
    index = np.arange(side)
    fourier = np.exp(-2j * np.pi * (index[:, None] * index[None, :] % side) / side)
    wavenumber = np.where(index < side // 2, index, index - side)
    kernel = np.exp(-1j * np.pi * (wavenumber * wavenumber % (8 * side)) / (4 * side))
    line = np.fft.ifft(kernel)
    line = (line + line[-index % side]) / 2
    fresnel = line[(index[:, None] - index[None, :]) % side]
    scaled = fourier / math.sqrt(side)
    pieces = []
    for matrix in (fresnel, scaled):
        pieces += halves(matrix.real) + halves(matrix.imag)
    return np.stack(pieces)


def expand_kernel(pieces, *outs):
    side = pieces.shape[-1]
    for which in range(2):
        left, right = outs[2 * which], outs[2 * which + 1]
        real_high, real_low, imag_high, imag_low = [pieces[4 * which + k] for k in range(4)]
        real = [real_high, real_low, real_high]
        imag = [imag_high, imag_low, imag_high]
        minus = [-imag_high, -imag_low, -imag_high]
        for column, blocks in enumerate((real + minus, imag + real)):
            for row, block in enumerate(blocks):
                rows, cols = pl.ds(row * side, side), pl.ds(column * side, side)
                right[rows, cols] = block
                left[cols, rows] = block


def expand(side):
    pieces = jnp.asarray(compact_tables(side))
    left = jax.ShapeDtypeStruct((2 * side, 6 * side), jnp.bfloat16)
    right = jax.ShapeDtypeStruct((6 * side, 2 * side), jnp.bfloat16)
    return pl.pallas_call(
        expand_kernel,
        in_specs=[VMEM],
        out_specs=[VMEM] * 4,
        out_shape=[left, right, left, right],
        compiler_params=params(16),
        name="expand",
    )(pieces)


def split(value):
    high = value.astype(jnp.bfloat16)
    low = (value - high.astype(jnp.float32)).astype(jnp.bfloat16)
    return high, low


def two_sided(left, right, real, imag):
    side = real.shape[-1]
    real_high, real_low = split(real)
    imag_high, imag_low = split(imag)
    wide = jnp.concatenate([real_high, real_high, real_low, imag_high, imag_high, imag_low], axis=1)
    inner = jnp.dot(wide, right[...], preferred_element_type=jnp.float32)
    real_high, real_low = split(inner[:, :side])
    imag_high, imag_low = split(inner[:, side:])
    tall = jnp.concatenate([real_high, real_high, real_low, imag_high, imag_high, imag_low], axis=0)
    outer = jnp.dot(left[...], tall, preferred_element_type=jnp.float32)
    return outer[:side], outer[side:]


def transmission(phase, absorption):
    square = phase * phase
    sine = jnp.full_like(phase, SIN[-1])
    cosine = jnp.full_like(phase, COS[-1])
    for a, b in zip(SIN[-2::-1], COS[-2::-1]):
        sine = sine * square + a
        cosine = cosine * square + b
    damping = jnp.exp(-absorption)
    return damping * cosine, damping * sine * phase


def slot_kernel(kind, *args):
    if kind == "last":

        @pl.when(lax.axis_index("tile") == lax.axis_size("tile") - 1)
        def _():
            slot_body(kind, *args)
    else:
        slot_body(kind, *args)


def slot_body(kind, base, each, sections, pairs, probe, measured, *refs):
    pieces = 1 if kind == "last" else 2
    own = refs[:pieces]
    others = refs[pieces : pieces + sections - 1]
    refs = refs[pieces + sections - 1 :]
    prop_left, prop_right, dft_left, dft_right = refs[:4]
    outs = refs[4 : 4 + sections]
    wave, trans = refs[4 + sections : 6 + sections]
    side = probe.shape[-1]
    slab = lax.axis_index("slab")
    index = base + slab * each
    row = lax.rem(pairs[0, index], side)
    col = lax.rem(pairs[1, index], side)
    if kind == "up":
        amplitude = own[0].at[2]
        fetch = None
    else:
        amplitude, sem = refs[6 + sections :]
        fetch = pltpu.make_async_copy(measured.at[index], amplitude, sem)
        fetch.start()
    rows = lax.broadcasted_iota(jnp.int32, (side, side), 0)
    patch = [own[0][0], own[0][1]]
    if pieces == 2:
        patch = [jnp.where(rows >= row, own[0][k], own[1][k]) for k in range(2)]
    trans[slab, 0], trans[slab, 1] = transmission(patch[0], patch[1])
    for distance in range(1, sections):
        owner = lax.rem(slab + (sections - distance), sections)
        real, imag = transmission(others[distance - 1][0], others[distance - 1][1])
        trans[owner, 0] = real
        trans[owner, 1] = imag
    for part in range(2):
        wave[0, part] = pltpu.roll(pltpu.roll(probe[part], row, 0), col, 1)
    for step in range(sections):
        a, b, c, d = wave[step, 0], wave[step, 1], trans[step, 0], trans[step, 1]
        real, imag = a * c - b * d, a * d + b * c
        if step < sections - 1:
            real, imag = two_sided(prop_left, prop_right, real, imag)
            wave[step + 1, 0] = real
            wave[step + 1, 1] = imag
    real, imag = two_sided(dft_left, dft_right, real, imag)
    if fetch is not None:
        fetch.wait()
    factor = 1.0 - amplitude[...] * lax.rsqrt(jnp.maximum(real * real + imag * imag, 0.25))
    real, minus = two_sided(dft_left, dft_right, real * factor, -imag * factor)
    for step in range(sections - 1, -1, -1):
        a, b = wave[step, 0], wave[step, 1]
        wave[step, 0] = a * real - b * minus
        wave[step, 1] = -(a * minus + b * real)
        if step > 0:
            c, d = trans[step, 0], trans[step, 1]
            real, minus = c * real - d * minus, c * minus + d * real
            real, minus = two_sided(prop_left, prop_right, real, minus)
    for distance in range(sections):
        outs[distance][...] = wave[lax.rem(slab + distance, sections)]


def run_slot(kind, base, each, pairs, probe, measured, own, others, constants):
    sections = len(others) + 1
    side = probe.shape[-1]
    shape = jax.ShapeDtypeStruct((2, side, side), jnp.float32)
    scratch = [pltpu.VMEM((sections, 2, side, side), jnp.float32)] * 2
    if kind != "up":
        scratch += [pltpu.VMEM((side, side), jnp.float32), pltpu.SemaphoreType.DMA(())]
    return pl.pallas_call(
        lambda *refs: slot_kernel(kind, base, each, sections, *refs),
        in_specs=[SMEM, VMEM, HBM]
        + [VMEM] * (len(own) + len(others) + 4),
        out_specs=[VMEM] * sections,
        out_shape=[shape] * sections,
        scratch_shapes=scratch,
        compiler_params=params(32),
        name="slot_" + kind,
    )(pairs, probe, measured, *own, *others, *constants)


def position(k, bases, slab, sections):
    base, each, distance = bases[k]
    return base + lax.rem(slab + distance, sections) * each


def cut_kernel(bases, sections, send, pairs, phase, absorption, *refs):
    count = len(bases)
    side = phase.shape[1]
    blocks = phase.shape[2] // side
    slab = lax.axis_index("slab")
    extra = None
    if send is not None:
        extra = (refs[0].at[send[0] + slab * send[1]], refs[1].at[2], refs[-3])
        extra = pltpu.make_async_copy(*extra)
        refs = refs[1:]
    outs = refs[:count]
    buffer, sems = refs[-2], refs[-1]
    copies, columns = [], []
    for k in range(count):
        column = pairs[1, position(k, bases, slab, sections)]
        first = lax.div(column, side)
        columns.append(lax.rem(column, side))
        for which, source in enumerate((phase, absorption)):
            for half in range(2):
                block = first if half == 0 else jnp.minimum(first + 1, blocks - 1)
                copies.append(
                    pltpu.make_async_copy(
                        source.at[0, :, pl.ds(pl.multiple_of(block * side, side), side)],
                        buffer.at[k, which, half],
                        sems.at[k, which, half],
                    )
                )
    for copy in copies:
        copy.start()
    if extra is not None:
        extra.start()
    lane = lax.broadcasted_iota(jnp.int32, (side, side), 1)
    for k in range(count):
        own = lane >= columns[k]
        for which in range(2):
            for half in range(2):
                copies[4 * k + 2 * which + half].wait()
            outs[k][which] = jnp.where(own, buffer[k, which, 0], buffer[k, which, 1])
    if extra is not None:
        extra.wait()


def cut(bases, pairs, phase, absorption, measured=None, send=None):
    side = phase.shape[1]
    count = len(bases)
    sections = lax.axis_size("slab")
    shapes = [jax.ShapeDtypeStruct((2, side, side), jnp.float32)] * count
    scratch = [
        pltpu.VMEM((count, 2, 2, side, side), jnp.float32),
        pltpu.SemaphoreType.DMA((count, 2, 2)),
    ]
    inputs = [pairs, phase, absorption]
    if send is not None:
        shapes = [jax.ShapeDtypeStruct((3, side, side), jnp.float32)] + shapes[1:]
        scratch = [pltpu.SemaphoreType.DMA(())] + scratch
        inputs.append(measured)
    return pl.pallas_call(
        lambda *refs: cut_kernel(bases, sections, send, *refs),
        in_specs=[SMEM] + [HBM] * (len(inputs) - 1),
        out_specs=[VMEM] * count,
        out_shape=shapes,
        scratch_shapes=scratch,
        compiler_params=params(16),
        name="cut",
    )(*inputs)


def join_kernel(bases, sections, pairs, here, there, out):
    side = out.shape[-1]
    slab = lax.axis_index("slab")
    row = lax.rem(pairs[0, position(0, bases, slab, sections)], side)
    rows = lax.broadcasted_iota(jnp.int32, (side, side), 0)
    for part in range(2):
        out[part] = jnp.where(rows >= row, here[part], there[part])


def join(base, pairs, here, there):
    sections = lax.axis_size("slab")
    return pl.pallas_call(
        lambda *refs: join_kernel([base], sections, *refs),
        in_specs=[SMEM, VMEM, VMEM],
        out_specs=VMEM,
        out_shape=jax.ShapeDtypeStruct(here.shape, jnp.float32),
        compiler_params=params(8),
        name="join",
    )(pairs, here, there)


def pack_kernel(*refs):
    out = refs[-1]
    for k, term in enumerate(refs[:-1]):
        out[k] = term[...]


def pack(terms):
    if len(terms) == 1:
        return terms[0][None]
    return pl.pallas_call(
        pack_kernel,
        in_specs=[VMEM] * len(terms),
        out_specs=VMEM,
        out_shape=jax.ShapeDtypeStruct((len(terms), *terms[0].shape), jnp.float32),
        compiler_params=params(8),
        name="pack",
    )(*terms)


def spread(metas, terms):
    views, kinds = [], []
    for kind, term in zip(metas, terms):
        if isinstance(kind, list):
            views += [term.at[i] for i in range(len(kind))]
            kinds += kind
        else:
            views.append(term)
            kinds.append(kind)
    return views, kinds


def spans(metas, tables, side, sections):
    slab = lax.axis_index("slab")
    last = lax.axis_index("tile") == lax.axis_size("tile") - 1
    out = []
    for source, base, mode in metas:
        index = position(0, [base], slab, sections)
        row, col = tables[source][0, index], tables[source][1, index]
        row = lax.rem(row, side)
        low, high = row, jnp.int32(side)
        if mode == "below":
            low, high = jnp.int32(0), row
        elif mode == "last":
            low = jnp.where(last, row, side)
        elif mode == "inner":
            low = jnp.where(last, side, row)
        out.append((lax.div(col, side), lax.rem(col, side), low, high))
    return out


def early_kernel(metas, sections, *refs):
    count = len(metas)
    tables, terms = refs[:4], refs[4 : 4 + count]
    out, copied, sem = refs[4 + count :]
    terms, metas = spread(metas, terms)
    side = terms[0].shape[-1]
    blocks = out.shape[-1] // side
    rows = lax.broadcasted_iota(jnp.int32, (side, side), 0)
    lane = lax.broadcasted_iota(jnp.int32, (side, side), 1)

    @pl.loop(0, blocks)
    def _(block):
        out[:, :, pl.ds(pl.multiple_of(block * side, side), side)] = jnp.zeros((2, side, side), jnp.float32)

    for k, (first, col, low, high) in enumerate(spans(metas, tables, side, sections)):
        for half in range(2):
            block = first + half

            @pl.when((block < blocks) & (high > low))
            def _():
                keep = (rows >= low) & (rows < high)
                keep = keep & ((lane < col) if half else (lane >= col))
                place = pl.ds(pl.multiple_of(block * side, side), side)
                for part in range(2):
                    out[part, :, place] += jnp.where(keep, terms[k][part], 0.0)

    copy = pltpu.make_async_copy(out, copied.at[:, 0], sem)
    copy.start()
    copy.wait()


def early(metas, tables, terms, cols_total):
    side = terms[0].shape[-1]
    sections = lax.axis_size("slab")
    return pl.pallas_call(
        lambda *refs: early_kernel(metas, sections, *refs),
        in_specs=[SMEM] * 4 + [VMEM] * len(terms),
        out_specs=[VMEM, HBM],
        out_shape=[
            jax.ShapeDtypeStruct((2, side, cols_total), jnp.float32),
            jax.ShapeDtypeStruct((2, 1, side, cols_total), jnp.float32),
        ],
        scratch_shapes=[pltpu.SemaphoreType.DMA(())],
        compiler_params=params(20),
        name="early",
    )(*tables, *terms)


def late_kernel(metas, sections, *refs):
    count = len(metas)
    tables, total, terms = refs[:4], refs[4], refs[5 : 5 + count]
    out, stage, sems = refs[6 + count :]
    side = terms[0].shape[-1]
    blocks = out.shape[-1] // side
    rows = lax.broadcasted_iota(jnp.int32, (side, side), 0)
    lane = lax.broadcasted_iota(jnp.int32, (side, side), 1)
    ranges = spans(metas, tables, side, sections)

    def place(block):
        return pl.ds(pl.multiple_of(block * side, side), side)

    def send(block):
        where = place(block)
        return pltpu.make_async_copy(stage.at[:, :, where], out.at[:, 0, :, where], sems.at[block])

    def touched(block):
        hit = jnp.bool_(False)
        for first, col, low, high in ranges:
            hit = hit | (((block == first) | (block == first + 1)) & (high > low))
        return hit

    @pl.loop(0, blocks)
    def _(block):
        @pl.when(touched(block))
        def _():
            where = place(block)
            stage[:, :, where] = total[:, :, where]
            for k, (first, col, low, high) in enumerate(ranges):
                for half in range(2):

                    @pl.when((first + half == block) & (high > low))
                    def _():
                        keep = (rows >= low) & (rows < high)
                        keep = keep & ((lane < col) if half else (lane >= col))
                        for part in range(2):
                            stage[part, :, where] += jnp.where(keep, terms[k][part], 0.0)

            send(block).start()

    @pl.loop(0, blocks)
    def _(block):
        @pl.when(touched(block))
        def _():
            send(block).wait()


def late(metas, tables, total, copied, terms):
    side = terms[0].shape[-1]
    cols_total = total.shape[-1]
    sections = lax.axis_size("slab")
    return pl.pallas_call(
        lambda *refs: late_kernel(metas, sections, *refs),
        in_specs=[SMEM] * 4 + [VMEM] * (1 + len(terms)) + [HBM],
        out_specs=HBM,
        input_output_aliases={5 + len(terms): 0},
        out_shape=jax.ShapeDtypeStruct((2, 1, side, cols_total), jnp.float32),
        scratch_shapes=[
            pltpu.VMEM((2, side, cols_total), jnp.float32),
            pltpu.SemaphoreType.DMA((cols_total // side,)),
        ],
        compiler_params=params(28),
        name="late",
    )(*tables, total, *terms, copied)


def local(phase, absorption, probe, measured, offsets):
    side = probe.shape[-1]
    cols_total = phase.shape[2]
    sections = lax.axis_size("slab")
    each = offsets.shape[0] // sections
    n_up = each // 2
    n_here = each - n_up
    distances = list(range(sections))

    pairs = offsets.T
    here = lambda k, d: (k, n_here, d)
    up = lambda k, d: (sections * n_here + k, n_up, d)
    back = lambda d: (sections - d) % sections

    far = distances[1:]
    phase = pltpu.with_memory_space_constraint(phase, pltpu.HBM)
    absorption = pltpu.with_memory_space_constraint(absorption, pltpu.HBM)
    measured = pltpu.with_memory_space_constraint(measured, pltpu.HBM)
    done = [pairs]

    def step(kernel, scalars, *args):
        out = kernel(after(scalars, *done), *args)
        done[:] = [out[0] if isinstance(out, (list, tuple)) else out]
        return out

    def cutter(table, kinds, *args):
        return step(lambda p: cut(kinds, p, phase, absorption, *args), table)

    def joiner(table, kind, *args):
        return step(lambda p: join(kind, p, *args), table)

    def slotter(table, kind, base, each, *args):
        return step(lambda p: run_slot(kind, base, each, p, probe, *args, constants), table)

    below = move(pairs, "tile", 1)
    lower = [
        cutter(pairs, [up(k, d) for d in distances], measured, (up(k, 0)[0], n_up))
        for k in range(n_up)
    ]
    extra = [[rotate_last(lower[k][d], d) for d in far] for k in range(n_up)]
    raised = [[move(after(lower[k][d], below), "tile", 1) for d in far] for k in range(n_up)]
    for k in range(n_up):
        raised[k].insert(0, move(after(lower[k][0], below), "tile", 1))
    low_cuts = [cutter(below, [here(k, d) for d in distances]) for k in range(n_here)]
    lowered = [[move(low_cuts[k][d], "tile", -1) for d in far] for k in range(n_here)]
    for k in range(n_here):
        lowered[k].insert(0, move(low_cuts[k][0], "tile", -1))
    up_cuts = [cutter(below, [up(k, d) for d in distances]) for k in range(n_up)]
    own_cuts = [cutter(pairs, [here(k, d) for d in distances]) for k in range(n_here)]
    constants = expand(side)
    up_joined = [
        [joiner(below, up(k, d), raised[k][d], up_cuts[k][d]) for d in far] for k in range(n_up)
    ]
    up_other = [[rotate(up_joined[k][d - 1], "slab", d) for d in far] for k in range(n_up)]
    here_joined = [
        [joiner(pairs, here(k, d), own_cuts[k][d], lowered[k][d]) for d in far]
        for k in range(n_here)
    ]
    here_other = [[rotate(here_joined[k][d - 1], "slab", d) for d in far] for k in range(n_here)]

    other_pairs, other_below = rotate(pairs, "batch", 1), rotate(below, "batch", 1)
    done += [other_pairs, other_below]
    tables = [pairs, below, other_pairs, other_below]

    up_outs = [
        slotter(
            below, "up", up(k, 0)[0], n_up, measured, [raised[k][0], up_cuts[k][0]], up_other[k]
        )
        for k in range(n_up)
    ]
    up_back = [[rotate(up_outs[k][d], "slab", d) for d in far] for k in range(n_up)]
    fallen = [move(up_outs[k][0], "tile", -1) for k in range(n_up)]
    here_outs = [
        slotter(
            pairs, "here", here(k, 0)[0], n_here, measured,
            [own_cuts[k][0], lowered[k][0]], here_other[k],
        )
        for k in range(n_here)
    ]
    last_outs = [
        slotter(pairs, "last", up(k, 0)[0], n_up, measured, [lower[k][0]], extra[k])
        for k in range(n_up)
    ]
    here_back = [[rotate(here_outs[k][d], "slab", d) for d in far] for k in range(n_here)]
    risen = [move(here_outs[k][0], "tile", 1) for k in range(n_here)]

    twin = lambda kind: (kind[0] + 2, kind[1], kind[2])
    terms, kinds = [], []

    def group(items, gate=None):
        values = [value for value, kind in items]
        if gate is not None:
            values[0] = after(values[0], gate)
        twins = rotate(pack(values), "batch", 1)
        terms.extend(values + [twins])
        kinds.extend([kind for value, kind in items] + [[twin(kind) for value, kind in items]])
        return twins

    items = []
    for k in range(n_up):
        items.append((last_outs[k][0], (0, up(k, 0), "last")))
        items.append((up_outs[k][0], (1, up(k, 0), "below")))
        items.append((fallen[k], (0, up(k, 0), "inner")))
        for d in far:
            items.append((up_back[k][d - 1], (1, up(k, back(d)), "below")))
    if items:
        group(items)
    falling = [[move(value, "tile", -1) for value in row] for row in up_back]
    rising = [[move(value, "tile", 1) for value in row] for row in here_back]
    ending = [
        [rotate_last(after(last_outs[k][d], *here_back[0]), d) for d in far] for k in range(n_up)
    ]
    items = []
    for k in range(n_here):
        items.append((here_outs[k][0], (0, here(k, 0), "above")))
        for d in far:
            items.append((here_back[k][d - 1], (0, here(k, back(d)), "above")))
        items.append((risen[k], (1, here(k, 0), "below")))
    group(items)
    total, copied = early(kinds, tables, terms, cols_total)
    final, final_kinds = [], []

    def add(value, kind):
        final.extend([value, rotate(after(value, total), "batch", 1)])
        final_kinds.extend([kind, twin(kind)])

    for k in range(n_up):
        for d in far:
            add(falling[k][d - 1], (0, up(k, back(d)), "inner"))
            add(ending[k][d - 1], (0, up(k, back(d)), "last"))
    for k in range(n_here):
        for d in far:
            add(rising[k][d - 1], (1, here(k, back(d)), "below"))
    return late(final_kinds, tables, total, copied, final)


def solution(mesh):
    in_specs = (
        P(("groups", "slab"), "tile", None),
        P(("groups", "slab"), "tile", None),
        P(),
        P(("groups", "tile", "batch"), None, None),
        P(("groups", "tile", "batch"), None),
    )
    out_specs = P(None, ("groups", "slab"), "tile", None)
    return jax.shard_map(local, mesh=mesh, in_specs=in_specs, out_specs=out_specs, check_vma=False)
```

```python
import math

import numpy as np
import jax
import jax.numpy as jnp
from jax import lax
from jax.experimental import pallas as pl
from jax.experimental.pallas import tpu as pltpu
from jax.sharding import PartitionSpec as P

SIN = [(-1.0) ** k / math.factorial(2 * k + 1) for k in range(8)]
COS = [(-1.0) ** k / math.factorial(2 * k) for k in range(8)]
VMEM = pl.BlockSpec(memory_space=pltpu.VMEM)
SMEM = pl.BlockSpec(memory_space=pltpu.SMEM)
HBM = pl.BlockSpec(memory_space=pltpu.HBM)


def params(mib):
    return pltpu.CompilerParams(vmem_limit_bytes=mib << 20)


def cost(microseconds):
    return pl.CostEstimate(flops=int(microseconds * 1e9), transcendentals=0, bytes_accessed=0)


def after(value, *others):
    return lax.optimization_barrier((value, *others))[0]


def move(block, axis, distance):
    size = lax.axis_size(axis)
    route = [(i, i + distance) for i in range(size) if 0 <= i + distance < size]
    return lax.ppermute(block, axis, route)


def rotate(block, axis, distance):
    size = lax.axis_size(axis)
    return lax.ppermute(block, axis, [(i, (i + distance) % size) for i in range(size)])


def rotate_last(block, distance):
    tiles, size = lax.axis_size("tile"), lax.axis_size("slab")
    base = (tiles - 1) * size
    route = [(base + i, base + (i + distance) % size) for i in range(size)]
    return lax.ppermute(block, ("tile", "slab"), route)


def halves(matrix):
    high = matrix.astype(np.float32).astype(jnp.bfloat16)
    low = (matrix - high.astype(np.float64)).astype(np.float32).astype(jnp.bfloat16)
    return [high, low]


def compact_tables(side):
    index = np.arange(side)
    fourier = np.exp(-2j * np.pi * (index[:, None] * index[None, :] % side) / side)
    wavenumber = np.where(index < side // 2, index, index - side)
    kernel = np.exp(-1j * np.pi * (wavenumber * wavenumber % (8 * side)) / (4 * side))
    line = np.fft.ifft(kernel)
    line = (line + line[-index % side]) / 2
    fresnel = line[(index[:, None] - index[None, :]) % side]
    scaled = fourier / math.sqrt(side)
    pieces = []
    for matrix in (fresnel, scaled):
        pieces += halves(matrix.real) + halves(matrix.imag)
    return np.stack(pieces)


def expand_kernel(pieces, *outs):
    side = pieces.shape[-1]
    for which in range(2):
        left, right = outs[2 * which], outs[2 * which + 1]
        real_high, real_low, imag_high, imag_low = [pieces[4 * which + k] for k in range(4)]
        real = [real_high, real_low, real_high]
        imag = [imag_high, imag_low, imag_high]
        minus = [-imag_high, -imag_low, -imag_high]
        for column, blocks in enumerate((real + minus, imag + real)):
            for row, block in enumerate(blocks):
                rows, cols = pl.ds(row * side, side), pl.ds(column * side, side)
                right[rows, cols] = block
                left[cols, rows] = block


def expand(side):
    pieces = jnp.asarray(compact_tables(side))
    left = jax.ShapeDtypeStruct((2 * side, 6 * side), jnp.bfloat16)
    right = jax.ShapeDtypeStruct((6 * side, 2 * side), jnp.bfloat16)
    return pl.pallas_call(
        expand_kernel,
        in_specs=[VMEM],
        out_specs=[VMEM] * 4,
        out_shape=[left, right, left, right],
        compiler_params=params(16),
        name="expand",
    )(pieces)


def split(value):
    high = value.astype(jnp.bfloat16)
    low = (value - high.astype(jnp.float32)).astype(jnp.bfloat16)
    return high, low


def two_sided(left, right, real, imag):
    side = real.shape[-1]
    real_high, real_low = split(real)
    imag_high, imag_low = split(imag)
    wide = jnp.concatenate([real_high, real_high, real_low, imag_high, imag_high, imag_low], axis=1)
    inner = jnp.dot(wide, right[...], preferred_element_type=jnp.float32)
    real_high, real_low = split(inner[:, :side])
    imag_high, imag_low = split(inner[:, side:])
    tall = jnp.concatenate([real_high, real_high, real_low, imag_high, imag_high, imag_low], axis=0)
    outer = jnp.dot(left[...], tall, preferred_element_type=jnp.float32)
    return outer[:side], outer[side:]


def transmission(phase, absorption):
    square = phase * phase
    sine = jnp.full_like(phase, SIN[-1])
    cosine = jnp.full_like(phase, COS[-1])
    for a, b in zip(SIN[-2::-1], COS[-2::-1]):
        sine = sine * square + a
        cosine = cosine * square + b
    damping = jnp.exp(-absorption)
    return damping * cosine, damping * sine * phase


def slot_kernel(kind, *args):
    if kind == "last":

        @pl.when(lax.axis_index("tile") == lax.axis_size("tile") - 1)
        def _():
            slot_body(kind, *args)
    else:
        slot_body(kind, *args)


def slot_body(kind, base, each, sections, pairs, probe, measured, *refs):
    pieces = 1 if kind == "last" else 2
    own = refs[:pieces]
    others = refs[pieces : pieces + sections - 1]
    refs = refs[pieces + sections - 1 :]
    prop_left, prop_right, dft_left, dft_right = refs[:4]
    outs = refs[4 : 4 + sections]
    wave, trans = refs[4 + sections : 6 + sections]
    side = probe.shape[-1]
    slab = lax.axis_index("slab")
    index = base + slab * each
    row = lax.rem(pairs[0, index], side)
    col = lax.rem(pairs[1, index], side)
    if kind == "up":
        amplitude = own[0].at[2]
        fetch = None
    else:
        amplitude, sem = refs[6 + sections :]
        fetch = pltpu.make_async_copy(measured.at[index], amplitude, sem)
        fetch.start()
    rows = lax.broadcasted_iota(jnp.int32, (side, side), 0)
    patch = [own[0][0], own[0][1]]
    if pieces == 2:
        patch = [jnp.where(rows >= row, own[0][k], own[1][k]) for k in range(2)]
    trans[slab, 0], trans[slab, 1] = transmission(patch[0], patch[1])
    for distance in range(1, sections):
        owner = lax.rem(slab + (sections - distance), sections)
        real, imag = transmission(others[distance - 1][0], others[distance - 1][1])
        trans[owner, 0] = real
        trans[owner, 1] = imag
    for part in range(2):
        wave[0, part] = pltpu.roll(pltpu.roll(probe[part], row, 0), col, 1)
    for step in range(sections):
        a, b, c, d = wave[step, 0], wave[step, 1], trans[step, 0], trans[step, 1]
        real, imag = a * c - b * d, a * d + b * c
        if step < sections - 1:
            real, imag = two_sided(prop_left, prop_right, real, imag)
            wave[step + 1, 0] = real
            wave[step + 1, 1] = imag
    real, imag = two_sided(dft_left, dft_right, real, imag)
    if fetch is not None:
        fetch.wait()
    factor = 1.0 - amplitude[...] * lax.rsqrt(jnp.maximum(real * real + imag * imag, 0.25))
    real, minus = two_sided(dft_left, dft_right, real * factor, -imag * factor)
    for step in range(sections - 1, -1, -1):
        a, b = wave[step, 0], wave[step, 1]
        wave[step, 0] = a * real - b * minus
        wave[step, 1] = -(a * minus + b * real)
        if step > 0:
            c, d = trans[step, 0], trans[step, 1]
            real, minus = c * real - d * minus, c * minus + d * real
            real, minus = two_sided(prop_left, prop_right, real, minus)
    for distance in range(sections):
        outs[distance][...] = wave[lax.rem(slab + distance, sections)]


def run_slot(kind, base, each, pairs, probe, measured, own, others, constants):
    sections = len(others) + 1
    side = probe.shape[-1]
    shape = jax.ShapeDtypeStruct((2, side, side), jnp.float32)
    scratch = [pltpu.VMEM((sections, 2, side, side), jnp.float32)] * 2
    if kind != "up":
        scratch += [pltpu.VMEM((side, side), jnp.float32), pltpu.SemaphoreType.DMA(())]
    return pl.pallas_call(
        lambda *refs: slot_kernel(kind, base, each, sections, *refs),
        in_specs=[SMEM, VMEM, HBM]
        + [VMEM] * (len(own) + len(others) + 4),
        out_specs=[VMEM] * sections,
        out_shape=[shape] * sections,
        scratch_shapes=scratch,
        compiler_params=params(32),
        name="slot_" + kind,
    )(pairs, probe, measured, *own, *others, *constants)


def position(k, bases, slab, sections):
    base, each, distance = bases[k]
    return base + lax.rem(slab + distance, sections) * each


def cut_kernel(bases, sections, send, pairs, phase, absorption, *refs):
    count = len(bases)
    side = phase.shape[1]
    blocks = phase.shape[2] // side
    slab = lax.axis_index("slab")
    extra = None
    if send is not None:
        extra = (refs[0].at[send[0] + slab * send[1]], refs[1].at[2], refs[-3])
        extra = pltpu.make_async_copy(*extra)
        refs = refs[1:]
    outs = refs[:count]
    buffer, sems = refs[-2], refs[-1]
    copies, columns = [], []
    for k in range(count):
        column = pairs[1, position(k, bases, slab, sections)]
        first = lax.div(column, side)
        columns.append(lax.rem(column, side))
        for which, source in enumerate((phase, absorption)):
            for half in range(2):
                block = first if half == 0 else jnp.minimum(first + 1, blocks - 1)
                copies.append(
                    pltpu.make_async_copy(
                        source.at[0, :, pl.ds(pl.multiple_of(block * side, side), side)],
                        buffer.at[k, which, half],
                        sems.at[k, which, half],
                    )
                )
    for copy in copies:
        copy.start()
    if extra is not None:
        extra.start()
    lane = lax.broadcasted_iota(jnp.int32, (side, side), 1)
    for k in range(count):
        own = lane >= columns[k]
        for which in range(2):
            for half in range(2):
                copies[4 * k + 2 * which + half].wait()
            outs[k][which] = jnp.where(own, buffer[k, which, 0], buffer[k, which, 1])
    if extra is not None:
        extra.wait()


def cut(bases, pairs, phase, absorption, measured=None, send=None):
    side = phase.shape[1]
    count = len(bases)
    sections = lax.axis_size("slab")
    shapes = [jax.ShapeDtypeStruct((2, side, side), jnp.float32)] * count
    scratch = [
        pltpu.VMEM((count, 2, 2, side, side), jnp.float32),
        pltpu.SemaphoreType.DMA((count, 2, 2)),
    ]
    inputs = [pairs, phase, absorption]
    if send is not None:
        shapes = [jax.ShapeDtypeStruct((3, side, side), jnp.float32)] + shapes[1:]
        scratch = [pltpu.SemaphoreType.DMA(())] + scratch
        inputs.append(measured)
    return pl.pallas_call(
        lambda *refs: cut_kernel(bases, sections, send, *refs),
        in_specs=[SMEM] + [HBM] * (len(inputs) - 1),
        out_specs=[VMEM] * count,
        out_shape=shapes,
        scratch_shapes=scratch,
        compiler_params=params(16),
        name="cut",
    )(*inputs)


def join_kernel(bases, sections, pairs, here, there, out):
    side = out.shape[-1]
    slab = lax.axis_index("slab")
    row = lax.rem(pairs[0, position(0, bases, slab, sections)], side)
    rows = lax.broadcasted_iota(jnp.int32, (side, side), 0)
    for part in range(2):
        out[part] = jnp.where(rows >= row, here[part], there[part])


def join(base, pairs, here, there):
    sections = lax.axis_size("slab")
    return pl.pallas_call(
        lambda *refs: join_kernel([base], sections, *refs),
        in_specs=[SMEM, VMEM, VMEM],
        out_specs=VMEM,
        out_shape=jax.ShapeDtypeStruct(here.shape, jnp.float32),
        compiler_params=params(8),
        name="join",
    )(pairs, here, there)


def pack_kernel(*refs):
    out = refs[-1]
    for k, term in enumerate(refs[:-1]):
        out[k] = term[...]


def pack(terms):
    if len(terms) == 1:
        return terms[0][None]
    return pl.pallas_call(
        pack_kernel,
        in_specs=[VMEM] * len(terms),
        out_specs=VMEM,
        out_shape=jax.ShapeDtypeStruct((len(terms), *terms[0].shape), jnp.float32),
        compiler_params=params(8),
        name="pack",
    )(*terms)


def spread(metas, terms):
    views, kinds = [], []
    for kind, term in zip(metas, terms):
        if isinstance(kind, list):
            views += [term.at[i] for i in range(len(kind))]
            kinds += kind
        else:
            views.append(term)
            kinds.append(kind)
    return views, kinds


def spans(metas, tables, side, sections):
    slab = lax.axis_index("slab")
    last = lax.axis_index("tile") == lax.axis_size("tile") - 1
    out = []
    for source, base, mode in metas:
        index = position(0, [base], slab, sections)
        row, col = tables[source][0, index], tables[source][1, index]
        row = lax.rem(row, side)
        low, high = row, jnp.int32(side)
        if mode == "below":
            low, high = jnp.int32(0), row
        elif mode == "last":
            low = jnp.where(last, row, side)
        elif mode == "inner":
            low = jnp.where(last, side, row)
        out.append((lax.div(col, side), lax.rem(col, side), low, high))
    return out


def early_kernel(metas, sections, *refs):
    count = len(metas)
    tables, terms = refs[:4], refs[4 : 4 + count]
    out, copied, sem = refs[4 + count :]
    terms, metas = spread(metas, terms)
    side = terms[0].shape[-1]
    blocks = out.shape[-1] // side
    rows = lax.broadcasted_iota(jnp.int32, (side, side), 0)
    lane = lax.broadcasted_iota(jnp.int32, (side, side), 1)

    @pl.loop(0, blocks)
    def _(block):
        out[:, :, pl.ds(pl.multiple_of(block * side, side), side)] = jnp.zeros((2, side, side), jnp.float32)

    for k, (first, col, low, high) in enumerate(spans(metas, tables, side, sections)):
        for half in range(2):
            block = first + half

            @pl.when((block < blocks) & (high > low))
            def _():
                keep = (rows >= low) & (rows < high)
                keep = keep & ((lane < col) if half else (lane >= col))
                place = pl.ds(pl.multiple_of(block * side, side), side)
                for part in range(2):
                    out[part, :, place] += jnp.where(keep, terms[k][part], 0.0)

    copy = pltpu.make_async_copy(out, copied.at[:, 0], sem)
    copy.start()
    copy.wait()


def early(metas, tables, terms, cols_total):
    side = terms[0].shape[-1]
    sections = lax.axis_size("slab")
    return pl.pallas_call(
        lambda *refs: early_kernel(metas, sections, *refs),
        in_specs=[SMEM] * 4 + [VMEM] * len(terms),
        out_specs=[VMEM, HBM],
        out_shape=[
            jax.ShapeDtypeStruct((2, side, cols_total), jnp.float32),
            jax.ShapeDtypeStruct((2, 1, side, cols_total), jnp.float32),
        ],
        scratch_shapes=[pltpu.SemaphoreType.DMA(())],
        compiler_params=params(20),
        name="early",
    )(*tables, *terms)


def late_kernel(metas, sections, *refs):
    count = len(metas)
    tables, total, terms = refs[:4], refs[4], refs[5 : 5 + count]
    out, stage, sems = refs[6 + count :]
    side = terms[0].shape[-1]
    blocks = out.shape[-1] // side
    rows = lax.broadcasted_iota(jnp.int32, (side, side), 0)
    lane = lax.broadcasted_iota(jnp.int32, (side, side), 1)
    ranges = spans(metas, tables, side, sections)

    def place(block):
        return pl.ds(pl.multiple_of(block * side, side), side)

    def send(block):
        where = place(block)
        return pltpu.make_async_copy(stage.at[:, :, where], out.at[:, 0, :, where], sems.at[block])

    def touched(block):
        hit = jnp.bool_(False)
        for first, col, low, high in ranges:
            hit = hit | (((block == first) | (block == first + 1)) & (high > low))
        return hit

    @pl.loop(0, blocks)
    def _(block):
        @pl.when(touched(block))
        def _():
            where = place(block)
            stage[:, :, where] = total[:, :, where]
            for k, (first, col, low, high) in enumerate(ranges):
                for half in range(2):

                    @pl.when((first + half == block) & (high > low))
                    def _():
                        keep = (rows >= low) & (rows < high)
                        keep = keep & ((lane < col) if half else (lane >= col))
                        for part in range(2):
                            stage[part, :, where] += jnp.where(keep, terms[k][part], 0.0)

            send(block).start()

    @pl.loop(0, blocks)
    def _(block):
        @pl.when(touched(block))
        def _():
            send(block).wait()


def late(metas, tables, total, copied, terms):
    side = terms[0].shape[-1]
    cols_total = total.shape[-1]
    sections = lax.axis_size("slab")
    return pl.pallas_call(
        lambda *refs: late_kernel(metas, sections, *refs),
        in_specs=[SMEM] * 4 + [VMEM] * (1 + len(terms)) + [HBM],
        out_specs=HBM,
        input_output_aliases={5 + len(terms): 0},
        out_shape=jax.ShapeDtypeStruct((2, 1, side, cols_total), jnp.float32),
        scratch_shapes=[
            pltpu.VMEM((2, side, cols_total), jnp.float32),
            pltpu.SemaphoreType.DMA((cols_total // side,)),
        ],
        compiler_params=params(28),
        name="late",
    )(*tables, total, *terms, copied)


def local(phase, absorption, probe, measured, offsets):
    side = probe.shape[-1]
    cols_total = phase.shape[2]
    sections = lax.axis_size("slab")
    each = offsets.shape[0] // sections
    n_up = each // 2
    n_here = each - n_up
    distances = list(range(sections))

    pairs = offsets.T
    here = lambda k, d: (k, n_here, d)
    up = lambda k, d: (sections * n_here + k, n_up, d)
    back = lambda d: (sections - d) % sections

    far = distances[1:]
    phase = pltpu.with_memory_space_constraint(phase, pltpu.HBM)
    absorption = pltpu.with_memory_space_constraint(absorption, pltpu.HBM)
    measured = pltpu.with_memory_space_constraint(measured, pltpu.HBM)
    done = [pairs]

    def step(kernel, scalars, *args):
        out = kernel(after(scalars, *done), *args)
        done[:] = [out[0] if isinstance(out, (list, tuple)) else out]
        return out

    def cutter(table, kinds, *args):
        return step(lambda p: cut(kinds, p, phase, absorption, *args), table)

    def joiner(table, kind, *args):
        return step(lambda p: join(kind, p, *args), table)

    def slotter(table, kind, base, each, *args):
        return step(lambda p: run_slot(kind, base, each, p, probe, *args, constants), table)

    below = move(pairs, "tile", 1)
    lower = [
        cutter(pairs, [up(k, d) for d in distances], measured, (up(k, 0)[0], n_up))
        for k in range(n_up)
    ]
    extra = [[rotate_last(after(lower[k][d], below), d) for d in far] for k in range(n_up)]
    raised = [[move(after(lower[k][d], below), "tile", 1) for d in far] for k in range(n_up)]
    for k in range(n_up):
        raised[k].insert(0, move(after(lower[k][0], below), "tile", 1))
    low_cuts = [cutter(below, [here(k, d) for d in distances]) for k in range(n_here)]
    lowered = [[move(low_cuts[k][d], "tile", -1) for d in far] for k in range(n_here)]
    for k in range(n_here):
        lowered[k].insert(0, move(low_cuts[k][0], "tile", -1))
    up_cuts = [cutter(below, [up(k, d) for d in distances]) for k in range(n_up)]
    own_cuts = [cutter(pairs, [here(k, d) for d in distances]) for k in range(n_here)]
    constants = expand(side)
    done += [value for row in extra for value in row]
    up_joined = [
        [joiner(below, up(k, d), raised[k][d], up_cuts[k][d]) for d in far] for k in range(n_up)
    ]
    up_other = [[rotate(up_joined[k][d - 1], "slab", d) for d in far] for k in range(n_up)]
    here_joined = [
        [joiner(pairs, here(k, d), own_cuts[k][d], lowered[k][d]) for d in far]
        for k in range(n_here)
    ]
    here_other = [[rotate(here_joined[k][d - 1], "slab", d) for d in far] for k in range(n_here)]

    other_pairs, other_below = rotate(pairs, "batch", 1), rotate(below, "batch", 1)
    done += [other_pairs, other_below]
    tables = [pairs, below, other_pairs, other_below]

    up_outs = [
        slotter(
            below, "up", up(k, 0)[0], n_up, measured, [raised[k][0], up_cuts[k][0]], up_other[k]
        )
        for k in range(n_up)
    ]
    up_back = [[rotate(up_outs[k][d], "slab", d) for d in far] for k in range(n_up)]
    fallen = [move(up_outs[k][0], "tile", -1) for k in range(n_up)]
    here_outs = [
        slotter(
            pairs, "here", here(k, 0)[0], n_here, measured,
            [own_cuts[k][0], lowered[k][0]], here_other[k],
        )
        for k in range(n_here)
    ]
    last_outs = [
        slotter(pairs, "last", up(k, 0)[0], n_up, measured, [lower[k][0]], extra[k])
        for k in range(n_up)
    ]
    here_back = [[rotate(here_outs[k][d], "slab", d) for d in far] for k in range(n_here)]
    risen = [move(here_outs[k][0], "tile", 1) for k in range(n_here)]

    twin = lambda kind: (kind[0] + 2, kind[1], kind[2])
    terms, kinds = [], []

    def group(items, gate=None):
        values = [value for value, kind in items]
        if gate is not None:
            values[0] = after(values[0], gate)
        twins = rotate(pack(values), "batch", 1)
        terms.extend(values + [twins])
        kinds.extend([kind for value, kind in items] + [[twin(kind) for value, kind in items]])
        return twins

    items = []
    for k in range(n_up):
        items.append((last_outs[k][0], (0, up(k, 0), "last")))
        items.append((up_outs[k][0], (1, up(k, 0), "below")))
        items.append((fallen[k], (0, up(k, 0), "inner")))
        for d in far:
            items.append((up_back[k][d - 1], (1, up(k, back(d)), "below")))
    if items:
        group(items)
    falling = [[move(value, "tile", -1) for value in row] for row in up_back]
    rising = [[move(value, "tile", 1) for value in row] for row in here_back]
    ending = [
        [rotate_last(after(last_outs[k][d], *here_back[0]), d) for d in far] for k in range(n_up)
    ]
    items = []
    for k in range(n_here):
        items.append((here_outs[k][0], (0, here(k, 0), "above")))
        for d in far:
            items.append((here_back[k][d - 1], (0, here(k, back(d)), "above")))
        items.append((risen[k], (1, here(k, 0), "below")))
    group(items)
    total, copied = early(kinds, tables, terms, cols_total)
    final, final_kinds = [], []

    def add(value, kind):
        final.extend([value, rotate(after(value, total), "batch", 1)])
        final_kinds.extend([kind, twin(kind)])

    for k in range(n_up):
        for d in far:
            add(falling[k][d - 1], (0, up(k, back(d)), "inner"))
            add(ending[k][d - 1], (0, up(k, back(d)), "last"))
    for k in range(n_here):
        for d in far:
            add(rising[k][d - 1], (1, here(k, back(d)), "below"))
    return late(final_kinds, tables, total, copied, final)


def solution(mesh):
    in_specs = (
        P(("groups", "slab"), "tile", None),
        P(("groups", "slab"), "tile", None),
        P(),
        P(("groups", "tile", "batch"), None, None),
        P(("groups", "tile", "batch"), None),
    )
    out_specs = P(None, ("groups", "slab"), "tile", None)
    return jax.shard_map(local, mesh=mesh, in_specs=in_specs, out_specs=out_specs, check_vma=False)
```

```python
import math

import numpy as np
import jax
import jax.numpy as jnp
from jax import lax
from jax.experimental import pallas as pl
from jax.experimental.pallas import tpu as pltpu
from jax.sharding import PartitionSpec as P

SIN = [(-1.0) ** k / math.factorial(2 * k + 1) for k in range(8)]
COS = [(-1.0) ** k / math.factorial(2 * k) for k in range(8)]
VMEM = pl.BlockSpec(memory_space=pltpu.VMEM)
SMEM = pl.BlockSpec(memory_space=pltpu.SMEM)
HBM = pl.BlockSpec(memory_space=pltpu.HBM)


def params(mib):
    return pltpu.CompilerParams(vmem_limit_bytes=mib << 20)


def cost(microseconds):
    return pl.CostEstimate(flops=int(microseconds * 1e9), transcendentals=0, bytes_accessed=0)


def after(value, *others):
    return lax.optimization_barrier((value, *others))[0]


def move(block, axis, distance):
    size = lax.axis_size(axis)
    route = [(i, i + distance) for i in range(size) if 0 <= i + distance < size]
    return lax.ppermute(block, axis, route)


def rotate(block, axis, distance):
    size = lax.axis_size(axis)
    return lax.ppermute(block, axis, [(i, (i + distance) % size) for i in range(size)])


def swap(block, axis, phase):
    size = lax.axis_size(axis)
    route = []
    for lower in range(phase, size - 1, 2):
        route += [(lower, lower + 1), (lower + 1, lower)]
    return lax.ppermute(block, axis, route)


def rotate_last(block, distance):
    tiles, size = lax.axis_size("tile"), lax.axis_size("slab")
    base = (tiles - 1) * size
    route = [(base + i, base + (i + distance) % size) for i in range(size)]
    return lax.ppermute(block, ("tile", "slab"), route)


def halves(matrix):
    high = matrix.astype(np.float32).astype(jnp.bfloat16)
    low = (matrix - high.astype(np.float64)).astype(np.float32).astype(jnp.bfloat16)
    return [high, low]


def compact_tables(side):
    index = np.arange(side)
    fourier = np.exp(-2j * np.pi * (index[:, None] * index[None, :] % side) / side)
    wavenumber = np.where(index < side // 2, index, index - side)
    kernel = np.exp(-1j * np.pi * (wavenumber * wavenumber % (8 * side)) / (4 * side))
    line = np.fft.ifft(kernel)
    line = (line + line[-index % side]) / 2
    fresnel = line[(index[:, None] - index[None, :]) % side]
    scaled = fourier / math.sqrt(side)
    pieces = []
    for matrix in (fresnel, scaled):
        pieces += halves(matrix.real) + halves(matrix.imag)
    return np.stack(pieces)


def expand_kernel(pieces, *outs):
    side = pieces.shape[-1]
    for which in range(2):
        left, right = outs[2 * which], outs[2 * which + 1]
        real_high, real_low, imag_high, imag_low = [pieces[4 * which + k] for k in range(4)]
        real = [real_high, real_low, real_high]
        imag = [imag_high, imag_low, imag_high]
        minus = [-imag_high, -imag_low, -imag_high]
        for column, blocks in enumerate((real + minus, imag + real)):
            for row, block in enumerate(blocks):
                rows, cols = pl.ds(row * side, side), pl.ds(column * side, side)
                right[rows, cols] = block
                left[cols, rows] = block


def expand(side):
    pieces = jnp.asarray(compact_tables(side))
    left = jax.ShapeDtypeStruct((2 * side, 6 * side), jnp.bfloat16)
    right = jax.ShapeDtypeStruct((6 * side, 2 * side), jnp.bfloat16)
    return pl.pallas_call(
        expand_kernel,
        in_specs=[VMEM],
        out_specs=[VMEM] * 4,
        out_shape=[left, right, left, right],
        compiler_params=params(16),
        name="expand",
    )(pieces)


def split(value):
    high = value.astype(jnp.bfloat16)
    low = (value - high.astype(jnp.float32)).astype(jnp.bfloat16)
    return high, low


def two_sided(left, right, real, imag):
    side = real.shape[-1]
    real_high, real_low = split(real)
    imag_high, imag_low = split(imag)
    wide = jnp.concatenate([real_high, real_high, real_low, imag_high, imag_high, imag_low], axis=1)
    inner = jnp.dot(wide, right[...], preferred_element_type=jnp.float32)
    real_high, real_low = split(inner[:, :side])
    imag_high, imag_low = split(inner[:, side:])
    tall = jnp.concatenate([real_high, real_high, real_low, imag_high, imag_high, imag_low], axis=0)
    outer = jnp.dot(left[...], tall, preferred_element_type=jnp.float32)
    return outer[:side], outer[side:]


def transmission(phase, absorption):
    square = phase * phase
    sine = jnp.full_like(phase, SIN[-1])
    cosine = jnp.full_like(phase, COS[-1])
    for a, b in zip(SIN[-2::-1], COS[-2::-1]):
        sine = sine * square + a
        cosine = cosine * square + b
    damping = jnp.exp(-absorption)
    return damping * cosine, damping * sine * phase


def is_lower(phase):
    if isinstance(phase, str):
        return phase == "lo"
    return lax.rem(lax.axis_index("tile"), 2) == phase


def pick(lower, first, second):
    if isinstance(lower, bool):
        return first if lower else second
    return jnp.where(lower, first, second)


def locate(spot, layout, tables, twin=0):
    which, phase, k, distance = spot
    sections, n_here, n_up, side = layout
    owner = lax.rem(lax.axis_index("slab") + distance, sections)
    here, up = owner * n_here + k, sections * n_here + owner * n_up + k
    pairs, below = tables[2 * twin], tables[2 * twin + 1]
    lower = True if which == "last" else is_lower(phase)
    own, other = (here, up) if which == "slot" else (up, here)
    row = lax.rem(pick(lower, pairs[0, own], below[0, other]), side)
    col = pick(lower, pairs[1, own], below[1, other])
    low, high = pick(lower, row, jnp.int32(0)), pick(lower, jnp.int32(side), row)
    last = lax.axis_index("tile") == lax.axis_size("tile") - 1
    if which == "last":
        low = jnp.where(last, low, side)
    elif which == "swap":
        low = jnp.where(last & lower, side, low)
    return pick(lower, own, other), row, col, low, high


def slot_kernel(kind, *args):
    if kind == "last":

        @pl.when(lax.axis_index("tile") == lax.axis_size("tile") - 1)
        def _():
            slot_body(*args)
    else:
        slot_body(*args)


def slot_body(spot, layout, pairs, below, probe, measured, *refs):
    sections = layout[0]
    which, phase = spot[:2]
    pieces = 1 if which == "last" else 2
    own = refs[:pieces]
    others = refs[pieces : pieces + sections - 1]
    refs = refs[pieces + sections - 1 :]
    prop_left, prop_right, dft_left, dft_right = refs[:4]
    outs = refs[4 : 4 + sections]
    wave, trans, amplitude, sem = refs[4 + sections :]
    side = probe.shape[-1]
    slab = lax.axis_index("slab")
    index, row, col, low, high = locate(spot, layout, (pairs, below))
    col = lax.rem(col, side)
    lower = True if which == "last" else is_lower(phase)

    def fetch():
        return pltpu.make_async_copy(measured.at[index], amplitude, sem)

    if lower is True:
        fetch().start()
    elif lower is False:
        amplitude[...] = own[1][2]
    else:

        @pl.when(lower)
        def _():
            fetch().start()
            fetch().wait()

        @pl.when(jnp.logical_not(lower))
        def _():
            amplitude[...] = own[1][2]

    rows = lax.broadcasted_iota(jnp.int32, (side, side), 0)
    patch = [own[0][0], own[0][1]]
    if pieces == 2:
        local_rows = (rows >= low) & (rows < high)
        patch = [jnp.where(local_rows, own[0][k], own[1][k]) for k in range(2)]
    trans[slab, 0], trans[slab, 1] = transmission(patch[0], patch[1])
    for distance in range(1, sections):
        owner = lax.rem(slab + (sections - distance), sections)
        real, imag = transmission(others[distance - 1][0], others[distance - 1][1])
        trans[owner, 0] = real
        trans[owner, 1] = imag
    for part in range(2):
        wave[0, part] = pltpu.roll(pltpu.roll(probe[part], row, 0), col, 1)
    for step in range(sections):
        a, b, c, d = wave[step, 0], wave[step, 1], trans[step, 0], trans[step, 1]
        real, imag = a * c - b * d, a * d + b * c
        if step < sections - 1:
            real, imag = two_sided(prop_left, prop_right, real, imag)
            wave[step + 1, 0] = real
            wave[step + 1, 1] = imag
    real, imag = two_sided(dft_left, dft_right, real, imag)
    if lower is True:
        fetch().wait()
    factor = 1.0 - amplitude[...] * lax.rsqrt(jnp.maximum(real * real + imag * imag, 0.25))
    real, minus = two_sided(dft_left, dft_right, real * factor, -imag * factor)
    for step in range(sections - 1, -1, -1):
        a, b = wave[step, 0], wave[step, 1]
        wave[step, 0] = a * real - b * minus
        wave[step, 1] = -(a * minus + b * real)
        if step > 0:
            c, d = trans[step, 0], trans[step, 1]
            real, minus = c * real - d * minus, c * minus + d * real
            real, minus = two_sided(prop_left, prop_right, real, minus)
    for distance in range(sections):
        outs[distance][...] = wave[lax.rem(slab + distance, sections)]


def run_slot(kind, spot, layout, pairs, below, probe, measured, own, others, constants):
    sections, side = layout[0], layout[3]
    shape = jax.ShapeDtypeStruct((2, side, side), jnp.float32)
    return pl.pallas_call(
        lambda *refs: slot_kernel(kind, spot, layout, *refs),
        in_specs=[SMEM, SMEM, VMEM, HBM] + [VMEM] * (len(own) + len(others) + 4),
        out_specs=[VMEM] * sections,
        out_shape=[shape] * sections,
        scratch_shapes=[pltpu.VMEM((sections, 2, side, side), jnp.float32)] * 2
        + [pltpu.VMEM((side, side), jnp.float32), pltpu.SemaphoreType.DMA(())],
        compiler_params=params(32),
        name="slot_" + kind,
    )(pairs, below, probe, measured, *own, *others, *constants)


def cut_kernel(spots, layout, with_measured, pairs, below, phase, absorption, *refs):
    count, side = len(spots), layout[3]
    blocks = phase.shape[2] // side
    extra = None
    if with_measured:
        sections, n_here, n_up, side = layout
        index = sections * n_here + lax.axis_index("slab") * n_up + spots[0][2]
        extra = pltpu.make_async_copy(refs[0].at[index], refs[1].at[2], refs[-3])
        refs = refs[1:]
    outs = refs[:count]
    buffer, sems = refs[-2], refs[-1]
    copies, columns = [], []
    for k in range(count):
        column = locate(spots[k], layout, (pairs, below))[2]
        first = lax.div(column, side)
        columns.append(lax.rem(column, side))
        for which, source in enumerate((phase, absorption)):
            for half in range(2):
                block = first if half == 0 else jnp.minimum(first + 1, blocks - 1)
                copies.append(
                    pltpu.make_async_copy(
                        source.at[0, :, pl.ds(pl.multiple_of(block * side, side), side)],
                        buffer.at[k, which, half],
                        sems.at[k, which, half],
                    )
                )
    for copy in copies:
        copy.start()
    if extra is not None:
        extra.start()
    lane = lax.broadcasted_iota(jnp.int32, (side, side), 1)
    for k in range(count):
        own = lane >= columns[k]
        for which in range(2):
            for half in range(2):
                copies[4 * k + 2 * which + half].wait()
            outs[k][which] = jnp.where(own, buffer[k, which, 0], buffer[k, which, 1])
    if extra is not None:
        extra.wait()


def cut(spots, layout, pairs, below, phase, absorption, measured=None):
    side = layout[3]
    count = len(spots)
    shapes = [jax.ShapeDtypeStruct((2, side, side), jnp.float32)] * count
    scratch = [
        pltpu.VMEM((count, 2, 2, side, side), jnp.float32),
        pltpu.SemaphoreType.DMA((count, 2, 2)),
    ]
    inputs = [phase, absorption]
    if measured is not None:
        shapes = [jax.ShapeDtypeStruct((3, side, side), jnp.float32)] + shapes[1:]
        scratch = [pltpu.SemaphoreType.DMA(())] + scratch
        inputs.append(measured)
    return pl.pallas_call(
        lambda *refs: cut_kernel(spots, layout, measured is not None, *refs),
        in_specs=[SMEM, SMEM] + [HBM] * len(inputs),
        out_specs=[VMEM] * count,
        out_shape=shapes,
        scratch_shapes=scratch,
        compiler_params=params(16),
        name="cut",
    )(pairs, below, *inputs)


def join_kernel(spot, layout, pairs, below, here, there, out):
    side = layout[3]
    low, high = locate(spot, layout, (pairs, below))[3:]
    rows = lax.broadcasted_iota(jnp.int32, (side, side), 0)
    keep = (rows >= low) & (rows < high)
    for part in range(2):
        out[part] = jnp.where(keep, here[part], there[part])


def join(spot, layout, pairs, below, here, there):
    return pl.pallas_call(
        lambda *refs: join_kernel(spot, layout, *refs),
        in_specs=[SMEM, SMEM, VMEM, VMEM],
        out_specs=VMEM,
        out_shape=jax.ShapeDtypeStruct(here.shape, jnp.float32),
        compiler_params=params(8),
        name="join",
    )(pairs, below, here, there)


def pack_kernel(*refs):
    out = refs[-1]
    for k, term in enumerate(refs[:-1]):
        out[k] = term[...]


def pack(terms):
    if len(terms) == 1:
        return terms[0][None]
    return pl.pallas_call(
        pack_kernel,
        in_specs=[VMEM] * len(terms),
        out_specs=VMEM,
        out_shape=jax.ShapeDtypeStruct((len(terms), *terms[0].shape), jnp.float32),
        compiler_params=params(8),
        name="pack",
    )(*terms)


def spread(metas, terms):
    views, kinds = [], []
    for kind, term in zip(metas, terms):
        if isinstance(kind, list):
            views += [term.at[i] for i in range(len(kind))]
            kinds += kind
        else:
            views.append(term)
            kinds.append(kind)
    return views, kinds


def spans(metas, tables, layout):
    side = layout[3]
    out = []
    for twin, spot in metas:
        index, row, col, low, high = locate(spot, layout, tables, twin)
        out.append((lax.div(col, side), lax.rem(col, side), low, high))
    return out


def early_kernel(metas, layout, *refs):
    count = len(metas)
    tables, terms = refs[:4], refs[4 : 4 + count]
    out, copied, sem = refs[4 + count :]
    terms, metas = spread(metas, terms)
    side = terms[0].shape[-1]
    blocks = out.shape[-1] // side
    rows = lax.broadcasted_iota(jnp.int32, (side, side), 0)
    lane = lax.broadcasted_iota(jnp.int32, (side, side), 1)

    @pl.loop(0, blocks)
    def _(block):
        out[:, :, pl.ds(pl.multiple_of(block * side, side), side)] = jnp.zeros((2, side, side), jnp.float32)

    for k, (first, col, low, high) in enumerate(spans(metas, tables, layout)):
        for half in range(2):
            block = first + half

            @pl.when((block < blocks) & (high > low))
            def _():
                keep = (rows >= low) & (rows < high)
                keep = keep & ((lane < col) if half else (lane >= col))
                place = pl.ds(pl.multiple_of(block * side, side), side)
                for part in range(2):
                    out[part, :, place] += jnp.where(keep, terms[k][part], 0.0)

    copy = pltpu.make_async_copy(out, copied.at[:, 0], sem)
    copy.start()
    copy.wait()


def early(metas, layout, tables, terms, cols_total):
    side = layout[3]
    return pl.pallas_call(
        lambda *refs: early_kernel(metas, layout, *refs),
        in_specs=[SMEM] * 4 + [VMEM] * len(terms),
        out_specs=[VMEM, HBM],
        out_shape=[
            jax.ShapeDtypeStruct((2, side, cols_total), jnp.float32),
            jax.ShapeDtypeStruct((2, 1, side, cols_total), jnp.float32),
        ],
        scratch_shapes=[pltpu.SemaphoreType.DMA(())],
        compiler_params=params(20),
        name="early",
    )(*tables, *terms)


def late_kernel(metas, layout, *refs):
    count = len(metas)
    tables, total, terms = refs[:4], refs[4], refs[5 : 5 + count]
    out, stage, sems = refs[6 + count :]
    side = terms[0].shape[-1]
    blocks = out.shape[-1] // side
    rows = lax.broadcasted_iota(jnp.int32, (side, side), 0)
    lane = lax.broadcasted_iota(jnp.int32, (side, side), 1)
    ranges = spans(metas, tables, layout)

    def place(block):
        return pl.ds(pl.multiple_of(block * side, side), side)

    def send(block):
        where = place(block)
        return pltpu.make_async_copy(stage.at[:, :, where], out.at[:, 0, :, where], sems.at[block])

    def touched(block):
        hit = jnp.bool_(False)
        for first, col, low, high in ranges:
            hit = hit | (((block == first) | (block == first + 1)) & (high > low))
        return hit

    @pl.loop(0, blocks)
    def _(block):
        @pl.when(touched(block))
        def _():
            where = place(block)
            stage[:, :, where] = total[:, :, where]
            for k, (first, col, low, high) in enumerate(ranges):
                for half in range(2):

                    @pl.when((first + half == block) & (high > low))
                    def _():
                        keep = (rows >= low) & (rows < high)
                        keep = keep & ((lane < col) if half else (lane >= col))
                        for part in range(2):
                            stage[part, :, where] += jnp.where(keep, terms[k][part], 0.0)

            send(block).start()

    @pl.loop(0, blocks)
    def _(block):
        @pl.when(touched(block))
        def _():
            send(block).wait()


def late(metas, layout, tables, total, copied, terms):
    side = layout[3]
    cols_total = total.shape[-1]
    return pl.pallas_call(
        lambda *refs: late_kernel(metas, layout, *refs),
        in_specs=[SMEM] * 4 + [VMEM] * (1 + len(terms)) + [HBM],
        out_specs=HBM,
        input_output_aliases={5 + len(terms): 0},
        out_shape=jax.ShapeDtypeStruct((2, 1, side, cols_total), jnp.float32),
        scratch_shapes=[
            pltpu.VMEM((2, side, cols_total), jnp.float32),
            pltpu.SemaphoreType.DMA((cols_total // side,)),
        ],
        compiler_params=params(28),
        name="late",
    )(*tables, total, *terms, copied)


def local(phase, absorption, probe, measured, offsets):
    side = probe.shape[-1]
    cols_total = phase.shape[2]
    sections = lax.axis_size("slab")
    each = offsets.shape[0] // sections
    n_up = each // 2
    n_here = each - n_up
    distances = list(range(sections))

    layout = (sections, n_here, n_up, side)
    pairs = offsets.T
    below = move(pairs, "tile", 1)
    back = lambda d: (sections - d) % sections
    far = distances[1:]
    phase = pltpu.with_memory_space_constraint(phase, pltpu.HBM)
    absorption = pltpu.with_memory_space_constraint(absorption, pltpu.HBM)
    measured = pltpu.with_memory_space_constraint(measured, pltpu.HBM)

    rounds, last_round = [], {}
    for k in range(n_here):
        if n_here == n_up:
            last_round[k] = 2 * k + (lax.axis_size("tile") - 1) % 2
            for parity in range(2):
                there = lambda value, parity=parity: swap(value, "tile", parity)
                rounds.append((k, parity, parity, there, there))
        else:
            rise = lambda value: move(value, "tile", 1)
            fall = lambda value: move(value, "tile", -1)
            if k < n_up:
                last_round[k] = len(rounds)
                rounds.append((k, "hi", "lo", rise, fall))
            rounds.append((k, "lo", "hi", fall, rise))
    count = len(rounds)
    done = [pairs]

    def step(kernel):
        out = kernel(after(pairs, *done))
        done[:] = [out[0] if isinstance(out, (list, tuple)) else out]
        return out

    spots = [("send", rounds[i][2], rounds[i][0], d) for i in range(count) for d in far]
    pieces = step(lambda p: cut(spots, layout, p, below, phase, absorption)) if spots else []
    sent, got = [], []
    for i, (k, role, send_role, there, home) in enumerate(rounds):
        sent.append([None, *pieces[i * len(far) : (i + 1) * len(far)]])
        got.append([None] + [there(piece) for piece in sent[i][1:]])
    for i, (k, role, send_role, there, home) in enumerate(rounds):
        extra_input = [] if role == "lo" else [measured]
        spots = [("send", send_role, k, 0)]
        sent[i][0] = step(lambda p: cut(spots, layout, p, below, phase, absorption, *extra_input))[0]
        got[i][0] = there(sent[i][0])
    ends = sorted(last_round)
    extra = [[rotate_last(sent[last_round[k]][d], d) for d in far] for k in ends]
    held = []
    for k, role, send_role, there, home in rounds:
        spots = [("slot", role, k, d) for d in distances]
        held.append(step(lambda p: cut(spots, layout, p, below, phase, absorption)))
    constants = expand(side)
    done += [value for row in extra for value in row]
    others = []
    for i, (k, role, send_role, there, home) in enumerate(rounds):
        joined = []
        for d in far:
            spot = ("slot", role, k, d)
            joined.append(step(lambda p: join(spot, layout, p, below, held[i][d], got[i][d])))
        others.append([rotate(joined[d - 1], "slab", d) for d in far])

    other_pairs, other_below = rotate(pairs, "batch", 1), rotate(below, "batch", 1)
    done += [other_pairs, other_below]
    tables = [pairs, below, other_pairs, other_below]

    def slot(kind, spot, own, rest):
        return step(
            lambda p: run_slot(kind, spot, layout, p, below, probe, measured, own, rest, constants)
        )

    outs, backs, homes = [], [], []
    for i, (k, role, send_role, there, home) in enumerate(rounds):
        outs.append(slot(f"{i}", ("slot", role, k, 0), [held[i][0], got[i][0]], others[i]))
        backs.append([rotate(outs[i][d], "slab", d) for d in far])
        homes.append(home(outs[i][0]))
    last_outs = [
        slot("last", ("last", "lo", k, 0), [sent[last_round[k]][0]], extra[n])
        for n, k in enumerate(ends)
    ]
    terms, kinds = [], []

    def group(items):
        values = [value for value, spot in items]
        twins = rotate(pack(values), "batch", 1)
        terms.extend(values + [twins])
        kinds.extend([(0, spot) for value, spot in items] + [[(1, spot) for value, spot in items]])

    final, final_kinds = [], []
    ending = [
        [rotate_last(after(last_outs[n][d], *backs[-1]), d) for d in far] for n in range(len(ends))
    ]
    last_items = [(last_outs[n][0], ("last", "lo", k, 0)) for n, k in enumerate(ends)]
    for i, (k, role, send_role, there, home) in enumerate(rounds):
        items = [(outs[i][0], ("slot", role, k, 0))]
        items += [(backs[i][d - 1], ("slot", role, k, back(d))) for d in far]
        items.append((homes[i], ("swap", send_role, k, 0)))
        if i == 0:
            items = last_items + items
        group(items)
        for d in far:
            final.append((home(backs[i][d - 1]), ("swap", send_role, k, back(d))))
    for n, k in enumerate(ends):
        final += [(ending[n][d - 1], ("last", "lo", k, back(d))) for d in far]
    total, copied = early(kinds, layout, tables, terms, cols_total)
    values = []
    for value, spot in final:
        values += [value, rotate(after(value, total), "batch", 1)]
        final_kinds += [(0, spot), (1, spot)]
    return late(final_kinds, layout, tables, total, copied, values)


def solution(mesh):
    in_specs = (
        P(("groups", "slab"), "tile", None),
        P(("groups", "slab"), "tile", None),
        P(),
        P(("groups", "tile", "batch"), None, None),
        P(("groups", "tile", "batch"), None),
    )
    out_specs = P(None, ("groups", "slab"), "tile", None)
    return jax.shard_map(local, mesh=mesh, in_specs=in_specs, out_specs=out_specs, check_vma=False)
```

```python
import math

import numpy as np
import jax
import jax.numpy as jnp
from jax import lax
from jax.experimental import pallas as pl
from jax.experimental.pallas import tpu as pltpu
from jax.sharding import PartitionSpec as P

SIN = [(-1.0) ** k / math.factorial(2 * k + 1) for k in range(8)]
COS = [(-1.0) ** k / math.factorial(2 * k) for k in range(8)]
VMEM = pl.BlockSpec(memory_space=pltpu.VMEM)
SMEM = pl.BlockSpec(memory_space=pltpu.SMEM)
HBM = pl.BlockSpec(memory_space=pltpu.HBM)


def params(mib):
    return pltpu.CompilerParams(vmem_limit_bytes=mib << 20)


def cost(microseconds):
    return pl.CostEstimate(flops=int(microseconds * 1e9), transcendentals=0, bytes_accessed=0)


def after(value, *others):
    return lax.optimization_barrier((value, *others))[0]


def move(block, axis, distance):
    size = lax.axis_size(axis)
    route = [(i, i + distance) for i in range(size) if 0 <= i + distance < size]
    return lax.ppermute(block, axis, route)


def rotate(block, axis, distance):
    size = lax.axis_size(axis)
    return lax.ppermute(block, axis, [(i, (i + distance) % size) for i in range(size)])


def swap(block, axis, phase):
    size = lax.axis_size(axis)
    route = []
    for lower in range(phase, size - 1, 2):
        route += [(lower, lower + 1), (lower + 1, lower)]
    return lax.ppermute(block, axis, route)


def rotate_last(block, distance):
    tiles, size = lax.axis_size("tile"), lax.axis_size("slab")
    base = (tiles - 1) * size
    route = [(base + i, base + (i + distance) % size) for i in range(size)]
    return lax.ppermute(block, ("tile", "slab"), route)


def halves(matrix):
    high = matrix.astype(np.float32).astype(jnp.bfloat16)
    low = (matrix - high.astype(np.float64)).astype(np.float32).astype(jnp.bfloat16)
    return [high, low]


def compact_tables(side):
    index = np.arange(side)
    fourier = np.exp(-2j * np.pi * (index[:, None] * index[None, :] % side) / side)
    wavenumber = np.where(index < side // 2, index, index - side)
    kernel = np.exp(-1j * np.pi * (wavenumber * wavenumber % (8 * side)) / (4 * side))
    line = np.fft.ifft(kernel)
    line = (line + line[-index % side]) / 2
    fresnel = line[(index[:, None] - index[None, :]) % side]
    scaled = fourier / math.sqrt(side)
    pieces = []
    for matrix in (fresnel, scaled):
        pieces += halves(matrix.real) + halves(matrix.imag)
    return np.stack(pieces)


def expand_kernel(pieces, *outs):
    side = pieces.shape[-1]
    for which in range(2):
        left, right = outs[2 * which], outs[2 * which + 1]
        real_high, real_low, imag_high, imag_low = [pieces[4 * which + k] for k in range(4)]
        real = [real_high, real_low, real_high]
        imag = [imag_high, imag_low, imag_high]
        minus = [-imag_high, -imag_low, -imag_high]
        for column, blocks in enumerate((real + minus, imag + real)):
            for row, block in enumerate(blocks):
                rows, cols = pl.ds(row * side, side), pl.ds(column * side, side)
                right[rows, cols] = block
                left[cols, rows] = block


def expand(side):
    pieces = jnp.asarray(compact_tables(side))
    left = jax.ShapeDtypeStruct((2 * side, 6 * side), jnp.bfloat16)
    right = jax.ShapeDtypeStruct((6 * side, 2 * side), jnp.bfloat16)
    return pl.pallas_call(
        expand_kernel,
        in_specs=[VMEM],
        out_specs=[VMEM] * 4,
        out_shape=[left, right, left, right],
        compiler_params=params(16),
        name="expand",
    )(pieces)


def split(value):
    high = value.astype(jnp.bfloat16)
    low = (value - high.astype(jnp.float32)).astype(jnp.bfloat16)
    return high, low


def two_sided(left, right, real, imag):
    side = real.shape[-1]
    real_high, real_low = split(real)
    imag_high, imag_low = split(imag)
    wide = jnp.concatenate([real_high, real_high, real_low, imag_high, imag_high, imag_low], axis=1)
    inner = jnp.dot(wide, right[...], preferred_element_type=jnp.float32)
    real_high, real_low = split(inner[:, :side])
    imag_high, imag_low = split(inner[:, side:])
    tall = jnp.concatenate([real_high, real_high, real_low, imag_high, imag_high, imag_low], axis=0)
    outer = jnp.dot(left[...], tall, preferred_element_type=jnp.float32)
    return outer[:side], outer[side:]


def transmission(phase, absorption):
    square = phase * phase
    sine = jnp.full_like(phase, SIN[-1])
    cosine = jnp.full_like(phase, COS[-1])
    for a, b in zip(SIN[-2::-1], COS[-2::-1]):
        sine = sine * square + a
        cosine = cosine * square + b
    damping = jnp.exp(-absorption)
    return damping * cosine, damping * sine * phase


def is_lower(phase):
    if isinstance(phase, str):
        return phase == "lo"
    return lax.rem(lax.axis_index("tile"), 2) == phase


def pick(lower, first, second):
    if isinstance(lower, bool):
        return first if lower else second
    return jnp.where(lower, first, second)


def locate(spot, layout, tables, twin=0):
    which, phase, k, distance = spot
    sections, n_here, n_up, side = layout
    owner = lax.rem(lax.axis_index("slab") + distance, sections)
    here, up = owner * n_here + k, sections * n_here + owner * n_up + k
    width = len(tables) // 2 if len(tables) > 3 else len(tables)
    pairs = tables[width * twin]
    below = tables[width * twin + 1 + (0 if isinstance(phase, str) else phase)]
    lower = True if which == "last" else is_lower(phase)
    own, other = (here, up) if which == "slot" else (up, here)
    row = lax.rem(pick(lower, pairs[0, own], below[0, other]), side)
    col = pick(lower, pairs[1, own], below[1, other])
    low, high = pick(lower, row, jnp.int32(0)), pick(lower, jnp.int32(side), row)
    last = lax.axis_index("tile") == lax.axis_size("tile") - 1
    if which == "last":
        low = jnp.where(last, low, side)
    elif which == "swap":
        low = jnp.where(last & lower, side, low)
    return pick(lower, own, other), row, col, low, high


def slot_kernel(kind, *args):
    if kind == "last":

        @pl.when(lax.axis_index("tile") == lax.axis_size("tile") - 1)
        def _():
            slot_body(*args)
    else:
        slot_body(*args)


def slot_body(spot, layout, n_tables, *refs):
    tables, (probe, measured), refs = refs[:n_tables], refs[n_tables : n_tables + 2], refs[n_tables + 2 :]
    sections = layout[0]
    which, phase = spot[:2]
    pieces = 1 if which == "last" else 2
    own = refs[:pieces]
    others = refs[pieces : pieces + sections - 1]
    refs = refs[pieces + sections - 1 :]
    prop_left, prop_right, dft_left, dft_right = refs[:4]
    outs = refs[4 : 4 + sections]
    wave, trans, amplitude, sem = refs[4 + sections :]
    side = probe.shape[-1]
    slab = lax.axis_index("slab")
    index, row, col, low, high = locate(spot, layout, tables)
    col = lax.rem(col, side)
    lower = True if which == "last" else is_lower(phase)

    def fetch():
        return pltpu.make_async_copy(measured.at[index], amplitude, sem)

    if lower is True:
        fetch().start()
    elif lower is False:
        amplitude[...] = own[1][2]
    else:

        @pl.when(lower)
        def _():
            fetch().start()
            fetch().wait()

        @pl.when(jnp.logical_not(lower))
        def _():
            amplitude[...] = own[1][2]

    rows = lax.broadcasted_iota(jnp.int32, (side, side), 0)
    patch = [own[0][0], own[0][1]]
    if pieces == 2:
        local_rows = (rows >= low) & (rows < high)
        patch = [jnp.where(local_rows, own[0][k], own[1][k]) for k in range(2)]
    trans[slab, 0], trans[slab, 1] = transmission(patch[0], patch[1])
    for distance in range(1, sections):
        owner = lax.rem(slab + (sections - distance), sections)
        real, imag = transmission(others[distance - 1][0], others[distance - 1][1])
        trans[owner, 0] = real
        trans[owner, 1] = imag
    for part in range(2):
        wave[0, part] = pltpu.roll(pltpu.roll(probe[part], row, 0), col, 1)
    for step in range(sections):
        a, b, c, d = wave[step, 0], wave[step, 1], trans[step, 0], trans[step, 1]
        real, imag = a * c - b * d, a * d + b * c
        if step < sections - 1:
            real, imag = two_sided(prop_left, prop_right, real, imag)
            wave[step + 1, 0] = real
            wave[step + 1, 1] = imag
    real, imag = two_sided(dft_left, dft_right, real, imag)
    if lower is True:
        fetch().wait()
    factor = 1.0 - amplitude[...] * lax.rsqrt(jnp.maximum(real * real + imag * imag, 0.25))
    real, minus = two_sided(dft_left, dft_right, real * factor, -imag * factor)
    for step in range(sections - 1, -1, -1):
        a, b = wave[step, 0], wave[step, 1]
        wave[step, 0] = a * real - b * minus
        wave[step, 1] = -(a * minus + b * real)
        if step > 0:
            c, d = trans[step, 0], trans[step, 1]
            real, minus = c * real - d * minus, c * minus + d * real
            real, minus = two_sided(prop_left, prop_right, real, minus)
    for distance in range(sections):
        outs[distance][...] = wave[lax.rem(slab + distance, sections)]


def run_slot(kind, spot, layout, tables, probe, measured, own, others, constants):
    sections, side = layout[0], layout[3]
    shape = jax.ShapeDtypeStruct((2, side, side), jnp.float32)
    return pl.pallas_call(
        lambda *refs: slot_kernel(kind, spot, layout, len(tables), *refs),
        in_specs=[SMEM] * len(tables) + [VMEM, HBM] + [VMEM] * (len(own) + len(others) + 4),
        out_specs=[VMEM] * sections,
        out_shape=[shape] * sections,
        scratch_shapes=[pltpu.VMEM((sections, 2, side, side), jnp.float32)] * 2
        + [pltpu.VMEM((side, side), jnp.float32), pltpu.SemaphoreType.DMA(())],
        compiler_params=params(32),
        name="slot_" + kind,
    )(*tables, probe, measured, *own, *others, *constants)


def cut_kernel(spots, layout, with_measured, n_tables, *refs):
    tables, (phase, absorption) = refs[:n_tables], refs[n_tables : n_tables + 2]
    refs = refs[n_tables + 2 :]
    count, side = len(spots), layout[3]
    blocks = phase.shape[2] // side
    extra = None
    if with_measured:
        sections, n_here, n_up, side = layout
        index = sections * n_here + lax.axis_index("slab") * n_up + spots[0][2]
        extra = pltpu.make_async_copy(refs[0].at[index], refs[1].at[2], refs[-3])
        refs = refs[1:]
    outs = refs[:count]
    buffer, sems = refs[-2], refs[-1]
    copies, columns = [], []
    for k in range(count):
        column = locate(spots[k], layout, tables)[2]
        first = lax.div(column, side)
        columns.append(lax.rem(column, side))
        for which, source in enumerate((phase, absorption)):
            for half in range(2):
                block = first if half == 0 else jnp.minimum(first + 1, blocks - 1)
                copies.append(
                    pltpu.make_async_copy(
                        source.at[0, :, pl.ds(pl.multiple_of(block * side, side), side)],
                        buffer.at[k, which, half],
                        sems.at[k, which, half],
                    )
                )
    for copy in copies:
        copy.start()
    if extra is not None:
        extra.start()
    lane = lax.broadcasted_iota(jnp.int32, (side, side), 1)
    for k in range(count):
        own = lane >= columns[k]
        for which in range(2):
            for half in range(2):
                copies[4 * k + 2 * which + half].wait()
            outs[k][which] = jnp.where(own, buffer[k, which, 0], buffer[k, which, 1])
    if extra is not None:
        extra.wait()


def cut(spots, layout, tables, phase, absorption, measured=None):
    side = layout[3]
    count = len(spots)
    shapes = [jax.ShapeDtypeStruct((2, side, side), jnp.float32)] * count
    scratch = [
        pltpu.VMEM((count, 2, 2, side, side), jnp.float32),
        pltpu.SemaphoreType.DMA((count, 2, 2)),
    ]
    inputs = [phase, absorption]
    if measured is not None:
        shapes = [jax.ShapeDtypeStruct((3, side, side), jnp.float32)] + shapes[1:]
        scratch = [pltpu.SemaphoreType.DMA(())] + scratch
        inputs.append(measured)
    return pl.pallas_call(
        lambda *refs: cut_kernel(spots, layout, measured is not None, len(tables), *refs),
        in_specs=[SMEM] * len(tables) + [HBM] * len(inputs),
        out_specs=[VMEM] * count,
        out_shape=shapes,
        scratch_shapes=scratch,
        compiler_params=params(16),
        name="cut",
    )(*tables, *inputs)


def join_kernel(spot, layout, *refs):
    tables, (here, there, out) = refs[:-3], refs[-3:]
    side = layout[3]
    low, high = locate(spot, layout, tables)[3:]
    rows = lax.broadcasted_iota(jnp.int32, (side, side), 0)
    keep = (rows >= low) & (rows < high)
    for part in range(2):
        out[part] = jnp.where(keep, here[part], there[part])


def join(spot, layout, tables, here, there):
    return pl.pallas_call(
        lambda *refs: join_kernel(spot, layout, *refs),
        in_specs=[SMEM] * len(tables) + [VMEM, VMEM],
        out_specs=VMEM,
        out_shape=jax.ShapeDtypeStruct(here.shape, jnp.float32),
        compiler_params=params(8),
        name="join",
    )(*tables, here, there)


def pack_kernel(*refs):
    out = refs[-1]
    for k, term in enumerate(refs[:-1]):
        out[k] = term[...]


def pack(terms):
    if len(terms) == 1:
        return terms[0][None]
    return pl.pallas_call(
        pack_kernel,
        in_specs=[VMEM] * len(terms),
        out_specs=VMEM,
        out_shape=jax.ShapeDtypeStruct((len(terms), *terms[0].shape), jnp.float32),
        compiler_params=params(8),
        name="pack",
    )(*terms)


def spread(metas, terms):
    views, kinds = [], []
    for kind, term in zip(metas, terms):
        if isinstance(kind, list):
            views += [term.at[i] for i in range(len(kind))]
            kinds += kind
        else:
            views.append(term)
            kinds.append(kind)
    return views, kinds


def spans(metas, tables, layout):
    side = layout[3]
    out = []
    for twin, spot in metas:
        index, row, col, low, high = locate(spot, layout, tables, twin)
        out.append((lax.div(col, side), lax.rem(col, side), low, high))
    return out


def early_kernel(metas, layout, *refs):
    out, copied, sem = refs[-3:]
    width = len(refs) - 3 - len(metas)
    tables, terms = refs[:width], refs[width:-3]
    terms, metas = spread(metas, terms)
    side = terms[0].shape[-1]
    blocks = out.shape[-1] // side
    rows = lax.broadcasted_iota(jnp.int32, (side, side), 0)
    lane = lax.broadcasted_iota(jnp.int32, (side, side), 1)

    @pl.loop(0, blocks)
    def _(block):
        out[:, :, pl.ds(pl.multiple_of(block * side, side), side)] = jnp.zeros((2, side, side), jnp.float32)

    for k, (first, col, low, high) in enumerate(spans(metas, tables, layout)):
        for half in range(2):
            block = first + half

            @pl.when((block < blocks) & (high > low))
            def _():
                keep = (rows >= low) & (rows < high)
                keep = keep & ((lane < col) if half else (lane >= col))
                place = pl.ds(pl.multiple_of(block * side, side), side)
                for part in range(2):
                    out[part, :, place] += jnp.where(keep, terms[k][part], 0.0)

    copy = pltpu.make_async_copy(out, copied.at[:, 0], sem)
    copy.start()
    copy.wait()


def early(metas, layout, tables, terms, cols_total):
    side = layout[3]
    return pl.pallas_call(
        lambda *refs: early_kernel(metas, layout, *refs),
        in_specs=[SMEM] * len(tables) + [VMEM] * len(terms),
        out_specs=[VMEM, HBM],
        out_shape=[
            jax.ShapeDtypeStruct((2, side, cols_total), jnp.float32),
            jax.ShapeDtypeStruct((2, 1, side, cols_total), jnp.float32),
        ],
        scratch_shapes=[pltpu.SemaphoreType.DMA(())],
        compiler_params=params(20),
        name="early",
    )(*tables, *terms)


def late_kernel(metas, layout, *refs):
    width = len(refs) - 5 - len(metas)
    tables, total, terms = refs[:width], refs[width], refs[width + 1 : -4]
    out, stage, sems = refs[-3:]
    side = terms[0].shape[-1]
    blocks = out.shape[-1] // side
    rows = lax.broadcasted_iota(jnp.int32, (side, side), 0)
    lane = lax.broadcasted_iota(jnp.int32, (side, side), 1)
    ranges = spans(metas, tables, layout)

    def place(block):
        return pl.ds(pl.multiple_of(block * side, side), side)

    def send(block):
        where = place(block)
        return pltpu.make_async_copy(stage.at[:, :, where], out.at[:, 0, :, where], sems.at[block])

    def touched(block):
        hit = jnp.bool_(False)
        for first, col, low, high in ranges:
            hit = hit | (((block == first) | (block == first + 1)) & (high > low))
        return hit

    @pl.loop(0, blocks)
    def _(block):
        @pl.when(touched(block))
        def _():
            where = place(block)
            stage[:, :, where] = total[:, :, where]
            for k, (first, col, low, high) in enumerate(ranges):
                for half in range(2):

                    @pl.when((first + half == block) & (high > low))
                    def _():
                        keep = (rows >= low) & (rows < high)
                        keep = keep & ((lane < col) if half else (lane >= col))
                        for part in range(2):
                            stage[part, :, where] += jnp.where(keep, terms[k][part], 0.0)

            send(block).start()

    @pl.loop(0, blocks)
    def _(block):
        @pl.when(touched(block))
        def _():
            send(block).wait()


def late(metas, layout, tables, total, copied, terms):
    side = layout[3]
    cols_total = total.shape[-1]
    return pl.pallas_call(
        lambda *refs: late_kernel(metas, layout, *refs),
        in_specs=[SMEM] * len(tables) + [VMEM] * (1 + len(terms)) + [HBM],
        out_specs=HBM,
        input_output_aliases={len(tables) + 1 + len(terms): 0},
        out_shape=jax.ShapeDtypeStruct((2, 1, side, cols_total), jnp.float32),
        scratch_shapes=[
            pltpu.VMEM((2, side, cols_total), jnp.float32),
            pltpu.SemaphoreType.DMA((cols_total // side,)),
        ],
        compiler_params=params(28),
        name="late",
    )(*tables, total, *terms, copied)


def local(phase, absorption, probe, measured, offsets):
    side = probe.shape[-1]
    cols_total = phase.shape[2]
    sections = lax.axis_size("slab")
    each = offsets.shape[0] // sections
    n_up = each // 2
    n_here = each - n_up
    distances = list(range(sections))

    layout = (sections, n_here, n_up, side)
    pairs = offsets.T
    if n_here == n_up:
        tables = [pairs] + [swap(pairs, "tile", parity) for parity in range(2)]
    else:
        tables = [pairs, move(pairs, "tile", 1)]
    back = lambda d: (sections - d) % sections
    far = distances[1:]
    phase = pltpu.with_memory_space_constraint(phase, pltpu.HBM)
    absorption = pltpu.with_memory_space_constraint(absorption, pltpu.HBM)
    measured = pltpu.with_memory_space_constraint(measured, pltpu.HBM)

    rounds, last_round = [], {}
    for k in range(n_here):
        if n_here == n_up:
            last_round[k] = 2 * k + (lax.axis_size("tile") - 1) % 2
            for parity in range(2):
                there = lambda value, parity=parity: swap(value, "tile", parity)
                rounds.append((k, parity, parity, there, there))
        else:
            rise = lambda value: move(value, "tile", 1)
            fall = lambda value: move(value, "tile", -1)
            if k < n_up:
                last_round[k] = len(rounds)
                rounds.append((k, "hi", "lo", rise, fall))
            rounds.append((k, "lo", "hi", fall, rise))
    count = len(rounds)
    done = [pairs]

    def step(kernel):
        out = kernel([after(pairs, *done)] + tables[1:])
        done[:] = [out[0] if isinstance(out, (list, tuple)) else out]
        return out

    spots = [("send", rounds[i][2], rounds[i][0], d) for i in range(count) for d in far]
    pieces = step(lambda p: cut(spots, layout, p, phase, absorption)) if spots else []
    sent, got = [], []
    for i, (k, role, send_role, there, home) in enumerate(rounds):
        sent.append([None, *pieces[i * len(far) : (i + 1) * len(far)]])
        got.append([None] + [there(piece) for piece in sent[i][1:]])
    for i, (k, role, send_role, there, home) in enumerate(rounds):
        extra_input = [] if role == "lo" else [measured]
        spots = [("send", send_role, k, 0)]
        sent[i][0] = step(lambda p: cut(spots, layout, p, phase, absorption, *extra_input))[0]
        got[i][0] = there(sent[i][0])
    ends = sorted(last_round)
    extra = [[rotate_last(sent[last_round[k]][d], d) for d in far] for k in ends]
    held = []
    for k, role, send_role, there, home in rounds:
        spots = [("slot", role, k, d) for d in distances]
        held.append(step(lambda p: cut(spots, layout, p, phase, absorption)))
    constants = expand(side)
    others = []
    for i, (k, role, send_role, there, home) in enumerate(rounds):
        joined = []
        for d in far:
            spot = ("slot", role, k, d)
            joined.append(step(lambda p: join(spot, layout, p, held[i][d], got[i][d])))
        others.append([rotate(joined[d - 1], "slab", d) for d in far])
        if i == 0:
            done += [value for row in extra for value in row]

    twin_tables = [rotate(table, "batch", 1) for table in tables]
    done += twin_tables

    def slot(kind, spot, own, rest):
        return step(
            lambda p: run_slot(kind, spot, layout, p, probe, measured, own, rest, constants)
        )

    outs, backs, homes = [], [], []
    for i, (k, role, send_role, there, home) in enumerate(rounds):
        outs.append(slot(f"{i}", ("slot", role, k, 0), [held[i][0], got[i][0]], others[i]))
        backs.append([rotate(outs[i][d], "slab", d) for d in far])
        homes.append(home(outs[i][0]))
    last_outs = [
        slot("last", ("last", "lo", k, 0), [sent[last_round[k]][0]], extra[n])
        for n, k in enumerate(ends)
    ]
    terms, kinds = [], []

    def group(items):
        values = [value for value, spot in items]
        twins = rotate(pack(values), "batch", 1)
        terms.extend(values + [twins])
        kinds.extend([(0, spot) for value, spot in items] + [[(1, spot) for value, spot in items]])
        return twins

    final, final_kinds = [], []
    ending = [
        [rotate_last(after(last_outs[n][d], *backs[-1]), d) for d in far] for n in range(len(ends))
    ]
    for n, k in enumerate(ends):
        final += [(ending[n][d - 1], ("last", "lo", k, back(d))) for d in far]
    last_items = [(last_outs[n][0], ("last", "lo", k, 0)) for n, k in enumerate(ends)]
    for i, (k, role, send_role, there, home) in enumerate(rounds):
        items = [(outs[i][0], ("slot", role, k, 0))]
        items += [(backs[i][d - 1], ("slot", role, k, back(d))) for d in far]
        items.append((homes[i], ("swap", send_role, k, 0)))
        if i == 0:
            items = last_items + items
        twins = group(items)
        for d in far:
            final.append((home(backs[i][d - 1]), ("swap", send_role, k, back(d))))
    total, copied = early(kinds, layout, tables + twin_tables, terms, cols_total)
    values = []
    for value, spot in final:
        values += [value, rotate(after(value, total), "batch", 1)]
        final_kinds += [(0, spot), (1, spot)]
    return late(final_kinds, layout, tables + twin_tables, total, copied, values)


def solution(mesh):
    in_specs = (
        P(("groups", "slab"), "tile", None),
        P(("groups", "slab"), "tile", None),
        P(),
        P(("groups", "tile", "batch"), None, None),
        P(("groups", "tile", "batch"), None),
    )
    out_specs = P(None, ("groups", "slab"), "tile", None)
    return jax.shard_map(local, mesh=mesh, in_specs=in_specs, out_specs=out_specs, check_vma=False)
```

```python
import math

import numpy as np
import jax
import jax.numpy as jnp
from jax import lax
from jax.experimental import pallas as pl
from jax.experimental.pallas import tpu as pltpu
from jax.sharding import PartitionSpec as P

SIN = [(-1.0) ** k / math.factorial(2 * k + 1) for k in range(8)]
COS = [(-1.0) ** k / math.factorial(2 * k) for k in range(8)]
VMEM = pl.BlockSpec(memory_space=pltpu.VMEM)
SMEM = pl.BlockSpec(memory_space=pltpu.SMEM)
HBM = pl.BlockSpec(memory_space=pltpu.HBM)


def params(mib):
    return pltpu.CompilerParams(vmem_limit_bytes=mib << 20)


def cost(microseconds):
    return pl.CostEstimate(flops=int(microseconds * 1e9), transcendentals=0, bytes_accessed=0)


def after(value, *others):
    return lax.optimization_barrier((value, *others))[0]


def move(block, axis, distance):
    size = lax.axis_size(axis)
    route = [(i, i + distance) for i in range(size) if 0 <= i + distance < size]
    return lax.ppermute(block, axis, route)


def rotate(block, axis, distance):
    size = lax.axis_size(axis)
    return lax.ppermute(block, axis, [(i, (i + distance) % size) for i in range(size)])


def swap(block, axis, phase):
    size = lax.axis_size(axis)
    route = []
    for lower in range(phase, size - 1, 2):
        route += [(lower, lower + 1), (lower + 1, lower)]
    return lax.ppermute(block, axis, route)


def rotate_last(block, distance):
    tiles, size = lax.axis_size("tile"), lax.axis_size("slab")
    base = (tiles - 1) * size
    route = [(base + i, base + (i + distance) % size) for i in range(size)]
    return lax.ppermute(block, ("tile", "slab"), route)


def halves(matrix):
    high = matrix.astype(np.float32).astype(jnp.bfloat16)
    low = (matrix - high.astype(np.float64)).astype(np.float32).astype(jnp.bfloat16)
    return [high, low]


def compact_tables(side):
    index = np.arange(side)
    fourier = np.exp(-2j * np.pi * (index[:, None] * index[None, :] % side) / side)
    wavenumber = np.where(index < side // 2, index, index - side)
    kernel = np.exp(-1j * np.pi * (wavenumber * wavenumber % (8 * side)) / (4 * side))
    line = np.fft.ifft(kernel)
    line = (line + line[-index % side]) / 2
    fresnel = line[(index[:, None] - index[None, :]) % side]
    scaled = fourier / math.sqrt(side)
    pieces = []
    for matrix in (fresnel, scaled):
        pieces += halves(matrix.real) + halves(matrix.imag)
    return np.stack(pieces)


def expand_kernel(pieces, *outs):
    side = pieces.shape[-1]
    for which in range(2):
        left, right = outs[2 * which], outs[2 * which + 1]
        real_high, real_low, imag_high, imag_low = [pieces[4 * which + k] for k in range(4)]
        real = [real_high, real_low, real_high]
        imag = [imag_high, imag_low, imag_high]
        minus = [-imag_high, -imag_low, -imag_high]
        for column, blocks in enumerate((real + minus, imag + real)):
            for row, block in enumerate(blocks):
                rows, cols = pl.ds(row * side, side), pl.ds(column * side, side)
                right[rows, cols] = block
                left[cols, rows] = block


def expand(side):
    pieces = jnp.asarray(compact_tables(side))
    left = jax.ShapeDtypeStruct((2 * side, 6 * side), jnp.bfloat16)
    right = jax.ShapeDtypeStruct((6 * side, 2 * side), jnp.bfloat16)
    return pl.pallas_call(
        expand_kernel,
        in_specs=[VMEM],
        out_specs=[VMEM] * 4,
        out_shape=[left, right, left, right],
        compiler_params=params(16),
        name="expand",
    )(pieces)


def split(value):
    high = value.astype(jnp.bfloat16)
    low = (value - high.astype(jnp.float32)).astype(jnp.bfloat16)
    return high, low


def two_sided(left, right, real, imag):
    side = real.shape[-1]
    real_high, real_low = split(real)
    imag_high, imag_low = split(imag)
    wide = jnp.concatenate([real_high, real_high, real_low, imag_high, imag_high, imag_low], axis=1)
    inner = jnp.dot(wide, right[...], preferred_element_type=jnp.float32)
    real_high, real_low = split(inner[:, :side])
    imag_high, imag_low = split(inner[:, side:])
    tall = jnp.concatenate([real_high, real_high, real_low, imag_high, imag_high, imag_low], axis=0)
    outer = jnp.dot(left[...], tall, preferred_element_type=jnp.float32)
    return outer[:side], outer[side:]


def transmission(phase, absorption):
    square = phase * phase
    sine = jnp.full_like(phase, SIN[-1])
    cosine = jnp.full_like(phase, COS[-1])
    for a, b in zip(SIN[-2::-1], COS[-2::-1]):
        sine = sine * square + a
        cosine = cosine * square + b
    damping = jnp.exp(-absorption)
    return damping * cosine, damping * sine * phase


def is_lower(phase):
    if isinstance(phase, str):
        return phase == "lo"
    return lax.rem(lax.axis_index("tile"), 2) == phase


def pick(lower, first, second):
    if isinstance(lower, bool):
        return first if lower else second
    return jnp.where(lower, first, second)


def locate(spot, layout, tables, twin=0):
    which, phase, k, distance = spot
    sections, n_here, n_up, side = layout
    owner = lax.rem(lax.axis_index("slab") + distance, sections)
    here, up = owner * n_here + k, sections * n_here + owner * n_up + k
    width = len(tables) // 2 if len(tables) > 3 else len(tables)
    pairs = tables[width * twin]
    if which == "last":
        below = pairs
    else:
        below = tables[width * twin + 1 + (0 if isinstance(phase, str) else phase)]
    lower = True if which == "last" else is_lower(phase)
    own, other = (here, up) if which == "slot" else (up, here)
    row = lax.rem(pick(lower, pairs[0, own], below[0, other]), side)
    col = pick(lower, pairs[1, own], below[1, other])
    low, high = pick(lower, row, jnp.int32(0)), pick(lower, jnp.int32(side), row)
    last = lax.axis_index("tile") == lax.axis_size("tile") - 1
    if which == "last":
        low = jnp.where(last, low, side)
    elif which == "swap":
        low = jnp.where(last & lower, side, low)
    return pick(lower, own, other), row, col, low, high


def slot_kernel(kind, *args):
    if kind == "last":

        @pl.when(lax.axis_index("tile") == lax.axis_size("tile") - 1)
        def _():
            slot_body(*args)
    else:
        slot_body(*args)


def slot_body(spot, layout, n_tables, *refs):
    tables, (probe, measured), refs = refs[:n_tables], refs[n_tables : n_tables + 2], refs[n_tables + 2 :]
    sections = layout[0]
    which, phase = spot[:2]
    pieces = 1 if which == "last" else 2
    own = refs[:pieces]
    others = refs[pieces : pieces + sections - 1]
    refs = refs[pieces + sections - 1 :]
    prop_left, prop_right, dft_left, dft_right = refs[:4]
    outs = refs[4 : 4 + sections]
    wave, trans, amplitude, sem = refs[4 + sections :]
    side = probe.shape[-1]
    slab = lax.axis_index("slab")
    index, row, col, low, high = locate(spot, layout, tables)
    col = lax.rem(col, side)
    lower = True if which == "last" else is_lower(phase)

    def fetch():
        return pltpu.make_async_copy(measured.at[index], amplitude, sem)

    if lower is True:
        fetch().start()
    elif lower is False:
        amplitude[...] = own[1][2]
    else:

        @pl.when(lower)
        def _():
            fetch().start()

        @pl.when(jnp.logical_not(lower))
        def _():
            amplitude[...] = own[1][2]

    rows = lax.broadcasted_iota(jnp.int32, (side, side), 0)
    patch = [own[0][0], own[0][1]]
    if pieces == 2:
        local_rows = (rows >= low) & (rows < high)
        patch = [jnp.where(local_rows, own[0][k], own[1][k]) for k in range(2)]
    trans[slab, 0], trans[slab, 1] = transmission(patch[0], patch[1])
    for distance in range(1, sections):
        owner = lax.rem(slab + (sections - distance), sections)
        real, imag = transmission(others[distance - 1][0], others[distance - 1][1])
        trans[owner, 0] = real
        trans[owner, 1] = imag
    for part in range(2):
        wave[0, part] = pltpu.roll(pltpu.roll(probe[part], row, 0), col, 1)
    for step in range(sections):
        a, b, c, d = wave[step, 0], wave[step, 1], trans[step, 0], trans[step, 1]
        real, imag = a * c - b * d, a * d + b * c
        if step < sections - 1:
            real, imag = two_sided(prop_left, prop_right, real, imag)
            wave[step + 1, 0] = real
            wave[step + 1, 1] = imag
    real, imag = two_sided(dft_left, dft_right, real, imag)
    if lower is True:
        fetch().wait()
    elif lower is not False:

        @pl.when(lower)
        def _():
            fetch().wait()

    factor = 1.0 - amplitude[...] * lax.rsqrt(jnp.maximum(real * real + imag * imag, 0.25))
    real, minus = two_sided(dft_left, dft_right, real * factor, -imag * factor)
    for step in range(sections - 1, -1, -1):
        a, b = wave[step, 0], wave[step, 1]
        wave[step, 0] = a * real - b * minus
        wave[step, 1] = -(a * minus + b * real)
        if step > 0:
            c, d = trans[step, 0], trans[step, 1]
            real, minus = c * real - d * minus, c * minus + d * real
            real, minus = two_sided(prop_left, prop_right, real, minus)
    for distance in range(sections):
        outs[distance][...] = wave[lax.rem(slab + distance, sections)]


def run_slot(kind, spot, layout, tables, probe, measured, own, others, constants):
    sections, side = layout[0], layout[3]
    shape = jax.ShapeDtypeStruct((2, side, side), jnp.float32)
    return pl.pallas_call(
        lambda *refs: slot_kernel(kind, spot, layout, len(tables), *refs),
        in_specs=[SMEM] * len(tables) + [VMEM, HBM] + [VMEM] * (len(own) + len(others) + 4),
        out_specs=[VMEM] * sections,
        out_shape=[shape] * sections,
        scratch_shapes=[pltpu.VMEM((sections, 2, side, side), jnp.float32)] * 2
        + [pltpu.VMEM((side, side), jnp.float32), pltpu.SemaphoreType.DMA(())],
        compiler_params=params(32),
        name="slot_" + kind,
    )(*tables, probe, measured, *own, *others, *constants)


def cut_kernel(spots, layout, with_measured, n_tables, *refs):
    tables, (phase, absorption) = refs[:n_tables], refs[n_tables : n_tables + 2]
    refs = refs[n_tables + 2 :]
    count, side = len(spots), layout[3]
    blocks = phase.shape[2] // side
    extra = None
    if with_measured:
        sections, n_here, n_up, side = layout
        index = sections * n_here + lax.axis_index("slab") * n_up + spots[0][2]
        extra = pltpu.make_async_copy(refs[0].at[index], refs[1].at[2], refs[-3])
        refs = refs[1:]
    outs = refs[:count]
    buffer, sems = refs[-2], refs[-1]
    copies, columns = [], []
    for k in range(count):
        column = locate(spots[k], layout, tables)[2]
        first = lax.div(column, side)
        columns.append(lax.rem(column, side))
        for which, source in enumerate((phase, absorption)):
            for half in range(2):
                block = first if half == 0 else jnp.minimum(first + 1, blocks - 1)
                copies.append(
                    pltpu.make_async_copy(
                        source.at[0, :, pl.ds(pl.multiple_of(block * side, side), side)],
                        buffer.at[k, which, half],
                        sems.at[k, which, half],
                    )
                )
    for copy in copies:
        copy.start()
    if extra is not None:
        extra.start()
    lane = lax.broadcasted_iota(jnp.int32, (side, side), 1)
    for k in range(count):
        own = lane >= columns[k]
        for which in range(2):
            for half in range(2):
                copies[4 * k + 2 * which + half].wait()
            outs[k][which] = jnp.where(own, buffer[k, which, 0], buffer[k, which, 1])
    if extra is not None:
        extra.wait()


def cut(spots, layout, tables, phase, absorption, measured=None):
    side = layout[3]
    count = len(spots)
    shapes = [jax.ShapeDtypeStruct((2, side, side), jnp.float32)] * count
    scratch = [
        pltpu.VMEM((count, 2, 2, side, side), jnp.float32),
        pltpu.SemaphoreType.DMA((count, 2, 2)),
    ]
    inputs = [phase, absorption]
    if measured is not None:
        shapes = [jax.ShapeDtypeStruct((3, side, side), jnp.float32)] + shapes[1:]
        scratch = [pltpu.SemaphoreType.DMA(())] + scratch
        inputs.append(measured)
    return pl.pallas_call(
        lambda *refs: cut_kernel(spots, layout, measured is not None, len(tables), *refs),
        in_specs=[SMEM] * len(tables) + [HBM] * len(inputs),
        out_specs=[VMEM] * count,
        out_shape=shapes,
        scratch_shapes=scratch,
        compiler_params=params(16),
        name="cut",
    )(*tables, *inputs)


def join_kernel(spot, layout, *refs):
    tables, (here, there, out) = refs[:-3], refs[-3:]
    side = layout[3]
    low, high = locate(spot, layout, tables)[3:]
    rows = lax.broadcasted_iota(jnp.int32, (side, side), 0)
    keep = (rows >= low) & (rows < high)
    for part in range(2):
        out[part] = jnp.where(keep, here[part], there[part])


def join(spot, layout, tables, here, there):
    return pl.pallas_call(
        lambda *refs: join_kernel(spot, layout, *refs),
        in_specs=[SMEM] * len(tables) + [VMEM, VMEM],
        out_specs=VMEM,
        out_shape=jax.ShapeDtypeStruct(here.shape, jnp.float32),
        compiler_params=params(8),
        name="join",
    )(*tables, here, there)


def pack_kernel(*refs):
    out = refs[-1]
    for k, term in enumerate(refs[:-1]):
        out[k] = term[...]


def pack(terms):
    if len(terms) == 1:
        return terms[0][None]
    return pl.pallas_call(
        pack_kernel,
        in_specs=[VMEM] * len(terms),
        out_specs=VMEM,
        out_shape=jax.ShapeDtypeStruct((len(terms), *terms[0].shape), jnp.float32),
        compiler_params=params(8),
        name="pack",
    )(*terms)


def spread(metas, terms):
    views, kinds = [], []
    for kind, term in zip(metas, terms):
        if isinstance(kind, list):
            views += [term.at[i] for i in range(len(kind))]
            kinds += kind
        else:
            views.append(term)
            kinds.append(kind)
    return views, kinds


def spans(metas, tables, layout):
    side = layout[3]
    out = []
    for twin, spot in metas:
        index, row, col, low, high = locate(spot, layout, tables, twin)
        out.append((lax.div(col, side), lax.rem(col, side), low, high))
    return out


def early_kernel(metas, layout, *refs):
    out, copied, sem = refs[-3:]
    width = len(refs) - 3 - len(metas)
    tables, terms = refs[:width], refs[width:-3]
    terms, metas = spread(metas, terms)
    side = terms[0].shape[-1]
    blocks = out.shape[-1] // side
    rows = lax.broadcasted_iota(jnp.int32, (side, side), 0)
    lane = lax.broadcasted_iota(jnp.int32, (side, side), 1)

    @pl.loop(0, blocks)
    def _(block):
        out[:, :, pl.ds(pl.multiple_of(block * side, side), side)] = jnp.zeros((2, side, side), jnp.float32)

    for k, (first, col, low, high) in enumerate(spans(metas, tables, layout)):
        for half in range(2):
            block = first + half

            @pl.when((block < blocks) & (high > low))
            def _():
                keep = (rows >= low) & (rows < high)
                keep = keep & ((lane < col) if half else (lane >= col))
                place = pl.ds(pl.multiple_of(block * side, side), side)
                for part in range(2):
                    out[part, :, place] += jnp.where(keep, terms[k][part], 0.0)

    copy = pltpu.make_async_copy(out, copied.at[:, 0], sem)
    copy.start()
    copy.wait()


def early(metas, layout, tables, terms, cols_total):
    side = layout[3]
    return pl.pallas_call(
        lambda *refs: early_kernel(metas, layout, *refs),
        in_specs=[SMEM] * len(tables) + [VMEM] * len(terms),
        out_specs=[VMEM, HBM],
        out_shape=[
            jax.ShapeDtypeStruct((2, side, cols_total), jnp.float32),
            jax.ShapeDtypeStruct((2, 1, side, cols_total), jnp.float32),
        ],
        scratch_shapes=[pltpu.SemaphoreType.DMA(())],
        compiler_params=params(20),
        name="early",
    )(*tables, *terms)


def late_kernel(metas, layout, *refs):
    width = len(refs) - 5 - len(metas)
    tables, total, terms = refs[:width], refs[width], refs[width + 1 : -4]
    out, stage, sems = refs[-3:]
    side = terms[0].shape[-1]
    blocks = out.shape[-1] // side
    rows = lax.broadcasted_iota(jnp.int32, (side, side), 0)
    lane = lax.broadcasted_iota(jnp.int32, (side, side), 1)
    ranges = spans(metas, tables, layout)

    def place(block):
        return pl.ds(pl.multiple_of(block * side, side), side)

    def send(block):
        where = place(block)
        return pltpu.make_async_copy(stage.at[:, :, where], out.at[:, 0, :, where], sems.at[block])

    def touched(block):
        hit = jnp.bool_(False)
        for first, col, low, high in ranges:
            hit = hit | (((block == first) | (block == first + 1)) & (high > low))
        return hit

    @pl.loop(0, blocks)
    def _(block):
        @pl.when(touched(block))
        def _():
            where = place(block)
            stage[:, :, where] = total[:, :, where]
            for k, (first, col, low, high) in enumerate(ranges):
                for half in range(2):

                    @pl.when((first + half == block) & (high > low))
                    def _():
                        keep = (rows >= low) & (rows < high)
                        keep = keep & ((lane < col) if half else (lane >= col))
                        for part in range(2):
                            stage[part, :, where] += jnp.where(keep, terms[k][part], 0.0)

            send(block).start()

    @pl.loop(0, blocks)
    def _(block):
        @pl.when(touched(block))
        def _():
            send(block).wait()


def late(metas, layout, tables, total, copied, terms):
    side = layout[3]
    cols_total = total.shape[-1]
    return pl.pallas_call(
        lambda *refs: late_kernel(metas, layout, *refs),
        in_specs=[SMEM] * len(tables) + [VMEM] * (1 + len(terms)) + [HBM],
        out_specs=HBM,
        input_output_aliases={len(tables) + 1 + len(terms): 0},
        out_shape=jax.ShapeDtypeStruct((2, 1, side, cols_total), jnp.float32),
        scratch_shapes=[
            pltpu.VMEM((2, side, cols_total), jnp.float32),
            pltpu.SemaphoreType.DMA((cols_total // side,)),
        ],
        compiler_params=params(28),
        name="late",
    )(*tables, total, *terms, copied)


def local(phase, absorption, probe, measured, offsets):
    side = probe.shape[-1]
    cols_total = phase.shape[2]
    sections = lax.axis_size("slab")
    each = offsets.shape[0] // sections
    n_up = each // 2
    n_here = each - n_up
    distances = list(range(sections))

    layout = (sections, n_here, n_up, side)
    pairs = offsets.T
    if n_here == n_up:
        tables = [pairs] + [swap(pairs, "tile", parity) for parity in range(2)]
    else:
        tables = [pairs, move(pairs, "tile", 1)]
    back = lambda d: (sections - d) % sections
    far = distances[1:]
    phase = pltpu.with_memory_space_constraint(phase, pltpu.HBM)
    absorption = pltpu.with_memory_space_constraint(absorption, pltpu.HBM)
    measured = pltpu.with_memory_space_constraint(measured, pltpu.HBM)

    rounds, last_round = [], {}
    for k in range(n_here):
        if n_here == n_up:
            last_round[k] = 2 * k + (lax.axis_size("tile") - 1) % 2
            for parity in range(2):
                there = lambda value, parity=parity: swap(value, "tile", parity)
                rounds.append((k, parity, parity, there, there))
        else:
            rise = lambda value: move(value, "tile", 1)
            fall = lambda value: move(value, "tile", -1)
            if k < n_up:
                last_round[k] = len(rounds)
                rounds.append((k, "hi", "lo", rise, fall))
            rounds.append((k, "lo", "hi", fall, rise))
    count = len(rounds)
    done = [pairs]

    def step(kernel):
        out = kernel([after(pairs, *done)] + tables[1:])
        done[:] = [out[0] if isinstance(out, (list, tuple)) else out]
        return out

    ends = sorted(last_round)
    spots = [("last", "lo", k, d) for k in ends for d in far]
    pieces = step(lambda p: cut(spots, layout, p[:1], phase, absorption)) if spots else []
    extra = []
    for n in range(len(ends)):
        row = pieces[n * len(far) : (n + 1) * len(far)]
        extra.append([rotate_last(piece, d) for piece, d in zip(row, far)])
    spots = [("send", rounds[i][2], rounds[i][0], d) for i in range(count) for d in far]
    pieces = step(lambda p: cut(spots, layout, p, phase, absorption)) if spots else []
    got = []
    for i, (k, role, send_role, there, home) in enumerate(rounds):
        row = pieces[i * len(far) : (i + 1) * len(far)]
        got.append([None] + [there(piece) for piece in row])
    done += [value for row in extra for value in row]
    held = []
    for k, role, send_role, there, home in rounds:
        spots = [("slot", role, k, d) for d in distances]
        held.append(step(lambda p: cut(spots, layout, p, phase, absorption)))
    for i, (k, role, send_role, there, home) in enumerate(rounds):
        extra_input = [] if role == "lo" else [measured]
        spots = [("send", send_role, k, 0)]
        piece = step(lambda p: cut(spots, layout, p, phase, absorption, *extra_input))[0]
        got[i][0] = there(piece)
    own_cut = [
        step(lambda p: cut([("last", "lo", k, 0)], layout, p[:1], phase, absorption)) for k in ends
    ]
    constants = expand(side)
    others = []
    for i, (k, role, send_role, there, home) in enumerate(rounds):
        joined = []
        for d in far:
            spot = ("slot", role, k, d)
            joined.append(step(lambda p: join(spot, layout, p, held[i][d], got[i][d])))
        others.append([rotate(joined[d - 1], "slab", d) for d in far])

    twin_tables = [rotate(table, "batch", 1) for table in tables]
    done += twin_tables

    def slot(kind, spot, own, rest):
        return step(
            lambda p: run_slot(kind, spot, layout, p, probe, measured, own, rest, constants)
        )

    outs, backs, homes = [], [], []
    for i, (k, role, send_role, there, home) in enumerate(rounds):
        outs.append(slot(f"{i}", ("slot", role, k, 0), [held[i][0], got[i][0]], others[i]))
        backs.append([rotate(outs[i][d], "slab", d) for d in far])
        homes.append(home)
    last_outs = [
        slot("last", ("last", "lo", k, 0), [own_cut[n][0]], extra[n])
        for n, k in enumerate(ends)
    ]
    for i in range(count):
        gates = backs[0] if i and i == count - 1 else []
        homes[i] = homes[i](after(outs[i][0], *gates))
    terms, kinds = [], []

    def group(items):
        values = [value for value, spot in items]
        twins = rotate(pack(values), "batch", 1)
        terms.extend(values + [twins])
        kinds.extend([(0, spot) for value, spot in items] + [[(1, spot) for value, spot in items]])
        return twins

    final, final_kinds = [], []
    ending = [
        [rotate_last(after(last_outs[n][d], *backs[-1]), d) for d in far] for n in range(len(ends))
    ]
    for n, k in enumerate(ends):
        final += [(ending[n][d - 1], ("last", "lo", k, back(d))) for d in far]
    last_items = [(last_outs[n][0], ("last", "lo", k, 0)) for n, k in enumerate(ends)]
    for i, (k, role, send_role, there, home) in enumerate(rounds):
        items = [(outs[i][0], ("slot", role, k, 0))]
        items += [(backs[i][d - 1], ("slot", role, k, back(d))) for d in far]
        items.append((homes[i], ("swap", send_role, k, 0)))
        if i == 0:
            items = last_items + items
        twins = group(items)
        for d in far:
            final.append((home(backs[i][d - 1]), ("swap", send_role, k, back(d))))
    total, copied = early(kinds, layout, tables + twin_tables, terms, cols_total)
    values = []
    for value, spot in final:
        values += [value, rotate(after(value, total), "batch", 1)]
        final_kinds += [(0, spot), (1, spot)]
    return late(final_kinds, layout, tables + twin_tables, total, copied, values)


def solution(mesh):
    in_specs = (
        P(("groups", "slab"), "tile", None),
        P(("groups", "slab"), "tile", None),
        P(),
        P(("groups", "tile", "batch"), None, None),
        P(("groups", "tile", "batch"), None),
    )
    out_specs = P(None, ("groups", "slab"), "tile", None)
    return jax.shard_map(local, mesh=mesh, in_specs=in_specs, out_specs=out_specs, check_vma=False)
```

```python
import math

import numpy as np
import jax
import jax.numpy as jnp
from jax import lax
from jax.experimental import pallas as pl
from jax.experimental.pallas import tpu as pltpu
from jax.sharding import PartitionSpec as P

SIN = [(-1.0) ** k / math.factorial(2 * k + 1) for k in range(8)]
COS = [(-1.0) ** k / math.factorial(2 * k) for k in range(8)]
VMEM = pl.BlockSpec(memory_space=pltpu.VMEM)
SMEM = pl.BlockSpec(memory_space=pltpu.SMEM)
HBM = pl.BlockSpec(memory_space=pltpu.HBM)


def params(mib):
    return pltpu.CompilerParams(vmem_limit_bytes=mib << 20)


def cost(microseconds):
    return pl.CostEstimate(flops=int(microseconds * 1e9), transcendentals=0, bytes_accessed=0)


def after(value, *others):
    return lax.optimization_barrier((value, *others))[0]


def move(block, axis, distance):
    size = lax.axis_size(axis)
    route = [(i, i + distance) for i in range(size) if 0 <= i + distance < size]
    return lax.ppermute(block, axis, route)


def rotate(block, axis, distance):
    size = lax.axis_size(axis)
    return lax.ppermute(block, axis, [(i, (i + distance) % size) for i in range(size)])


def swap(block, axis, phase):
    size = lax.axis_size(axis)
    route = []
    for lower in range(phase, size - 1, 2):
        route += [(lower, lower + 1), (lower + 1, lower)]
    return lax.ppermute(block, axis, route)


def rotate_last(block, distance):
    tiles, size = lax.axis_size("tile"), lax.axis_size("slab")
    base = (tiles - 1) * size
    route = [(base + i, base + (i + distance) % size) for i in range(size)]
    return lax.ppermute(block, ("tile", "slab"), route)


def halves(matrix):
    high = matrix.astype(np.float32).astype(jnp.bfloat16)
    low = (matrix - high.astype(np.float64)).astype(np.float32).astype(jnp.bfloat16)
    return [high, low]


def compact_tables(side):
    index = np.arange(side)
    fourier = np.exp(-2j * np.pi * (index[:, None] * index[None, :] % side) / side)
    wavenumber = np.where(index < side // 2, index, index - side)
    kernel = np.exp(-1j * np.pi * (wavenumber * wavenumber % (8 * side)) / (4 * side))
    line = np.fft.ifft(kernel)
    line = (line + line[-index % side]) / 2
    fresnel = line[(index[:, None] - index[None, :]) % side]
    scaled = fourier / math.sqrt(side)
    pieces = []
    for matrix in (fresnel, scaled):
        pieces += halves(matrix.real) + halves(matrix.imag)
    return np.stack(pieces)


def expand_kernel(pieces, *outs):
    side = pieces.shape[-1]
    for which in range(2):
        real_high, real_low, imag_high, imag_low = [pieces[4 * which + k] for k in range(4)]
        real = [real_high, real_low, real_high]
        imag = [imag_high, imag_low, imag_high]
        minus = [-imag_high, -imag_low, -imag_high]
        for column, blocks in enumerate((real + minus, imag + real)):
            for row, block in enumerate(blocks):
                outs[which][pl.ds(row * side, side), pl.ds(column * side, side)] = block


def expand(side):
    pieces = jnp.asarray(compact_tables(side))
    return pl.pallas_call(
        expand_kernel,
        in_specs=[VMEM],
        out_specs=[VMEM] * 2,
        out_shape=[jax.ShapeDtypeStruct((6 * side, 2 * side), jnp.bfloat16)] * 2,
        compiler_params=params(16),
        name="expand",
    )(pieces)


def split(value):
    high = value.astype(jnp.bfloat16)
    low = (value - high.astype(jnp.float32)).astype(jnp.bfloat16)
    return high, low


def right_product(table, real, imag):
    side = real.shape[-1]
    real_high, real_low = split(real)
    imag_high, imag_low = split(imag)
    wide = jnp.concatenate([real_high, real_high, real_low, imag_high, imag_high, imag_low], axis=1)
    out = jnp.dot(wide, table[...], preferred_element_type=jnp.float32)
    return out[:, :side], out[:, side:]


def two_sided_transposed(table, real, imag):
    real, imag = right_product(table, real, imag)
    return right_product(table, real.T, imag.T)


def two_sided(table, real, imag):
    real, imag = two_sided_transposed(table, real, imag)
    return real.T, imag.T


def transmission(phase, absorption):
    square = phase * phase
    sine = jnp.full_like(phase, SIN[-1])
    cosine = jnp.full_like(phase, COS[-1])
    for a, b in zip(SIN[-2::-1], COS[-2::-1]):
        sine = sine * square + a
        cosine = cosine * square + b
    damping = jnp.exp(-absorption)
    return damping * cosine, damping * sine * phase


def is_lower(phase):
    if isinstance(phase, str):
        return phase == "lo"
    return lax.rem(lax.axis_index("tile"), 2) == phase


def pick(lower, first, second):
    if isinstance(lower, bool):
        return first if lower else second
    return jnp.where(lower, first, second)


def locate(spot, layout, tables, twin=0):
    which, phase, k, distance = spot
    sections, n_here, n_up, side = layout
    owner = lax.rem(lax.axis_index("slab") + distance, sections)
    here, up = owner * n_here + k, sections * n_here + owner * n_up + k
    width = len(tables) // 2 if len(tables) > 3 else len(tables)
    pairs = tables[width * twin]
    below = tables[width * twin + 1 + (0 if isinstance(phase, str) else phase)]
    lower = True if which == "last" else is_lower(phase)
    own, other = (here, up) if which == "slot" else (up, here)
    row = lax.rem(pick(lower, pairs[0, own], below[0, other]), side)
    col = pick(lower, pairs[1, own], below[1, other])
    low, high = pick(lower, row, jnp.int32(0)), pick(lower, jnp.int32(side), row)
    last = lax.axis_index("tile") == lax.axis_size("tile") - 1
    if which == "last":
        low = jnp.where(last, low, side)
    elif which == "swap":
        low = jnp.where(last & lower, side, low)
    return pick(lower, own, other), row, col, low, high


def slot_kernel(kind, *args):
    if kind == "last":

        @pl.when(lax.axis_index("tile") == lax.axis_size("tile") - 1)
        def _():
            slot_body(*args)
    else:
        slot_body(*args)


def slot_body(spot, layout, n_tables, *refs):
    tables, (probe, measured), refs = refs[:n_tables], refs[n_tables : n_tables + 2], refs[n_tables + 2 :]
    sections = layout[0]
    which, phase = spot[:2]
    pieces = 1 if which == "last" else 2
    own = refs[:pieces]
    others = refs[pieces : pieces + sections - 1]
    refs = refs[pieces + sections - 1 :]
    prop, dft = refs[:2]
    outs = refs[2 : 2 + sections]
    wave, trans, amplitude, sem = refs[2 + sections :]
    side = probe.shape[-1]
    slab = lax.axis_index("slab")
    index, row, col, low, high = locate(spot, layout, tables)
    col = lax.rem(col, side)
    lower = True if which == "last" else is_lower(phase)

    def fetch():
        return pltpu.make_async_copy(measured.at[index], amplitude, sem)

    if lower is True:
        fetch().start()
    elif lower is False:
        amplitude[...] = own[1][2]
    else:

        @pl.when(lower)
        def _():
            fetch().start()

        @pl.when(jnp.logical_not(lower))
        def _():
            amplitude[...] = own[1][2]

    rows = lax.broadcasted_iota(jnp.int32, (side, side), 0)
    patch = [own[0][0], own[0][1]]
    if pieces == 2:
        local_rows = (rows >= low) & (rows < high)
        patch = [jnp.where(local_rows, own[0][k], own[1][k]) for k in range(2)]
    trans[slab, 0], trans[slab, 1] = transmission(patch[0], patch[1])
    for distance in range(1, sections):
        owner = lax.rem(slab + (sections - distance), sections)
        real, imag = transmission(others[distance - 1][0], others[distance - 1][1])
        trans[owner, 0] = real
        trans[owner, 1] = imag
    for part in range(2):
        wave[0, part] = pltpu.roll(pltpu.roll(probe[part], row, 0), col, 1)
    for step in range(sections):
        a, b, c, d = wave[step, 0], wave[step, 1], trans[step, 0], trans[step, 1]
        real, imag = a * c - b * d, a * d + b * c
        if step < sections - 1:
            real, imag = two_sided(prop, real, imag)
            wave[step + 1, 0] = real
            wave[step + 1, 1] = imag
    real, imag = two_sided_transposed(dft, real, imag)
    if lower is True:
        fetch().wait()
    elif lower is not False:

        @pl.when(lower)
        def _():
            fetch().wait()

    factor = 1.0 - amplitude[...].T * lax.rsqrt(jnp.maximum(real * real + imag * imag, 0.25))
    real, minus = two_sided_transposed(dft, real * factor, -imag * factor)
    for step in range(sections - 1, -1, -1):
        a, b = wave[step, 0], wave[step, 1]
        wave[step, 0] = a * real - b * minus
        wave[step, 1] = -(a * minus + b * real)
        if step > 0:
            c, d = trans[step, 0], trans[step, 1]
            real, minus = c * real - d * minus, c * minus + d * real
            real, minus = two_sided(prop, real, minus)
    for distance in range(sections):
        outs[distance][...] = wave[lax.rem(slab + distance, sections)]


def run_slot(kind, spot, layout, tables, probe, measured, own, others, constants):
    sections, side = layout[0], layout[3]
    shape = jax.ShapeDtypeStruct((2, side, side), jnp.float32)
    return pl.pallas_call(
        lambda *refs: slot_kernel(kind, spot, layout, len(tables), *refs),
        in_specs=[SMEM] * len(tables) + [VMEM, HBM] + [VMEM] * (len(own) + len(others) + 2),
        out_specs=[VMEM] * sections,
        out_shape=[shape] * sections,
        scratch_shapes=[pltpu.VMEM((sections, 2, side, side), jnp.float32)] * 2
        + [pltpu.VMEM((side, side), jnp.float32), pltpu.SemaphoreType.DMA(())],
        compiler_params=params(32),
        name="slot_" + kind,
    )(*tables, probe, measured, *own, *others, *constants)


def cut_kernel(spots, layout, with_measured, n_tables, *refs):
    tables, (phase, absorption) = refs[:n_tables], refs[n_tables : n_tables + 2]
    refs = refs[n_tables + 2 :]
    count, side = len(spots), layout[3]
    blocks = phase.shape[2] // side
    extra = None
    if with_measured:
        sections, n_here, n_up, side = layout
        index = sections * n_here + lax.axis_index("slab") * n_up + spots[0][2]
        extra = pltpu.make_async_copy(refs[0].at[index], refs[1].at[2], refs[-3])
        refs = refs[1:]
    outs = refs[:count]
    buffer, sems = refs[-2], refs[-1]
    copies, columns = [], []
    for k in range(count):
        column = locate(spots[k], layout, tables)[2]
        first = lax.div(column, side)
        columns.append(lax.rem(column, side))
        for which, source in enumerate((phase, absorption)):
            for half in range(2):
                block = first if half == 0 else jnp.minimum(first + 1, blocks - 1)
                copies.append(
                    pltpu.make_async_copy(
                        source.at[0, :, pl.ds(pl.multiple_of(block * side, side), side)],
                        buffer.at[k, which, half],
                        sems.at[k, which, half],
                    )
                )
    for copy in copies:
        copy.start()
    if extra is not None:
        extra.start()
    lane = lax.broadcasted_iota(jnp.int32, (side, side), 1)
    for k in range(count):
        own = lane >= columns[k]
        for which in range(2):
            for half in range(2):
                copies[4 * k + 2 * which + half].wait()
            outs[k][which] = jnp.where(own, buffer[k, which, 0], buffer[k, which, 1])
    if extra is not None:
        extra.wait()


def cut(spots, layout, tables, phase, absorption, measured=None):
    side = layout[3]
    count = len(spots)
    shapes = [jax.ShapeDtypeStruct((2, side, side), jnp.float32)] * count
    scratch = [
        pltpu.VMEM((count, 2, 2, side, side), jnp.float32),
        pltpu.SemaphoreType.DMA((count, 2, 2)),
    ]
    inputs = [phase, absorption]
    if measured is not None:
        shapes = [jax.ShapeDtypeStruct((3, side, side), jnp.float32)] + shapes[1:]
        scratch = [pltpu.SemaphoreType.DMA(())] + scratch
        inputs.append(measured)
    return pl.pallas_call(
        lambda *refs: cut_kernel(spots, layout, measured is not None, len(tables), *refs),
        in_specs=[SMEM] * len(tables) + [HBM] * len(inputs),
        out_specs=[VMEM] * count,
        out_shape=shapes,
        scratch_shapes=scratch,
        compiler_params=params(16),
        name="cut",
    )(*tables, *inputs)


def join_kernel(spot, layout, *refs):
    tables, (here, there, out) = refs[:-3], refs[-3:]
    side = layout[3]
    low, high = locate(spot, layout, tables)[3:]
    rows = lax.broadcasted_iota(jnp.int32, (side, side), 0)
    keep = (rows >= low) & (rows < high)
    for part in range(2):
        out[part] = jnp.where(keep, here[part], there[part])


def join(spot, layout, tables, here, there):
    return pl.pallas_call(
        lambda *refs: join_kernel(spot, layout, *refs),
        in_specs=[SMEM] * len(tables) + [VMEM, VMEM],
        out_specs=VMEM,
        out_shape=jax.ShapeDtypeStruct(here.shape, jnp.float32),
        compiler_params=params(8),
        name="join",
    )(*tables, here, there)


def pack_kernel(*refs):
    out = refs[-1]
    for k, term in enumerate(refs[:-1]):
        out[k] = term[...]


def pack(terms):
    if len(terms) == 1:
        return terms[0][None]
    return pl.pallas_call(
        pack_kernel,
        in_specs=[VMEM] * len(terms),
        out_specs=VMEM,
        out_shape=jax.ShapeDtypeStruct((len(terms), *terms[0].shape), jnp.float32),
        compiler_params=params(8),
        name="pack",
    )(*terms)


def spread(metas, terms):
    views, kinds = [], []
    for kind, term in zip(metas, terms):
        if isinstance(kind, list):
            views += [term.at[i] for i in range(len(kind))]
            kinds += kind
        else:
            views.append(term)
            kinds.append(kind)
    return views, kinds


def spans(metas, tables, layout):
    side = layout[3]
    out = []
    for twin, spot in metas:
        index, row, col, low, high = locate(spot, layout, tables, twin)
        out.append((lax.div(col, side), lax.rem(col, side), low, high))
    return out


def early_kernel(metas, layout, *refs):
    out, copied, sem = refs[-3:]
    width = len(refs) - 3 - len(metas)
    tables, terms = refs[:width], refs[width:-3]
    terms, metas = spread(metas, terms)
    side = terms[0].shape[-1]
    blocks = out.shape[-1] // side
    rows = lax.broadcasted_iota(jnp.int32, (side, side), 0)
    lane = lax.broadcasted_iota(jnp.int32, (side, side), 1)

    @pl.loop(0, blocks)
    def _(block):
        out[:, :, pl.ds(pl.multiple_of(block * side, side), side)] = jnp.zeros((2, side, side), jnp.float32)

    for k, (first, col, low, high) in enumerate(spans(metas, tables, layout)):
        for half in range(2):
            block = first + half

            @pl.when((block < blocks) & (high > low))
            def _():
                keep = (rows >= low) & (rows < high)
                keep = keep & ((lane < col) if half else (lane >= col))
                place = pl.ds(pl.multiple_of(block * side, side), side)
                for part in range(2):
                    out[part, :, place] += jnp.where(keep, terms[k][part], 0.0)

    copy = pltpu.make_async_copy(out, copied.at[:, 0], sem)
    copy.start()
    copy.wait()


def early(metas, layout, tables, terms, cols_total):
    side = layout[3]
    return pl.pallas_call(
        lambda *refs: early_kernel(metas, layout, *refs),
        in_specs=[SMEM] * len(tables) + [VMEM] * len(terms),
        out_specs=[VMEM, HBM],
        out_shape=[
            jax.ShapeDtypeStruct((2, side, cols_total), jnp.float32),
            jax.ShapeDtypeStruct((2, 1, side, cols_total), jnp.float32),
        ],
        scratch_shapes=[pltpu.SemaphoreType.DMA(())],
        compiler_params=params(20),
        name="early",
    )(*tables, *terms)


def late_kernel(metas, layout, *refs):
    width = len(refs) - 5 - len(metas)
    tables, total, terms = refs[:width], refs[width], refs[width + 1 : -4]
    out, stage, sems = refs[-3:]
    side = terms[0].shape[-1]
    blocks = out.shape[-1] // side
    rows = lax.broadcasted_iota(jnp.int32, (side, side), 0)
    lane = lax.broadcasted_iota(jnp.int32, (side, side), 1)
    ranges = spans(metas, tables, layout)

    def place(block):
        return pl.ds(pl.multiple_of(block * side, side), side)

    def send(block):
        where = place(block)
        return pltpu.make_async_copy(stage.at[:, :, where], out.at[:, 0, :, where], sems.at[block])

    def touched(block):
        hit = jnp.bool_(False)
        for first, col, low, high in ranges:
            hit = hit | (((block == first) | (block == first + 1)) & (high > low))
        return hit

    @pl.loop(0, blocks)
    def _(block):
        @pl.when(touched(block))
        def _():
            where = place(block)
            stage[:, :, where] = total[:, :, where]
            for k, (first, col, low, high) in enumerate(ranges):
                for half in range(2):

                    @pl.when((first + half == block) & (high > low))
                    def _():
                        keep = (rows >= low) & (rows < high)
                        keep = keep & ((lane < col) if half else (lane >= col))
                        for part in range(2):
                            stage[part, :, where] += jnp.where(keep, terms[k][part], 0.0)

            send(block).start()

    @pl.loop(0, blocks)
    def _(block):
        @pl.when(touched(block))
        def _():
            send(block).wait()


def late(metas, layout, tables, total, copied, terms):
    side = layout[3]
    cols_total = total.shape[-1]
    return pl.pallas_call(
        lambda *refs: late_kernel(metas, layout, *refs),
        in_specs=[SMEM] * len(tables) + [VMEM] * (1 + len(terms)) + [HBM],
        out_specs=HBM,
        input_output_aliases={len(tables) + 1 + len(terms): 0},
        out_shape=jax.ShapeDtypeStruct((2, 1, side, cols_total), jnp.float32),
        scratch_shapes=[
            pltpu.VMEM((2, side, cols_total), jnp.float32),
            pltpu.SemaphoreType.DMA((cols_total // side,)),
        ],
        compiler_params=params(28),
        name="late",
    )(*tables, total, *terms, copied)


def local(phase, absorption, probe, measured, offsets):
    side = probe.shape[-1]
    cols_total = phase.shape[2]
    sections = lax.axis_size("slab")
    each = offsets.shape[0] // sections
    n_up = each // 2
    n_here = each - n_up
    distances = list(range(sections))

    layout = (sections, n_here, n_up, side)
    pairs = offsets.T
    if n_here == n_up:
        tables = [pairs] + [swap(pairs, "tile", parity) for parity in range(2)]
    else:
        tables = [pairs, move(pairs, "tile", 1)]
    back = lambda d: (sections - d) % sections
    far = distances[1:]
    phase = pltpu.with_memory_space_constraint(phase, pltpu.HBM)
    absorption = pltpu.with_memory_space_constraint(absorption, pltpu.HBM)
    measured = pltpu.with_memory_space_constraint(measured, pltpu.HBM)

    rounds, last_round = [], {}
    for k in range(n_here):
        if n_here == n_up:
            last_round[k] = 2 * k + (lax.axis_size("tile") - 1) % 2
            for parity in range(2):
                there = lambda value, parity=parity: swap(value, "tile", parity)
                rounds.append((k, parity, parity, there, there))
        else:
            rise = lambda value: move(value, "tile", 1)
            fall = lambda value: move(value, "tile", -1)
            if k < n_up:
                last_round[k] = len(rounds)
                rounds.append((k, "hi", "lo", rise, fall))
            rounds.append((k, "lo", "hi", fall, rise))
    count = len(rounds)
    done = [pairs]

    def step(kernel):
        out = kernel([after(pairs, *done)] + tables[1:])
        done[:] = [out[0] if isinstance(out, (list, tuple)) else out]
        return out

    spots = [("send", rounds[i][2], rounds[i][0], d) for i in range(count) for d in far]
    pieces = step(lambda p: cut(spots, layout, p, phase, absorption)) if spots else []
    sent, got = [], []
    for i, (k, role, send_role, there, home) in enumerate(rounds):
        sent.append([None, *pieces[i * len(far) : (i + 1) * len(far)]])
        got.append([None] + [there(piece) for piece in sent[i][1:]])
    for i, (k, role, send_role, there, home) in enumerate(rounds):
        extra_input = [] if role == "lo" else [measured]
        spots = [("send", send_role, k, 0)]
        sent[i][0] = step(lambda p: cut(spots, layout, p, phase, absorption, *extra_input))[0]
        got[i][0] = there(sent[i][0])
    ends = sorted(last_round)
    extra = [[rotate_last(sent[last_round[k]][d], d) for d in far] for k in ends]
    held = []
    for k, role, send_role, there, home in rounds:
        spots = [("slot", role, k, d) for d in distances]
        held.append(step(lambda p: cut(spots, layout, p, phase, absorption)))
    constants = expand(side)
    others = []
    for i, (k, role, send_role, there, home) in enumerate(rounds):
        joined = []
        for d in far:
            spot = ("slot", role, k, d)
            joined.append(step(lambda p: join(spot, layout, p, held[i][d], got[i][d])))
        others.append([rotate(joined[d - 1], "slab", d) for d in far])
        if i == 0:
            done += [value for row in extra for value in row]

    twin_tables = [rotate(table, "batch", 1) for table in tables]
    done += twin_tables

    def slot(kind, spot, own, rest):
        return step(
            lambda p: run_slot(kind, spot, layout, p, probe, measured, own, rest, constants)
        )

    outs, backs, homes = [], [], []
    for i, (k, role, send_role, there, home) in enumerate(rounds):
        outs.append(slot(f"{i}", ("slot", role, k, 0), [held[i][0], got[i][0]], others[i]))
        backs.append([rotate(outs[i][d], "slab", d) for d in far])
        homes.append(home(outs[i][0]))
    last_outs = [
        slot("last", ("last", "lo", k, 0), [sent[last_round[k]][0]], extra[n])
        for n, k in enumerate(ends)
    ]
    terms, kinds = [], []

    def group(items):
        values = [value for value, spot in items]
        twins = rotate(pack(values), "batch", 1)
        terms.extend(values + [twins])
        kinds.extend([(0, spot) for value, spot in items] + [[(1, spot) for value, spot in items]])
        return twins

    final, final_kinds = [], []
    ending = [
        [rotate_last(after(last_outs[n][d], *backs[-1]), d) for d in far] for n in range(len(ends))
    ]
    for n, k in enumerate(ends):
        final += [(ending[n][d - 1], ("last", "lo", k, back(d))) for d in far]
    last_items = [(last_outs[n][0], ("last", "lo", k, 0)) for n, k in enumerate(ends)]
    for i, (k, role, send_role, there, home) in enumerate(rounds):
        items = [(outs[i][0], ("slot", role, k, 0))]
        items += [(backs[i][d - 1], ("slot", role, k, back(d))) for d in far]
        items.append((homes[i], ("swap", send_role, k, 0)))
        if i == 0:
            items = last_items + items
        twins = group(items)
        for d in far:
            final.append((home(backs[i][d - 1]), ("swap", send_role, k, back(d))))
    total, copied = early(kinds, layout, tables + twin_tables, terms, cols_total)
    values = []
    for value, spot in final:
        values += [value, rotate(after(value, total), "batch", 1)]
        final_kinds += [(0, spot), (1, spot)]
    return late(final_kinds, layout, tables + twin_tables, total, copied, values)


def solution(mesh):
    in_specs = (
        P(("groups", "slab"), "tile", None),
        P(("groups", "slab"), "tile", None),
        P(),
        P(("groups", "tile", "batch"), None, None),
        P(("groups", "tile", "batch"), None),
    )
    out_specs = P(None, ("groups", "slab"), "tile", None)
    return jax.shard_map(local, mesh=mesh, in_specs=in_specs, out_specs=out_specs, check_vma=False)
```

```python
import math

import numpy as np
import jax
import jax.numpy as jnp
from jax import lax
from jax.experimental import pallas as pl
from jax.experimental.pallas import tpu as pltpu
from jax.sharding import PartitionSpec as P

SIN = [(-1.0) ** k / math.factorial(2 * k + 1) for k in range(8)]
COS = [(-1.0) ** k / math.factorial(2 * k) for k in range(8)]
VMEM = pl.BlockSpec(memory_space=pltpu.VMEM)
SMEM = pl.BlockSpec(memory_space=pltpu.SMEM)
HBM = pl.BlockSpec(memory_space=pltpu.HBM)


def params(mib):
    return pltpu.CompilerParams(vmem_limit_bytes=mib << 20)


def cost(microseconds):
    return pl.CostEstimate(flops=int(microseconds * 1e9), transcendentals=0, bytes_accessed=0)


def after(value, *others):
    return lax.optimization_barrier((value, *others))[0]


def move(block, axis, distance):
    size = lax.axis_size(axis)
    route = [(i, i + distance) for i in range(size) if 0 <= i + distance < size]
    return lax.ppermute(block, axis, route)


def rotate(block, axis, distance):
    size = lax.axis_size(axis)
    return lax.ppermute(block, axis, [(i, (i + distance) % size) for i in range(size)])


def swap(block, axis, phase):
    size = lax.axis_size(axis)
    route = []
    for lower in range(phase, size - 1, 2):
        route += [(lower, lower + 1), (lower + 1, lower)]
    return lax.ppermute(block, axis, route)


def rotate_last(block, distance):
    tiles, size = lax.axis_size("tile"), lax.axis_size("slab")
    base = (tiles - 1) * size
    route = [(base + i, base + (i + distance) % size) for i in range(size)]
    return lax.ppermute(block, ("tile", "slab"), route)


def twin_last(block):
    tiles = lax.axis_size("tile")
    base = (tiles - 1) * 2
    return lax.ppermute(block, ("tile", "batch"), [(base, base + 1), (base + 1, base)])


def halves(matrix):
    high = matrix.astype(np.float32).astype(jnp.bfloat16)
    low = (matrix - high.astype(np.float64)).astype(np.float32).astype(jnp.bfloat16)
    return [high, low]


def compact_tables(side):
    index = np.arange(side)
    fourier = np.exp(-2j * np.pi * (index[:, None] * index[None, :] % side) / side)
    wavenumber = np.where(index < side // 2, index, index - side)
    kernel = np.exp(-1j * np.pi * (wavenumber * wavenumber % (8 * side)) / (4 * side))
    line = np.fft.ifft(kernel)
    line = (line + line[-index % side]) / 2
    fresnel = line[(index[:, None] - index[None, :]) % side]
    scaled = fourier / math.sqrt(side)
    pieces = []
    for matrix in (fresnel, scaled):
        pieces += halves(matrix.real) + halves(matrix.imag)
    return np.stack(pieces)


def expand_kernel(pieces, *outs):
    side = pieces.shape[-1]
    for which in range(2):
        real_high, real_low, imag_high, imag_low = [pieces[4 * which + k] for k in range(4)]
        real = [real_high, real_low, real_high]
        imag = [imag_high, imag_low, imag_high]
        minus = [-imag_high, -imag_low, -imag_high]
        for column, blocks in enumerate((real + minus, imag + real)):
            for row, block in enumerate(blocks):
                outs[which][pl.ds(row * side, side), pl.ds(column * side, side)] = block


def expand(side):
    pieces = jnp.asarray(compact_tables(side))
    return pl.pallas_call(
        expand_kernel,
        in_specs=[VMEM],
        out_specs=[VMEM] * 2,
        out_shape=[jax.ShapeDtypeStruct((6 * side, 2 * side), jnp.bfloat16)] * 2,
        compiler_params=params(16),
        name="expand",
    )(pieces)


def split(value):
    high = value.astype(jnp.bfloat16)
    low = (value - high.astype(jnp.float32)).astype(jnp.bfloat16)
    return high, low


def right_product(table, real, imag):
    side = real.shape[-1]
    real_high, real_low = split(real)
    imag_high, imag_low = split(imag)
    wide = jnp.concatenate([real_high, real_high, real_low, imag_high, imag_high, imag_low], axis=1)
    out = jnp.dot(wide, table[...], preferred_element_type=jnp.float32)
    return out[:, :side], out[:, side:]


def two_sided_transposed(table, real, imag):
    real, imag = right_product(table, real, imag)
    return right_product(table, real.T, imag.T)


def two_sided(table, real, imag):
    real, imag = two_sided_transposed(table, real, imag)
    return real.T, imag.T


def transmission(phase, absorption):
    square = phase * phase
    sine = jnp.full_like(phase, SIN[-1])
    cosine = jnp.full_like(phase, COS[-1])
    for a, b in zip(SIN[-2::-1], COS[-2::-1]):
        sine = sine * square + a
        cosine = cosine * square + b
    damping = jnp.exp(-absorption)
    return damping * cosine, damping * sine * phase


def is_lower(phase):
    if isinstance(phase, str):
        return phase == "lo"
    return lax.rem(lax.axis_index("tile"), 2) == phase


def pick(lower, first, second):
    if isinstance(lower, bool):
        return first if lower else second
    return jnp.where(lower, first, second)


def locate(spot, layout, tables, twin=0):
    which, phase, k, distance = spot
    sections, n_here, n_up, side = layout
    owner = lax.rem(lax.axis_index("slab") + distance, sections)
    here, up = owner * n_here + k, sections * n_here + owner * n_up + k
    width = len(tables) // 2 if len(tables) > 3 else len(tables)
    pairs = tables[width * twin]
    below = tables[width * twin + 1 + (0 if isinstance(phase, str) else phase)]
    lower = True if which == "last" else is_lower(phase)
    own, other = (here, up) if which == "slot" else (up, here)
    row = lax.rem(pick(lower, pairs[0, own], below[0, other]), side)
    col = pick(lower, pairs[1, own], below[1, other])
    low, high = pick(lower, row, jnp.int32(0)), pick(lower, jnp.int32(side), row)
    last = lax.axis_index("tile") == lax.axis_size("tile") - 1
    if which == "last":
        low = jnp.where(last, low, side)
    elif which == "swap":
        low = jnp.where(last & lower, side, low)
    return pick(lower, own, other), row, col, low, high


def slot_kernel(kind, *args):
    if kind == "last":

        @pl.when(lax.axis_index("tile") == lax.axis_size("tile") - 1)
        def _():
            slot_body(*args)
    else:
        slot_body(*args)


def slot_body(spot, layout, n_tables, *refs):
    tables, (probe, measured), refs = refs[:n_tables], refs[n_tables : n_tables + 2], refs[n_tables + 2 :]
    sections = layout[0]
    which, phase = spot[:2]
    pieces = 1 if which == "last" else 2
    own = refs[:pieces]
    others = refs[pieces : pieces + sections - 1]
    refs = refs[pieces + sections - 1 :]
    prop, dft = refs[:2]
    outs = refs[2 : 2 + sections]
    wave, trans, amplitude, sem = refs[2 + sections :]
    side = probe.shape[-1]
    slab = lax.axis_index("slab")
    index, row, col, low, high = locate(spot, layout, tables)
    col = lax.rem(col, side)
    lower = True if which == "last" else is_lower(phase)

    def fetch():
        return pltpu.make_async_copy(measured.at[index], amplitude, sem)

    if lower is True:
        fetch().start()
    elif lower is False:
        amplitude[...] = own[1][2]
    else:

        @pl.when(lower)
        def _():
            fetch().start()

        @pl.when(jnp.logical_not(lower))
        def _():
            amplitude[...] = own[1][2]

    rows = lax.broadcasted_iota(jnp.int32, (side, side), 0)
    patch = [own[0][0], own[0][1]]
    if pieces == 2:
        local_rows = (rows >= low) & (rows < high)
        patch = [jnp.where(local_rows, own[0][k], own[1][k]) for k in range(2)]
    trans[slab, 0], trans[slab, 1] = transmission(patch[0], patch[1])
    for distance in range(1, sections):
        owner = lax.rem(slab + (sections - distance), sections)
        real, imag = transmission(others[distance - 1][0], others[distance - 1][1])
        trans[owner, 0] = real
        trans[owner, 1] = imag
    for part in range(2):
        wave[0, part] = pltpu.roll(pltpu.roll(probe[part], row, 0), col, 1)
    for step in range(sections):
        a, b, c, d = wave[step, 0], wave[step, 1], trans[step, 0], trans[step, 1]
        real, imag = a * c - b * d, a * d + b * c
        if step < sections - 1:
            real, imag = two_sided(prop, real, imag)
            wave[step + 1, 0] = real
            wave[step + 1, 1] = imag
    real, imag = two_sided_transposed(dft, real, imag)
    if lower is True:
        fetch().wait()
    elif lower is not False:

        @pl.when(lower)
        def _():
            fetch().wait()

    factor = 1.0 - amplitude[...].T * lax.rsqrt(jnp.maximum(real * real + imag * imag, 0.25))
    real, minus = two_sided_transposed(dft, real * factor, -imag * factor)
    for step in range(sections - 1, -1, -1):
        a, b = wave[step, 0], wave[step, 1]
        wave[step, 0] = a * real - b * minus
        wave[step, 1] = -(a * minus + b * real)
        if step > 0:
            c, d = trans[step, 0], trans[step, 1]
            real, minus = c * real - d * minus, c * minus + d * real
            real, minus = two_sided(prop, real, minus)
    for distance in range(sections):
        outs[distance][...] = wave[lax.rem(slab + distance, sections)]


def run_slot(kind, spot, layout, tables, probe, measured, own, others, constants):
    sections, side = layout[0], layout[3]
    shape = jax.ShapeDtypeStruct((2, side, side), jnp.float32)
    return pl.pallas_call(
        lambda *refs: slot_kernel(kind, spot, layout, len(tables), *refs),
        in_specs=[SMEM] * len(tables) + [VMEM, HBM] + [VMEM] * (len(own) + len(others) + 2),
        out_specs=[VMEM] * sections,
        out_shape=[shape] * sections,
        scratch_shapes=[pltpu.VMEM((sections, 2, side, side), jnp.float32)] * 2
        + [pltpu.VMEM((side, side), jnp.float32), pltpu.SemaphoreType.DMA(())],
        compiler_params=params(32),
        name="slot_" + kind,
    )(*tables, probe, measured, *own, *others, *constants)


def cut_kernel(spots, layout, with_measured, n_tables, *refs):
    tables, (phase, absorption) = refs[:n_tables], refs[n_tables : n_tables + 2]
    refs = refs[n_tables + 2 :]
    count, side = len(spots), layout[3]
    blocks = phase.shape[2] // side
    extra = None
    if with_measured:
        sections, n_here, n_up, side = layout
        index = sections * n_here + lax.axis_index("slab") * n_up + spots[0][2]
        extra = pltpu.make_async_copy(refs[0].at[index], refs[1].at[2], refs[-3])
        refs = refs[1:]
    outs = refs[:count]
    buffer, sems = refs[-2], refs[-1]
    copies, columns = [], []
    for k in range(count):
        column = locate(spots[k], layout, tables)[2]
        first = lax.div(column, side)
        columns.append(lax.rem(column, side))
        for which, source in enumerate((phase, absorption)):
            for half in range(2):
                block = first if half == 0 else jnp.minimum(first + 1, blocks - 1)
                copies.append(
                    pltpu.make_async_copy(
                        source.at[0, :, pl.ds(pl.multiple_of(block * side, side), side)],
                        buffer.at[k, which, half],
                        sems.at[k, which, half],
                    )
                )
    for copy in copies:
        copy.start()
    if extra is not None:
        extra.start()
    lane = lax.broadcasted_iota(jnp.int32, (side, side), 1)
    for k in range(count):
        own = lane >= columns[k]
        for which in range(2):
            for half in range(2):
                copies[4 * k + 2 * which + half].wait()
            outs[k][which] = jnp.where(own, buffer[k, which, 0], buffer[k, which, 1])
    if extra is not None:
        extra.wait()


def cut(spots, layout, tables, phase, absorption, measured=None):
    side = layout[3]
    count = len(spots)
    shapes = [jax.ShapeDtypeStruct((2, side, side), jnp.float32)] * count
    scratch = [
        pltpu.VMEM((count, 2, 2, side, side), jnp.float32),
        pltpu.SemaphoreType.DMA((count, 2, 2)),
    ]
    inputs = [phase, absorption]
    if measured is not None:
        shapes = [jax.ShapeDtypeStruct((3, side, side), jnp.float32)] + shapes[1:]
        scratch = [pltpu.SemaphoreType.DMA(())] + scratch
        inputs.append(measured)
    return pl.pallas_call(
        lambda *refs: cut_kernel(spots, layout, measured is not None, len(tables), *refs),
        in_specs=[SMEM] * len(tables) + [HBM] * len(inputs),
        out_specs=[VMEM] * count,
        out_shape=shapes,
        scratch_shapes=scratch,
        compiler_params=params(16),
        name="cut",
    )(*tables, *inputs)


def join_kernel(spot, layout, *refs):
    tables, (here, there, out) = refs[:-3], refs[-3:]
    side = layout[3]
    low, high = locate(spot, layout, tables)[3:]
    rows = lax.broadcasted_iota(jnp.int32, (side, side), 0)
    keep = (rows >= low) & (rows < high)
    for part in range(2):
        out[part] = jnp.where(keep, here[part], there[part])


def join(spot, layout, tables, here, there):
    return pl.pallas_call(
        lambda *refs: join_kernel(spot, layout, *refs),
        in_specs=[SMEM] * len(tables) + [VMEM, VMEM],
        out_specs=VMEM,
        out_shape=jax.ShapeDtypeStruct(here.shape, jnp.float32),
        compiler_params=params(8),
        name="join",
    )(*tables, here, there)


def pack_kernel(*refs):
    out = refs[-1]
    for k, term in enumerate(refs[:-1]):
        out[k] = term[...]


def pack(terms):
    if len(terms) == 1:
        return terms[0][None]
    return pl.pallas_call(
        pack_kernel,
        in_specs=[VMEM] * len(terms),
        out_specs=VMEM,
        out_shape=jax.ShapeDtypeStruct((len(terms), *terms[0].shape), jnp.float32),
        compiler_params=params(8),
        name="pack",
    )(*terms)


def spread(metas, terms):
    views, kinds = [], []
    for kind, term in zip(metas, terms):
        if isinstance(kind, list):
            views += [term.at[i] for i in range(len(kind))]
            kinds += kind
        else:
            views.append(term)
            kinds.append(kind)
    return views, kinds


def spans(metas, tables, layout):
    side = layout[3]
    out = []
    for twin, spot in metas:
        index, row, col, low, high = locate(spot, layout, tables, twin)
        out.append((lax.div(col, side), lax.rem(col, side), low, high))
    return out


def early_kernel(metas, layout, *refs):
    out, copied, sem = refs[-3:]
    width = len(refs) - 3 - len(metas)
    tables, terms = refs[:width], refs[width:-3]
    terms, metas = spread(metas, terms)
    side = terms[0].shape[-1]
    blocks = out.shape[-1] // side
    rows = lax.broadcasted_iota(jnp.int32, (side, side), 0)
    lane = lax.broadcasted_iota(jnp.int32, (side, side), 1)

    @pl.loop(0, blocks)
    def _(block):
        out[:, :, pl.ds(pl.multiple_of(block * side, side), side)] = jnp.zeros((2, side, side), jnp.float32)

    for k, (first, col, low, high) in enumerate(spans(metas, tables, layout)):
        for half in range(2):
            block = first + half

            @pl.when((block < blocks) & (high > low))
            def _():
                keep = (rows >= low) & (rows < high)
                keep = keep & ((lane < col) if half else (lane >= col))
                place = pl.ds(pl.multiple_of(block * side, side), side)
                for part in range(2):
                    out[part, :, place] += jnp.where(keep, terms[k][part], 0.0)

    copy = pltpu.make_async_copy(out, copied.at[:, 0], sem)
    copy.start()
    copy.wait()


def early(metas, layout, tables, terms, cols_total):
    side = layout[3]
    return pl.pallas_call(
        lambda *refs: early_kernel(metas, layout, *refs),
        in_specs=[SMEM] * len(tables) + [VMEM] * len(terms),
        out_specs=[VMEM, HBM],
        out_shape=[
            jax.ShapeDtypeStruct((2, side, cols_total), jnp.float32),
            jax.ShapeDtypeStruct((2, 1, side, cols_total), jnp.float32),
        ],
        scratch_shapes=[pltpu.SemaphoreType.DMA(())],
        compiler_params=params(20),
        name="early",
    )(*tables, *terms)


def late_kernel(metas, layout, *refs):
    width = len(refs) - 5 - len(metas)
    tables, terms = refs[:width], refs[width + 1 : -4]
    out, stage, sems = refs[-3:]
    side = terms[0].shape[-1]
    blocks = out.shape[-1] // side
    rows = lax.broadcasted_iota(jnp.int32, (side, side), 0)
    lane = lax.broadcasted_iota(jnp.int32, (side, side), 1)
    ranges = spans(metas, tables, layout)

    def place(block):
        return pl.ds(pl.multiple_of(block * side, side), side)

    def send(block):
        where = place(block)
        return pltpu.make_async_copy(stage.at[:, :, where], out.at[:, 0, :, where], sems.at[block])

    def touched(block):
        hit = jnp.bool_(False)
        for first, col, low, high in ranges:
            hit = hit | (((block == first) | (block == first + 1)) & (high > low))
        return hit

    @pl.loop(0, blocks)
    def _(block):
        @pl.when(touched(block))
        def _():
            where = place(block)
            for k, (first, col, low, high) in enumerate(ranges):
                for half in range(2):

                    @pl.when((first + half == block) & (high > low))
                    def _():
                        keep = (rows >= low) & (rows < high)
                        keep = keep & ((lane < col) if half else (lane >= col))
                        for part in range(2):
                            stage[part, :, where] += jnp.where(keep, terms[k][part], 0.0)

            send(block).start()

    @pl.loop(0, blocks)
    def _(block):
        @pl.when(touched(block))
        def _():
            send(block).wait()


def late(metas, layout, tables, total, copied, terms):
    side = layout[3]
    cols_total = total.shape[-1]
    return pl.pallas_call(
        lambda *refs: late_kernel(metas, layout, *refs),
        in_specs=[SMEM] * len(tables) + [VMEM] * (1 + len(terms)) + [HBM],
        out_specs=[HBM, VMEM],
        input_output_aliases={len(tables) + 1 + len(terms): 0, len(tables): 1},
        out_shape=[
            jax.ShapeDtypeStruct((2, 1, side, cols_total), jnp.float32),
            jax.ShapeDtypeStruct((2, side, cols_total), jnp.float32),
        ],
        scratch_shapes=[pltpu.SemaphoreType.DMA((cols_total // side,))],
        compiler_params=params(20),
        name="late",
    )(*tables, total, *terms, copied)[0]


def local(phase, absorption, probe, measured, offsets):
    side = probe.shape[-1]
    cols_total = phase.shape[2]
    sections = lax.axis_size("slab")
    each = offsets.shape[0] // sections
    n_up = each // 2
    n_here = each - n_up
    distances = list(range(sections))

    layout = (sections, n_here, n_up, side)
    pairs = offsets.T
    if n_here == n_up:
        tables = [pairs] + [swap(pairs, "tile", parity) for parity in range(2)]
    else:
        tables = [pairs, move(pairs, "tile", 1)]
    back = lambda d: (sections - d) % sections
    far = distances[1:]
    phase = pltpu.with_memory_space_constraint(phase, pltpu.HBM)
    absorption = pltpu.with_memory_space_constraint(absorption, pltpu.HBM)
    measured = pltpu.with_memory_space_constraint(measured, pltpu.HBM)

    rounds, last_round = [], {}
    for k in range(n_here):
        if n_here == n_up:
            last_round[k] = 2 * k + (lax.axis_size("tile") - 1) % 2
            for parity in range(2):
                there = lambda value, parity=parity: swap(value, "tile", parity)
                rounds.append((k, parity, parity, there, there))
        else:
            rise = lambda value: move(value, "tile", 1)
            fall = lambda value: move(value, "tile", -1)
            if k < n_up:
                last_round[k] = len(rounds)
                rounds.append((k, "hi", "lo", rise, fall))
            rounds.append((k, "lo", "hi", fall, rise))
    count = len(rounds)
    done = [pairs]

    def step(kernel):
        out = kernel([after(pairs, *done)] + tables[1:])
        done[:] = [out[0] if isinstance(out, (list, tuple)) else out]
        return out

    sent, got, early_pieces = [], [], []
    for i, (k, role, send_role, there, home) in enumerate(rounds):
        spots = [("send", send_role, k, d) for d in far]
        if i == 0:
            spots += [("last", "lo", n, d) for n in sorted(last_round) for d in far]
        pieces = step(lambda p: cut(spots, layout, p, phase, absorption)) if far else []
        if i == 0:
            pieces, early_pieces = pieces[: len(far)], pieces[len(far) :]
        sent.append([None, *pieces])
        got.append([None] + [there(piece) for piece in pieces])
    for i, (k, role, send_role, there, home) in enumerate(rounds):
        extra_input = [] if role == "lo" else [measured]
        spots = [("send", send_role, k, 0)]
        sent[i][0] = step(lambda p: cut(spots, layout, p, phase, absorption, *extra_input))[0]
        got[i][0] = there(sent[i][0])
    ends = sorted(last_round)
    extra = [
        [rotate_last(early_pieces[n * len(far) + d - 1], d) for d in far] for n in range(len(ends))
    ]
    held = []
    for k, role, send_role, there, home in rounds:
        spots = [("slot", role, k, d) for d in distances]
        held.append(step(lambda p: cut(spots, layout, p, phase, absorption)))
    constants = expand(side)
    done += [value for row in extra for value in row]
    others = []
    for i, (k, role, send_role, there, home) in enumerate(rounds):
        joined = []
        for d in far:
            spot = ("slot", role, k, d)
            joined.append(step(lambda p: join(spot, layout, p, held[i][d], got[i][d])))
        others.append([rotate(joined[d - 1], "slab", d) for d in far])

    twin_tables = [rotate(table, "batch", 1) for table in tables]
    done += twin_tables

    def slot(kind, spot, own, rest):
        return step(
            lambda p: run_slot(kind, spot, layout, p, probe, measured, own, rest, constants)
        )

    outs, backs, homes = [], [], []
    for i, (k, role, send_role, there, home) in enumerate(rounds):
        outs.append(slot(f"{i}", ("slot", role, k, 0), [held[i][0], got[i][0]], others[i]))
        backs.append([rotate(outs[i][d], "slab", d) for d in far])
        homes.append(home(outs[i][0]))
    last_outs = [
        slot("last", ("last", "lo", k, 0), [sent[last_round[k]][0]], extra[n])
        for n, k in enumerate(ends)
    ]
    terms, kinds = [], []

    def group(items):
        values = [value for value, spot in items]
        twins = rotate(pack(values), "batch", 1)
        terms.extend(values + [twins])
        kinds.extend([(0, spot) for value, spot in items] + [[(1, spot) for value, spot in items]])
        return twins

    final, final_kinds = [], []
    ending = [
        [rotate_last(after(last_outs[n][d], *backs[-1]), d) for d in far] for n in range(len(ends))
    ]
    for n, k in enumerate(ends):
        final += [(ending[n][d - 1], ("last", "lo", k, back(d))) for d in far]
    last_items = [(last_outs[n][0], ("last", "lo", k, 0)) for n, k in enumerate(ends)]
    for i, (k, role, send_role, there, home) in enumerate(rounds):
        items = [(outs[i][0], ("slot", role, k, 0))]
        items += [(backs[i][d - 1], ("slot", role, k, back(d))) for d in far]
        items.append((homes[i], ("swap", send_role, k, 0)))
        if i == 0:
            items = last_items + items
        twins = group(items)
        for d in far:
            final.append((home(backs[i][d - 1]), ("swap", send_role, k, back(d))))
    total, copied = early(kinds, layout, tables + twin_tables, terms, cols_total)
    values = []
    for value, spot in final:
        gated = after(value, total)
        values += [value, twin_last(gated) if spot[0] == "last" else rotate(gated, "batch", 1)]
        final_kinds += [(0, spot), (1, spot)]
    return late(final_kinds, layout, tables + twin_tables, total, copied, values)


def solution(mesh):
    in_specs = (
        P(("groups", "slab"), "tile", None),
        P(("groups", "slab"), "tile", None),
        P(),
        P(("groups", "tile", "batch"), None, None),
        P(("groups", "tile", "batch"), None),
    )
    out_specs = P(None, ("groups", "slab"), "tile", None)
    return jax.shard_map(local, mesh=mesh, in_specs=in_specs, out_specs=out_specs, check_vma=False)
```

```python
import math

import numpy as np
import jax
import jax.numpy as jnp
from jax import lax
from jax.experimental import pallas as pl
from jax.experimental.pallas import tpu as pltpu
from jax.sharding import PartitionSpec as P

SIN = [(-1.0) ** k / math.factorial(2 * k + 1) for k in range(8)]
COS = [(-1.0) ** k / math.factorial(2 * k) for k in range(8)]
VMEM = pl.BlockSpec(memory_space=pltpu.VMEM)
SMEM = pl.BlockSpec(memory_space=pltpu.SMEM)
HBM = pl.BlockSpec(memory_space=pltpu.HBM)


def params(mib):
    return pltpu.CompilerParams(vmem_limit_bytes=mib << 20)


def cost(microseconds):
    return pl.CostEstimate(flops=int(microseconds * 1e9), transcendentals=0, bytes_accessed=0)


def after(value, *others):
    return lax.optimization_barrier((value, *others))[0]


def move(block, axis, distance):
    size = lax.axis_size(axis)
    route = [(i, i + distance) for i in range(size) if 0 <= i + distance < size]
    return lax.ppermute(block, axis, route)


def rotate(block, axis, distance):
    size = lax.axis_size(axis)
    return lax.ppermute(block, axis, [(i, (i + distance) % size) for i in range(size)])


def swap(block, axis, phase):
    size = lax.axis_size(axis)
    route = []
    for lower in range(phase, size - 1, 2):
        route += [(lower, lower + 1), (lower + 1, lower)]
    return lax.ppermute(block, axis, route)


def rotate_last(block, distance):
    tiles, size = lax.axis_size("tile"), lax.axis_size("slab")
    base = (tiles - 1) * size
    route = [(base + i, base + (i + distance) % size) for i in range(size)]
    return lax.ppermute(block, ("tile", "slab"), route)


def halves(matrix):
    high = matrix.astype(np.float32).astype(jnp.bfloat16)
    low = (matrix - high.astype(np.float64)).astype(np.float32).astype(jnp.bfloat16)
    return [high, low]


def compact_tables(side):
    index = np.arange(side)
    fourier = np.exp(-2j * np.pi * (index[:, None] * index[None, :] % side) / side)
    wavenumber = np.where(index < side // 2, index, index - side)
    kernel = np.exp(-1j * np.pi * (wavenumber * wavenumber % (8 * side)) / (4 * side))
    line = np.fft.ifft(kernel)
    line = (line + line[-index % side]) / 2
    fresnel = line[(index[:, None] - index[None, :]) % side]
    scaled = fourier / math.sqrt(side)
    pieces = []
    for matrix in (fresnel, scaled):
        pieces += halves(matrix.real) + halves(matrix.imag)
    return np.stack(pieces)


def expand_kernel(pieces, *outs):
    side = pieces.shape[-1]
    for which in range(2):
        real_high, real_low, imag_high, imag_low = [pieces[4 * which + k] for k in range(4)]
        real = [real_high, real_low, real_high]
        imag = [imag_high, imag_low, imag_high]
        minus = [-imag_high, -imag_low, -imag_high]
        for column, blocks in enumerate((real + minus, imag + real)):
            for row, block in enumerate(blocks):
                outs[which][pl.ds(row * side, side), pl.ds(column * side, side)] = block


def expand(side):
    pieces = jnp.asarray(compact_tables(side))
    return pl.pallas_call(
        expand_kernel,
        in_specs=[VMEM],
        out_specs=[VMEM] * 2,
        out_shape=[jax.ShapeDtypeStruct((6 * side, 2 * side), jnp.bfloat16)] * 2,
        compiler_params=params(16),
        name="expand",
    )(pieces)


def split(value):
    high = value.astype(jnp.bfloat16)
    low = (value - high.astype(jnp.float32)).astype(jnp.bfloat16)
    return high, low


def right_product(table, real, imag):
    side = real.shape[-1]
    real_high, real_low = split(real)
    imag_high, imag_low = split(imag)
    wide = jnp.concatenate([real_high, real_high, real_low, imag_high, imag_high, imag_low], axis=1)
    out = jnp.dot(wide, table[...], preferred_element_type=jnp.float32)
    return out[:, :side], out[:, side:]


def two_sided_transposed(table, real, imag):
    real, imag = right_product(table, real, imag)
    return right_product(table, real.T, imag.T)


def two_sided(table, real, imag):
    real, imag = two_sided_transposed(table, real, imag)
    return real.T, imag.T


def transmission(phase, absorption):
    square = phase * phase
    sine = jnp.full_like(phase, SIN[-1])
    cosine = jnp.full_like(phase, COS[-1])
    for a, b in zip(SIN[-2::-1], COS[-2::-1]):
        sine = sine * square + a
        cosine = cosine * square + b
    damping = jnp.exp(-absorption)
    return damping * cosine, damping * sine * phase


def is_lower(phase):
    if isinstance(phase, str):
        return phase == "lo"
    return lax.rem(lax.axis_index("tile"), 2) == phase


def pick(lower, first, second):
    if isinstance(lower, bool):
        return first if lower else second
    return jnp.where(lower, first, second)


def locate(spot, layout, tables, twin=0):
    which, phase, k, distance = spot
    sections, n_here, n_up, side = layout
    owner = lax.rem(lax.axis_index("slab") + distance, sections)
    here, up = owner * n_here + k, sections * n_here + owner * n_up + k
    width = len(tables) // 2 if len(tables) > 3 else len(tables)
    pairs = tables[width * twin]
    below = tables[width * twin + 1]
    lower = True if which == "last" else is_lower(phase)
    own, other = (here, up) if which == "slot" else (up, here)
    row = lax.rem(pick(lower, pairs[0, own], below[0, other]), side)
    col = pick(lower, pairs[1, own], below[1, other])
    low, high = pick(lower, row, jnp.int32(0)), pick(lower, jnp.int32(side), row)
    last = lax.axis_index("tile") == lax.axis_size("tile") - 1
    if which == "last":
        low = jnp.where(last, low, side)
    elif which == "swap":
        low = jnp.where(last & lower, side, low)
    return pick(lower, own, other), row, col, low, high


def slot_kernel(kind, *args):
    if kind == "last":

        @pl.when(lax.axis_index("tile") == lax.axis_size("tile") - 1)
        def _():
            slot_body(*args)
    else:
        slot_body(*args)


def slot_body(spot, layout, n_tables, *refs):
    tables, (probe, measured), refs = refs[:n_tables], refs[n_tables : n_tables + 2], refs[n_tables + 2 :]
    sections = layout[0]
    which, phase = spot[:2]
    pieces = 1 if which == "last" else 2
    own = refs[:pieces]
    others = refs[pieces : pieces + sections - 1]
    refs = refs[pieces + sections - 1 :]
    prop, dft = refs[:2]
    outs = refs[2 : 2 + sections]
    wave, trans, amplitude, sem = refs[2 + sections :]
    side = probe.shape[-1]
    slab = lax.axis_index("slab")
    index, row, col, low, high = locate(spot, layout, tables)
    col = lax.rem(col, side)
    lower = True if which == "last" else is_lower(phase)

    def fetch():
        return pltpu.make_async_copy(measured.at[index], amplitude, sem)

    if lower is True:
        fetch().start()
    elif lower is False:
        amplitude[...] = own[1][2]
    else:

        @pl.when(lower)
        def _():
            fetch().start()

        @pl.when(jnp.logical_not(lower))
        def _():
            amplitude[...] = own[1][2]

    rows = lax.broadcasted_iota(jnp.int32, (side, side), 0)
    patch = [own[0][0], own[0][1]]
    if pieces == 2:
        local_rows = (rows >= low) & (rows < high)
        patch = [jnp.where(local_rows, own[0][k], own[1][k]) for k in range(2)]
    trans[slab, 0], trans[slab, 1] = transmission(patch[0], patch[1])
    for distance in range(1, sections):
        owner = lax.rem(slab + (sections - distance), sections)
        real, imag = transmission(others[distance - 1][0], others[distance - 1][1])
        trans[owner, 0] = real
        trans[owner, 1] = imag
    for part in range(2):
        wave[0, part] = pltpu.roll(pltpu.roll(probe[part], row, 0), col, 1)
    for step in range(sections):
        a, b, c, d = wave[step, 0], wave[step, 1], trans[step, 0], trans[step, 1]
        real, imag = a * c - b * d, a * d + b * c
        if step < sections - 1:
            real, imag = two_sided(prop, real, imag)
            wave[step + 1, 0] = real
            wave[step + 1, 1] = imag
    real, imag = two_sided_transposed(dft, real, imag)
    if lower is True:
        fetch().wait()
    elif lower is not False:

        @pl.when(lower)
        def _():
            fetch().wait()

    factor = 1.0 - amplitude[...].T * lax.rsqrt(jnp.maximum(real * real + imag * imag, 0.25))
    real, minus = two_sided_transposed(dft, real * factor, -imag * factor)
    for step in range(sections - 1, -1, -1):
        a, b = wave[step, 0], wave[step, 1]
        wave[step, 0] = a * real - b * minus
        wave[step, 1] = -(a * minus + b * real)
        if step > 0:
            c, d = trans[step, 0], trans[step, 1]
            real, minus = c * real - d * minus, c * minus + d * real
            real, minus = two_sided(prop, real, minus)
    for distance in range(sections):
        outs[distance][...] = wave[lax.rem(slab + distance, sections)]


def run_slot(kind, spot, layout, tables, probe, measured, own, others, constants):
    sections, side = layout[0], layout[3]
    shape = jax.ShapeDtypeStruct((2, side, side), jnp.float32)
    return pl.pallas_call(
        lambda *refs: slot_kernel(kind, spot, layout, len(tables), *refs),
        in_specs=[SMEM] * len(tables) + [VMEM, HBM] + [VMEM] * (len(own) + len(others) + 2),
        out_specs=[VMEM] * sections,
        out_shape=[shape] * sections,
        scratch_shapes=[pltpu.VMEM((sections, 2, side, side), jnp.float32)] * 2
        + [pltpu.VMEM((side, side), jnp.float32), pltpu.SemaphoreType.DMA(())],
        compiler_params=params(32),
        name="slot_" + kind,
    )(*tables, probe, measured, *own, *others, *constants)


def cut_kernel(spots, layout, with_measured, n_tables, *refs):
    tables, (phase, absorption) = refs[:n_tables], refs[n_tables : n_tables + 2]
    refs = refs[n_tables + 2 :]
    count, side = len(spots), layout[3]
    blocks = phase.shape[2] // side
    extra = None
    if with_measured:
        sections, n_here, n_up, side = layout
        index = sections * n_here + lax.axis_index("slab") * n_up + spots[0][2]
        extra = pltpu.make_async_copy(refs[0].at[index], refs[1].at[2], refs[-3])
        refs = refs[1:]
    outs = refs[:count]
    buffer, sems = refs[-2], refs[-1]
    copies, columns = [], []
    for k in range(count):
        column = locate(spots[k], layout, tables)[2]
        first = lax.div(column, side)
        columns.append(lax.rem(column, side))
        for which, source in enumerate((phase, absorption)):
            for half in range(2):
                block = first if half == 0 else jnp.minimum(first + 1, blocks - 1)
                copies.append(
                    pltpu.make_async_copy(
                        source.at[0, :, pl.ds(pl.multiple_of(block * side, side), side)],
                        buffer.at[k, which, half],
                        sems.at[k, which, half],
                    )
                )
    for copy in copies:
        copy.start()
    if extra is not None:
        extra.start()
    lane = lax.broadcasted_iota(jnp.int32, (side, side), 1)
    for k in range(count):
        own = lane >= columns[k]
        for which in range(2):
            for half in range(2):
                copies[4 * k + 2 * which + half].wait()
            outs[k][which] = jnp.where(own, buffer[k, which, 0], buffer[k, which, 1])
    if extra is not None:
        extra.wait()


def cut(spots, layout, tables, phase, absorption, measured=None):
    side = layout[3]
    count = len(spots)
    shapes = [jax.ShapeDtypeStruct((2, side, side), jnp.float32)] * count
    scratch = [
        pltpu.VMEM((count, 2, 2, side, side), jnp.float32),
        pltpu.SemaphoreType.DMA((count, 2, 2)),
    ]
    inputs = [phase, absorption]
    if measured is not None:
        shapes = [jax.ShapeDtypeStruct((3, side, side), jnp.float32)] + shapes[1:]
        scratch = [pltpu.SemaphoreType.DMA(())] + scratch
        inputs.append(measured)
    return pl.pallas_call(
        lambda *refs: cut_kernel(spots, layout, measured is not None, len(tables), *refs),
        in_specs=[SMEM] * len(tables) + [HBM] * len(inputs),
        out_specs=[VMEM] * count,
        out_shape=shapes,
        scratch_shapes=scratch,
        compiler_params=params(16),
        name="cut",
    )(*tables, *inputs)


def join_kernel(spot, layout, *refs):
    tables, (here, there, out) = refs[:-3], refs[-3:]
    side = layout[3]
    low, high = locate(spot, layout, tables)[3:]
    rows = lax.broadcasted_iota(jnp.int32, (side, side), 0)
    keep = (rows >= low) & (rows < high)
    for part in range(2):
        out[part] = jnp.where(keep, here[part], there[part])


def join(spot, layout, tables, here, there):
    return pl.pallas_call(
        lambda *refs: join_kernel(spot, layout, *refs),
        in_specs=[SMEM] * len(tables) + [VMEM, VMEM],
        out_specs=VMEM,
        out_shape=jax.ShapeDtypeStruct(here.shape, jnp.float32),
        compiler_params=params(8),
        name="join",
    )(*tables, here, there)


def pack_kernel(*refs):
    out = refs[-1]
    for k, term in enumerate(refs[:-1]):
        out[k] = term[...]


def pack(terms):
    if len(terms) == 1:
        return terms[0][None]
    return pl.pallas_call(
        pack_kernel,
        in_specs=[VMEM] * len(terms),
        out_specs=VMEM,
        out_shape=jax.ShapeDtypeStruct((len(terms), *terms[0].shape), jnp.float32),
        compiler_params=params(8),
        name="pack",
    )(*terms)


def spread(metas, terms):
    views, kinds = [], []
    for kind, term in zip(metas, terms):
        if isinstance(kind, list):
            views += [term.at[i] for i in range(len(kind))]
            kinds += kind
        else:
            views.append(term)
            kinds.append(kind)
    return views, kinds


def spans(metas, tables, layout):
    side = layout[3]
    out = []
    for twin, spot in metas:
        index, row, col, low, high = locate(spot, layout, tables, twin)
        out.append((lax.div(col, side), lax.rem(col, side), low, high))
    return out


def early_kernel(metas, layout, *refs):
    out, copied, sem = refs[-3:]
    width = len(refs) - 3 - len(metas)
    tables, terms = refs[:width], refs[width:-3]
    terms, metas = spread(metas, terms)
    side = terms[0].shape[-1]
    blocks = out.shape[-1] // side
    rows = lax.broadcasted_iota(jnp.int32, (side, side), 0)
    lane = lax.broadcasted_iota(jnp.int32, (side, side), 1)

    @pl.loop(0, blocks)
    def _(block):
        out[:, :, pl.ds(pl.multiple_of(block * side, side), side)] = jnp.zeros((2, side, side), jnp.float32)

    for k, (first, col, low, high) in enumerate(spans(metas, tables, layout)):
        for half in range(2):
            block = first + half

            @pl.when((block < blocks) & (high > low))
            def _():
                keep = (rows >= low) & (rows < high)
                keep = keep & ((lane < col) if half else (lane >= col))
                place = pl.ds(pl.multiple_of(block * side, side), side)
                for part in range(2):
                    out[part, :, place] += jnp.where(keep, terms[k][part], 0.0)

    copy = pltpu.make_async_copy(out, copied.at[:, 0], sem)
    copy.start()
    copy.wait()


def early(metas, layout, tables, terms, cols_total):
    side = layout[3]
    return pl.pallas_call(
        lambda *refs: early_kernel(metas, layout, *refs),
        in_specs=[SMEM] * len(tables) + [VMEM] * len(terms),
        out_specs=[VMEM, HBM],
        out_shape=[
            jax.ShapeDtypeStruct((2, side, cols_total), jnp.float32),
            jax.ShapeDtypeStruct((2, 1, side, cols_total), jnp.float32),
        ],
        scratch_shapes=[pltpu.SemaphoreType.DMA(())],
        compiler_params=params(20),
        name="early",
    )(*tables, *terms)


def late_kernel(metas, layout, *refs):
    width = len(refs) - 5 - len(metas)
    tables, total, terms = refs[:width], refs[width], refs[width + 1 : -4]
    out, stage, sems = refs[-3:]
    side = terms[0].shape[-1]
    blocks = out.shape[-1] // side
    rows = lax.broadcasted_iota(jnp.int32, (side, side), 0)
    lane = lax.broadcasted_iota(jnp.int32, (side, side), 1)
    ranges = spans(metas, tables, layout)

    def place(block):
        return pl.ds(pl.multiple_of(block * side, side), side)

    def send(block):
        where = place(block)
        return pltpu.make_async_copy(stage.at[:, :, where], out.at[:, 0, :, where], sems.at[block])

    def touched(block):
        hit = jnp.bool_(False)
        for first, col, low, high in ranges:
            hit = hit | (((block == first) | (block == first + 1)) & (high > low))
        return hit

    @pl.loop(0, blocks)
    def _(block):
        @pl.when(touched(block))
        def _():
            where = place(block)
            stage[:, :, where] = total[:, :, where]
            for k, (first, col, low, high) in enumerate(ranges):
                for half in range(2):

                    @pl.when((first + half == block) & (high > low))
                    def _():
                        keep = (rows >= low) & (rows < high)
                        keep = keep & ((lane < col) if half else (lane >= col))
                        for part in range(2):
                            stage[part, :, where] += jnp.where(keep, terms[k][part], 0.0)

            send(block).start()

    @pl.loop(0, blocks)
    def _(block):
        @pl.when(touched(block))
        def _():
            send(block).wait()


def late(metas, layout, tables, total, copied, terms):
    side = layout[3]
    cols_total = total.shape[-1]
    return pl.pallas_call(
        lambda *refs: late_kernel(metas, layout, *refs),
        in_specs=[SMEM] * len(tables) + [VMEM] * (1 + len(terms)) + [HBM],
        out_specs=HBM,
        input_output_aliases={len(tables) + 1 + len(terms): 0},
        out_shape=jax.ShapeDtypeStruct((2, 1, side, cols_total), jnp.float32),
        scratch_shapes=[
            pltpu.VMEM((2, side, cols_total), jnp.float32),
            pltpu.SemaphoreType.DMA((cols_total // side,)),
        ],
        compiler_params=params(28),
        name="late",
    )(*tables, total, *terms, copied)


def local(phase, absorption, probe, measured, offsets):
    side = probe.shape[-1]
    cols_total = phase.shape[2]
    sections = lax.axis_size("slab")
    each = offsets.shape[0] // sections
    n_up = each // 2
    n_here = each - n_up
    distances = list(range(sections))

    layout = (sections, n_here, n_up, side)
    pairs = offsets.T
    tables = [pairs, move(pairs, "tile", 1)]
    back = lambda d: (sections - d) % sections
    far = distances[1:]
    phase = pltpu.with_memory_space_constraint(phase, pltpu.HBM)
    absorption = pltpu.with_memory_space_constraint(absorption, pltpu.HBM)
    measured = pltpu.with_memory_space_constraint(measured, pltpu.HBM)

    rounds, last_round = [], {}
    for k in range(n_here):
        if n_here == n_up:
            last_round[k] = 2 * k + (lax.axis_size("tile") - 1) % 2
            for parity in range(2):
                there = lambda value, parity=parity: swap(value, "tile", parity)
                rounds.append((k, parity, parity, there, there))
        else:
            rise = lambda value: move(value, "tile", 1)
            fall = lambda value: move(value, "tile", -1)
            if k < n_up:
                last_round[k] = len(rounds)
                rounds.append((k, "hi", "lo", rise, fall))
            rounds.append((k, "lo", "hi", fall, rise))
    count = len(rounds)
    done = [pairs]

    def step(kernel):
        out = kernel([after(pairs, *done)] + tables[1:])
        done[:] = [out[0] if isinstance(out, (list, tuple)) else out]
        return out

    spots = [("send", rounds[i][2], rounds[i][0], d) for i in range(count) for d in far]
    pieces = step(lambda p: cut(spots, layout, p, phase, absorption)) if spots else []
    sent, got = [], []
    for i, (k, role, send_role, there, home) in enumerate(rounds):
        sent.append([None, *pieces[i * len(far) : (i + 1) * len(far)]])
        got.append([None] + [there(piece) for piece in sent[i][1:]])
    for i, (k, role, send_role, there, home) in enumerate(rounds):
        extra_input = [] if role == "lo" else [measured]
        spots = [("send", send_role, k, 0)]
        sent[i][0] = step(lambda p: cut(spots, layout, p, phase, absorption, *extra_input))[0]
        got[i][0] = there(sent[i][0])
    ends = sorted(last_round)
    extra = [[rotate_last(sent[last_round[k]][d], d) for d in far] for k in ends]
    held = []
    for k, role, send_role, there, home in rounds:
        spots = [("slot", role, k, d) for d in distances]
        held.append(step(lambda p: cut(spots, layout, p, phase, absorption)))
    constants = expand(side)
    others = []
    for i, (k, role, send_role, there, home) in enumerate(rounds):
        joined = []
        for d in far:
            spot = ("slot", role, k, d)
            joined.append(step(lambda p: join(spot, layout, p, held[i][d], got[i][d])))
        others.append([rotate(joined[d - 1], "slab", d) for d in far])
        if i == 0:
            done += [value for row in extra for value in row]

    twin_tables = [rotate(table, "batch", 1) for table in tables]
    done += twin_tables

    def slot(kind, spot, own, rest):
        return step(
            lambda p: run_slot(kind, spot, layout, p, probe, measured, own, rest, constants)
        )

    outs, backs, homes = [], [], []
    for i, (k, role, send_role, there, home) in enumerate(rounds):
        outs.append(slot(f"{i}", ("slot", role, k, 0), [held[i][0], got[i][0]], others[i]))
        backs.append([rotate(outs[i][d], "slab", d) for d in far])
        homes.append(home(outs[i][0]))
    last_outs = [
        slot("last", ("last", "lo", k, 0), [sent[last_round[k]][0]], extra[n])
        for n, k in enumerate(ends)
    ]
    terms, kinds = [], []

    def group(items):
        values = [value for value, spot in items]
        twins = rotate(pack(values), "batch", 1)
        terms.extend(values + [twins])
        kinds.extend([(0, spot) for value, spot in items] + [[(1, spot) for value, spot in items]])
        return twins

    final, final_kinds = [], []
    ending = [
        [rotate_last(after(last_outs[n][d], *backs[-1]), d) for d in far] for n in range(len(ends))
    ]
    for n, k in enumerate(ends):
        final += [(ending[n][d - 1], ("last", "lo", k, back(d))) for d in far]
    last_items = [(last_outs[n][0], ("last", "lo", k, 0)) for n, k in enumerate(ends)]
    for i, (k, role, send_role, there, home) in enumerate(rounds):
        items = [(outs[i][0], ("slot", role, k, 0))]
        items += [(backs[i][d - 1], ("slot", role, k, back(d))) for d in far]
        items.append((homes[i], ("swap", send_role, k, 0)))
        if i == 0:
            items = last_items + items
        twins = group(items)
        for d in far:
            final.append((home(backs[i][d - 1]), ("swap", send_role, k, back(d))))
    total, copied = early(kinds, layout, tables + twin_tables, terms, cols_total)
    values = []
    for value, spot in final:
        values += [value, rotate(after(value, total), "batch", 1)]
        final_kinds += [(0, spot), (1, spot)]
    return late(final_kinds, layout, tables + twin_tables, total, copied, values)


def solution(mesh):
    in_specs = (
        P(("groups", "slab"), "tile", None),
        P(("groups", "slab"), "tile", None),
        P(),
        P(("groups", "tile", "batch"), None, None),
        P(("groups", "tile", "batch"), None),
    )
    out_specs = P(None, ("groups", "slab"), "tile", None)
    return jax.shard_map(local, mesh=mesh, in_specs=in_specs, out_specs=out_specs, check_vma=False)
```

```python
import math

import numpy as np
import jax
import jax.numpy as jnp
from jax import lax
from jax.experimental import pallas as pl
from jax.experimental.pallas import tpu as pltpu
from jax.sharding import PartitionSpec as P

SIN = [(-1.0) ** k / math.factorial(2 * k + 1) for k in range(8)]
COS = [(-1.0) ** k / math.factorial(2 * k) for k in range(8)]
VMEM = pl.BlockSpec(memory_space=pltpu.VMEM)
SMEM = pl.BlockSpec(memory_space=pltpu.SMEM)
HBM = pl.BlockSpec(memory_space=pltpu.HBM)


def params(mib):
    return pltpu.CompilerParams(vmem_limit_bytes=mib << 20)


def cost(microseconds):
    return pl.CostEstimate(flops=int(microseconds * 1e9), transcendentals=0, bytes_accessed=0)


def after(value, *others):
    return lax.optimization_barrier((value, *others))[0]


def move(block, axis, distance):
    size = lax.axis_size(axis)
    route = [(i, i + distance) for i in range(size) if 0 <= i + distance < size]
    return lax.ppermute(block, axis, route)


def rotate(block, axis, distance):
    size = lax.axis_size(axis)
    return lax.ppermute(block, axis, [(i, (i + distance) % size) for i in range(size)])


def swap(block, axis, phase):
    size = lax.axis_size(axis)
    route = []
    for lower in range(phase, size - 1, 2):
        route += [(lower, lower + 1), (lower + 1, lower)]
    return lax.ppermute(block, axis, route)


def rotate_last(block, distance):
    tiles, size = lax.axis_size("tile"), lax.axis_size("slab")
    base = (tiles - 1) * size
    route = [(base + i, base + (i + distance) % size) for i in range(size)]
    return lax.ppermute(block, ("tile", "slab"), route)


def halves(matrix):
    high = matrix.astype(np.float32).astype(jnp.bfloat16)
    low = (matrix - high.astype(np.float64)).astype(np.float32).astype(jnp.bfloat16)
    return [high, low]


def compact_tables(side):
    index = np.arange(side)
    fourier = np.exp(-2j * np.pi * (index[:, None] * index[None, :] % side) / side)
    wavenumber = np.where(index < side // 2, index, index - side)
    kernel = np.exp(-1j * np.pi * (wavenumber * wavenumber % (8 * side)) / (4 * side))
    line = np.fft.ifft(kernel)
    line = (line + line[-index % side]) / 2
    fresnel = line[(index[:, None] - index[None, :]) % side]
    scaled = fourier / math.sqrt(side)
    pieces = []
    for matrix in (fresnel, scaled):
        pieces += halves(matrix.real) + halves(matrix.imag)
    return np.stack(pieces)


def expand_kernel(pieces, *outs):
    side = pieces.shape[-1]
    for which in range(2):
        real_high, real_low, imag_high, imag_low = [pieces[4 * which + k] for k in range(4)]
        real = [real_high, real_low, real_high]
        imag = [imag_high, imag_low, imag_high]
        minus = [-imag_high, -imag_low, -imag_high]
        for column, blocks in enumerate((real + minus, imag + real)):
            for row, block in enumerate(blocks):
                outs[which][pl.ds(row * side, side), pl.ds(column * side, side)] = block


def expand(side, *gates):
    pieces = after(jnp.asarray(compact_tables(side)), *gates)
    return pl.pallas_call(
        expand_kernel,
        in_specs=[VMEM],
        out_specs=[VMEM] * 2,
        out_shape=[jax.ShapeDtypeStruct((6 * side, 2 * side), jnp.bfloat16)] * 2,
        compiler_params=params(16),
        name="expand",
    )(pieces)


def split(value):
    high = value.astype(jnp.bfloat16)
    low = (value - high.astype(jnp.float32)).astype(jnp.bfloat16)
    return high, low


def right_product(table, real, imag):
    side = real.shape[-1]
    real_high, real_low = split(real)
    imag_high, imag_low = split(imag)
    wide = jnp.concatenate([real_high, real_high, real_low, imag_high, imag_high, imag_low], axis=1)
    out = jnp.dot(wide, table[...], preferred_element_type=jnp.float32)
    return out[:, :side], out[:, side:]


def two_sided_transposed(table, real, imag):
    real, imag = right_product(table, real, imag)
    return right_product(table, real.T, imag.T)


def two_sided(table, real, imag):
    real, imag = two_sided_transposed(table, real, imag)
    return real.T, imag.T


def transmission(phase, absorption):
    square = phase * phase
    sine = jnp.full_like(phase, SIN[-1])
    cosine = jnp.full_like(phase, COS[-1])
    for a, b in zip(SIN[-2::-1], COS[-2::-1]):
        sine = sine * square + a
        cosine = cosine * square + b
    damping = jnp.exp(-absorption)
    return damping * cosine, damping * sine * phase


def is_lower(phase):
    if isinstance(phase, str):
        return phase == "lo"
    return lax.rem(lax.axis_index("tile"), 2) == phase


def pick(lower, first, second):
    if isinstance(lower, bool):
        return first if lower else second
    return jnp.where(lower, first, second)


def locate(spot, layout, tables, twin=0):
    which, phase, k, distance = spot
    sections, n_here, n_up, side = layout
    owner = lax.rem(lax.axis_index("slab") + distance, sections)
    here, up = owner * n_here + k, sections * n_here + owner * n_up + k
    width = len(tables) // 2 if len(tables) > 3 else len(tables)
    pairs = tables[width * twin]
    below = tables[width * twin + 1 + (0 if isinstance(phase, str) else phase)]
    lower = True if which == "last" else is_lower(phase)
    own, other = (here, up) if which == "slot" else (up, here)
    row = lax.rem(pick(lower, pairs[0, own], below[0, other]), side)
    col = pick(lower, pairs[1, own], below[1, other])
    low, high = pick(lower, row, jnp.int32(0)), pick(lower, jnp.int32(side), row)
    last = lax.axis_index("tile") == lax.axis_size("tile") - 1
    if which == "last":
        low = jnp.where(last, low, side)
    elif which == "swap":
        low = jnp.where(last & lower, side, low)
    return pick(lower, own, other), row, col, low, high


def slot_kernel(kind, *args):
    if kind == "last":

        @pl.when(lax.axis_index("tile") == lax.axis_size("tile") - 1)
        def _():
            slot_body(*args)
    else:
        slot_body(*args)


def slot_body(spot, layout, n_tables, *refs):
    tables, (probe, measured), refs = refs[:n_tables], refs[n_tables : n_tables + 2], refs[n_tables + 2 :]
    sections = layout[0]
    which, phase = spot[:2]
    pieces = 1 if which == "last" else 2
    own = refs[:pieces]
    others = refs[pieces : pieces + sections - 1]
    refs = refs[pieces + sections - 1 :]
    prop, dft = refs[:2]
    outs = refs[2 : 2 + sections]
    wave, trans, amplitude, sem = refs[2 + sections :]
    side = probe.shape[-1]
    slab = lax.axis_index("slab")
    index, row, col, low, high = locate(spot, layout, tables)
    col = lax.rem(col, side)
    lower = True if which == "last" else is_lower(phase)

    def fetch():
        return pltpu.make_async_copy(measured.at[index], amplitude, sem)

    if lower is True:
        fetch().start()
    elif lower is False:
        amplitude[...] = own[1][2]
    else:

        @pl.when(lower)
        def _():
            fetch().start()

        @pl.when(jnp.logical_not(lower))
        def _():
            amplitude[...] = own[1][2]

    rows = lax.broadcasted_iota(jnp.int32, (side, side), 0)
    patch = [own[0][0], own[0][1]]
    if pieces == 2:
        local_rows = (rows >= low) & (rows < high)
        patch = [jnp.where(local_rows, own[0][k], own[1][k]) for k in range(2)]
    trans[slab, 0], trans[slab, 1] = transmission(patch[0], patch[1])
    for distance in range(1, sections):
        owner = lax.rem(slab + (sections - distance), sections)
        real, imag = transmission(others[distance - 1][0], others[distance - 1][1])
        trans[owner, 0] = real
        trans[owner, 1] = imag
    for part in range(2):
        wave[0, part] = pltpu.roll(pltpu.roll(probe[part], row, 0), col, 1)
    for step in range(sections):
        a, b, c, d = wave[step, 0], wave[step, 1], trans[step, 0], trans[step, 1]
        real, imag = a * c - b * d, a * d + b * c
        if step < sections - 1:
            real, imag = two_sided(prop, real, imag)
            wave[step + 1, 0] = real
            wave[step + 1, 1] = imag
    real, imag = two_sided_transposed(dft, real, imag)
    if lower is True:
        fetch().wait()
    elif lower is not False:

        @pl.when(lower)
        def _():
            fetch().wait()

    factor = 1.0 - amplitude[...].T * lax.rsqrt(jnp.maximum(real * real + imag * imag, 0.25))
    real, minus = two_sided_transposed(dft, real * factor, -imag * factor)
    for step in range(sections - 1, -1, -1):
        a, b = wave[step, 0], wave[step, 1]
        wave[step, 0] = a * real - b * minus
        wave[step, 1] = -(a * minus + b * real)
        if step > 0:
            c, d = trans[step, 0], trans[step, 1]
            real, minus = c * real - d * minus, c * minus + d * real
            real, minus = two_sided(prop, real, minus)
    for distance in range(sections):
        outs[distance][...] = wave[lax.rem(slab + distance, sections)]


def run_slot(kind, spot, layout, tables, probe, measured, own, others, constants):
    sections, side = layout[0], layout[3]
    shape = jax.ShapeDtypeStruct((2, side, side), jnp.float32)
    return pl.pallas_call(
        lambda *refs: slot_kernel(kind, spot, layout, len(tables), *refs),
        in_specs=[SMEM] * len(tables) + [VMEM, HBM] + [VMEM] * (len(own) + len(others) + 2),
        out_specs=[VMEM] * sections,
        out_shape=[shape] * sections,
        scratch_shapes=[pltpu.VMEM((sections, 2, side, side), jnp.float32)] * 2
        + [pltpu.VMEM((side, side), jnp.float32), pltpu.SemaphoreType.DMA(())],
        compiler_params=params(32),
        name="slot_" + kind,
    )(*tables, probe, measured, *own, *others, *constants)


def cut_kernel(spots, layout, with_measured, n_tables, *refs):
    tables, (phase, absorption) = refs[:n_tables], refs[n_tables : n_tables + 2]
    refs = refs[n_tables + 2 :]
    count, side = len(spots), layout[3]
    blocks = phase.shape[2] // side
    extra = None
    if with_measured:
        sections, n_here, n_up, side = layout
        index = sections * n_here + lax.axis_index("slab") * n_up + spots[0][2]
        extra = pltpu.make_async_copy(refs[0].at[index], refs[1].at[2], refs[-3])
        refs = refs[1:]
    outs = refs[:count]
    buffer, sems = refs[-2], refs[-1]
    copies, columns = [], []
    for k in range(count):
        column = locate(spots[k], layout, tables)[2]
        first = lax.div(column, side)
        columns.append(lax.rem(column, side))
        for which, source in enumerate((phase, absorption)):
            for half in range(2):
                block = first if half == 0 else jnp.minimum(first + 1, blocks - 1)
                copies.append(
                    pltpu.make_async_copy(
                        source.at[0, :, pl.ds(pl.multiple_of(block * side, side), side)],
                        buffer.at[k, which, half],
                        sems.at[k, which, half],
                    )
                )
    for copy in copies:
        copy.start()
    if extra is not None:
        extra.start()
    lane = lax.broadcasted_iota(jnp.int32, (side, side), 1)
    for k in range(count):
        own = lane >= columns[k]
        for which in range(2):
            for half in range(2):
                copies[4 * k + 2 * which + half].wait()
            outs[k][which] = jnp.where(own, buffer[k, which, 0], buffer[k, which, 1])
    if extra is not None:
        extra.wait()


def cut(spots, layout, tables, phase, absorption, measured=None):
    side = layout[3]
    count = len(spots)
    shapes = [jax.ShapeDtypeStruct((2, side, side), jnp.float32)] * count
    scratch = [
        pltpu.VMEM((count, 2, 2, side, side), jnp.float32),
        pltpu.SemaphoreType.DMA((count, 2, 2)),
    ]
    inputs = [phase, absorption]
    if measured is not None:
        shapes = [jax.ShapeDtypeStruct((3, side, side), jnp.float32)] + shapes[1:]
        scratch = [pltpu.SemaphoreType.DMA(())] + scratch
        inputs.append(measured)
    return pl.pallas_call(
        lambda *refs: cut_kernel(spots, layout, measured is not None, len(tables), *refs),
        in_specs=[SMEM] * len(tables) + [HBM] * len(inputs),
        out_specs=[VMEM] * count,
        out_shape=shapes,
        scratch_shapes=scratch,
        compiler_params=params(16),
        name="cut",
    )(*tables, *inputs)


def join_kernel(spot, layout, *refs):
    tables, (here, there, out) = refs[:-3], refs[-3:]
    side = layout[3]
    low, high = locate(spot, layout, tables)[3:]
    rows = lax.broadcasted_iota(jnp.int32, (side, side), 0)
    keep = (rows >= low) & (rows < high)
    for part in range(2):
        out[part] = jnp.where(keep, here[part], there[part])


def join(spot, layout, tables, here, there):
    return pl.pallas_call(
        lambda *refs: join_kernel(spot, layout, *refs),
        in_specs=[SMEM] * len(tables) + [VMEM, VMEM],
        out_specs=VMEM,
        out_shape=jax.ShapeDtypeStruct(here.shape, jnp.float32),
        compiler_params=params(8),
        name="join",
    )(*tables, here, there)


def pack_kernel(*refs):
    out = refs[-1]
    for k, term in enumerate(refs[:-1]):
        out[k] = term[...]


def pack(terms):
    if len(terms) == 1:
        return terms[0][None]
    return pl.pallas_call(
        pack_kernel,
        in_specs=[VMEM] * len(terms),
        out_specs=VMEM,
        out_shape=jax.ShapeDtypeStruct((len(terms), *terms[0].shape), jnp.float32),
        compiler_params=params(8),
        name="pack",
    )(*terms)


def spread(metas, terms):
    views, kinds = [], []
    for kind, term in zip(metas, terms):
        if isinstance(kind, list):
            views += [term.at[i] for i in range(len(kind))]
            kinds += kind
        else:
            views.append(term)
            kinds.append(kind)
    return views, kinds


def spans(metas, tables, layout):
    side = layout[3]
    out = []
    for twin, spot in metas:
        index, row, col, low, high = locate(spot, layout, tables, twin)
        out.append((lax.div(col, side), lax.rem(col, side), low, high))
    return out


def early_kernel(metas, layout, *refs):
    out, copied, sem = refs[-3:]
    width = len(refs) - 3 - len(metas)
    tables, terms = refs[:width], refs[width:-3]
    terms, metas = spread(metas, terms)
    side = terms[0].shape[-1]
    blocks = out.shape[-1] // side
    rows = lax.broadcasted_iota(jnp.int32, (side, side), 0)
    lane = lax.broadcasted_iota(jnp.int32, (side, side), 1)

    @pl.loop(0, blocks)
    def _(block):
        out[:, :, pl.ds(pl.multiple_of(block * side, side), side)] = jnp.zeros((2, side, side), jnp.float32)

    for k, (first, col, low, high) in enumerate(spans(metas, tables, layout)):
        for half in range(2):
            block = first + half

            @pl.when((block < blocks) & (high > low))
            def _():
                keep = (rows >= low) & (rows < high)
                keep = keep & ((lane < col) if half else (lane >= col))
                place = pl.ds(pl.multiple_of(block * side, side), side)
                for part in range(2):
                    out[part, :, place] += jnp.where(keep, terms[k][part], 0.0)

    copy = pltpu.make_async_copy(out, copied.at[:, 0], sem)
    copy.start()
    copy.wait()


def early(metas, layout, tables, terms, cols_total):
    side = layout[3]
    return pl.pallas_call(
        lambda *refs: early_kernel(metas, layout, *refs),
        in_specs=[SMEM] * len(tables) + [VMEM] * len(terms),
        out_specs=[VMEM, HBM],
        out_shape=[
            jax.ShapeDtypeStruct((2, side, cols_total), jnp.float32),
            jax.ShapeDtypeStruct((2, 1, side, cols_total), jnp.float32),
        ],
        scratch_shapes=[pltpu.SemaphoreType.DMA(())],
        compiler_params=params(20),
        name="early",
    )(*tables, *terms)


def late_kernel(metas, layout, *refs):
    width = len(refs) - 5 - len(metas)
    tables, total, terms = refs[:width], refs[width], refs[width + 1 : -4]
    out, stage, sems = refs[-3:]
    side = terms[0].shape[-1]
    blocks = out.shape[-1] // side
    rows = lax.broadcasted_iota(jnp.int32, (side, side), 0)
    lane = lax.broadcasted_iota(jnp.int32, (side, side), 1)
    ranges = spans(metas, tables, layout)

    def place(block):
        return pl.ds(pl.multiple_of(block * side, side), side)

    def send(block):
        where = place(block)
        return pltpu.make_async_copy(stage.at[:, :, where], out.at[:, 0, :, where], sems.at[block])

    def touched(block):
        hit = jnp.bool_(False)
        for first, col, low, high in ranges:
            hit = hit | (((block == first) | (block == first + 1)) & (high > low))
        return hit

    @pl.loop(0, blocks)
    def _(block):
        @pl.when(touched(block))
        def _():
            where = place(block)
            stage[:, :, where] = total[:, :, where]
            for k, (first, col, low, high) in enumerate(ranges):
                for half in range(2):

                    @pl.when((first + half == block) & (high > low))
                    def _():
                        keep = (rows >= low) & (rows < high)
                        keep = keep & ((lane < col) if half else (lane >= col))
                        for part in range(2):
                            stage[part, :, where] += jnp.where(keep, terms[k][part], 0.0)

            send(block).start()

    @pl.loop(0, blocks)
    def _(block):
        @pl.when(touched(block))
        def _():
            send(block).wait()


def late(metas, layout, tables, total, copied, terms):
    side = layout[3]
    cols_total = total.shape[-1]
    return pl.pallas_call(
        lambda *refs: late_kernel(metas, layout, *refs),
        in_specs=[SMEM] * len(tables) + [VMEM] * (1 + len(terms)) + [HBM],
        out_specs=HBM,
        input_output_aliases={len(tables) + 1 + len(terms): 0},
        out_shape=jax.ShapeDtypeStruct((2, 1, side, cols_total), jnp.float32),
        scratch_shapes=[
            pltpu.VMEM((2, side, cols_total), jnp.float32),
            pltpu.SemaphoreType.DMA((cols_total // side,)),
        ],
        compiler_params=params(28),
        name="late",
    )(*tables, total, *terms, copied)


def local(phase, absorption, probe, measured, offsets):
    side = probe.shape[-1]
    cols_total = phase.shape[2]
    sections = lax.axis_size("slab")
    each = offsets.shape[0] // sections
    n_up = each // 2
    n_here = each - n_up
    distances = list(range(sections))

    layout = (sections, n_here, n_up, side)
    pairs = offsets.T
    if n_here == n_up:
        tables = [pairs] + [swap(pairs, "tile", parity) for parity in range(2)]
    else:
        tables = [pairs, move(pairs, "tile", 1)]
    back = lambda d: (sections - d) % sections
    far = distances[1:]
    phase = pltpu.with_memory_space_constraint(phase, pltpu.HBM)
    absorption = pltpu.with_memory_space_constraint(absorption, pltpu.HBM)
    measured = pltpu.with_memory_space_constraint(measured, pltpu.HBM)

    rounds, last_round = [], {}
    for k in range(n_here):
        if n_here == n_up:
            last_round[k] = 2 * k + (lax.axis_size("tile") - 1) % 2
            for parity in range(2):
                there = lambda value, parity=parity: swap(value, "tile", parity)
                rounds.append((k, parity, parity, there, there))
        else:
            rise = lambda value: move(value, "tile", 1)
            fall = lambda value: move(value, "tile", -1)
            if k < n_up:
                last_round[k] = len(rounds)
                rounds.append((k, "hi", "lo", rise, fall))
            rounds.append((k, "lo", "hi", fall, rise))
    count = len(rounds)
    done = [pairs]

    def step(kernel):
        out = kernel([after(pairs, *done)] + tables[1:])
        done[:] = [out[0] if isinstance(out, (list, tuple)) else out]
        return out

    spots = [("send", rounds[i][2], rounds[i][0], d) for i in range(count) for d in far]
    pieces = step(lambda p: cut(spots, layout, p, phase, absorption)) if spots else []
    sent, got = [], []
    for i, (k, role, send_role, there, home) in enumerate(rounds):
        sent.append([None, *pieces[i * len(far) : (i + 1) * len(far)]])
        got.append([None] + [there(piece) for piece in sent[i][1:]])
    for i, (k, role, send_role, there, home) in enumerate(rounds):
        extra_input = [] if role == "lo" else [measured]
        spots = [("send", send_role, k, 0)]
        sent[i][0] = step(lambda p: cut(spots, layout, p, phase, absorption, *extra_input))[0]
        got[i][0] = there(sent[i][0])
    ends = sorted(last_round)
    extra = [[rotate_last(sent[last_round[k]][d], d) for d in far] for k in ends]
    held = []
    for k, role, send_role, there, home in rounds:
        spots = [("slot", role, k, d) for d in distances]
        held.append(step(lambda p: cut(spots, layout, p, phase, absorption)))
    others = []
    for i, (k, role, send_role, there, home) in enumerate(rounds):
        joined = []
        for d in far:
            spot = ("slot", role, k, d)
            joined.append(step(lambda p: join(spot, layout, p, held[i][d], got[i][d])))
        others.append([rotate(joined[d - 1], "slab", d) for d in far])
        if i == 0:
            constants = expand(side, *done, *[value for row in extra for value in row])
            done[:] = [constants[0]]

    twin_tables = [rotate(table, "batch", 1) for table in tables]
    done += twin_tables

    def slot(kind, spot, own, rest):
        return step(
            lambda p: run_slot(kind, spot, layout, p, probe, measured, own, rest, constants)
        )

    outs, backs, homes = [], [], []
    for i, (k, role, send_role, there, home) in enumerate(rounds):
        outs.append(slot(f"{i}", ("slot", role, k, 0), [held[i][0], got[i][0]], others[i]))
        backs.append([rotate(outs[i][d], "slab", d) for d in far])
        homes.append(home(outs[i][0]))
    last_outs = [
        slot("last", ("last", "lo", k, 0), [sent[last_round[k]][0]], extra[n])
        for n, k in enumerate(ends)
    ]
    terms, kinds = [], []

    def group(items):
        values = [value for value, spot in items]
        twins = rotate(pack(values), "batch", 1)
        terms.extend(values + [twins])
        kinds.extend([(0, spot) for value, spot in items] + [[(1, spot) for value, spot in items]])
        return twins

    final, final_kinds = [], []
    ending = [
        [rotate_last(after(last_outs[n][d], *backs[-1]), d) for d in far] for n in range(len(ends))
    ]
    for n, k in enumerate(ends):
        final += [(ending[n][d - 1], ("last", "lo", k, back(d))) for d in far]
    last_items = [(last_outs[n][0], ("last", "lo", k, 0)) for n, k in enumerate(ends)]
    for i, (k, role, send_role, there, home) in enumerate(rounds):
        items = [(outs[i][0], ("slot", role, k, 0))]
        items += [(backs[i][d - 1], ("slot", role, k, back(d))) for d in far]
        items.append((homes[i], ("swap", send_role, k, 0)))
        if i == 0:
            items = last_items + items
        twins = group(items)
        for d in far:
            final.append((home(backs[i][d - 1]), ("swap", send_role, k, back(d))))
    total, copied = early(kinds, layout, tables + twin_tables, terms, cols_total)
    values = []
    for value, spot in final:
        values += [value, rotate(after(value, total), "batch", 1)]
        final_kinds += [(0, spot), (1, spot)]
    return late(final_kinds, layout, tables + twin_tables, total, copied, values)


def solution(mesh):
    in_specs = (
        P(("groups", "slab"), "tile", None),
        P(("groups", "slab"), "tile", None),
        P(),
        P(("groups", "tile", "batch"), None, None),
        P(("groups", "tile", "batch"), None),
    )
    out_specs = P(None, ("groups", "slab"), "tile", None)
    return jax.shard_map(local, mesh=mesh, in_specs=in_specs, out_specs=out_specs, check_vma=False)
```

```python
import math

import numpy as np
import jax
import jax.numpy as jnp
from jax import lax
from jax.experimental import pallas as pl
from jax.experimental.pallas import tpu as pltpu
from jax.sharding import PartitionSpec as P

SIN = [(-1.0) ** k / math.factorial(2 * k + 1) for k in range(8)]
COS = [(-1.0) ** k / math.factorial(2 * k) for k in range(8)]
VMEM = pl.BlockSpec(memory_space=pltpu.VMEM)
SMEM = pl.BlockSpec(memory_space=pltpu.SMEM)
HBM = pl.BlockSpec(memory_space=pltpu.HBM)


def params(mib):
    return pltpu.CompilerParams(vmem_limit_bytes=mib << 20)


def cost(microseconds):
    return pl.CostEstimate(flops=int(microseconds * 1e9), transcendentals=0, bytes_accessed=0)


def after(value, *others):
    return lax.optimization_barrier((value, *others))[0]


def move(block, axis, distance):
    size = lax.axis_size(axis)
    route = [(i, i + distance) for i in range(size) if 0 <= i + distance < size]
    return lax.ppermute(block, axis, route)


def rotate(block, axis, distance):
    size = lax.axis_size(axis)
    return lax.ppermute(block, axis, [(i, (i + distance) % size) for i in range(size)])


def swap(block, axis, phase):
    size = lax.axis_size(axis)
    route = []
    for lower in range(phase, size - 1, 2):
        route += [(lower, lower + 1), (lower + 1, lower)]
    return lax.ppermute(block, axis, route)


def rotate_last(block, distance):
    tiles, size = lax.axis_size("tile"), lax.axis_size("slab")
    base = (tiles - 1) * size
    route = [(base + i, base + (i + distance) % size) for i in range(size)]
    return lax.ppermute(block, ("tile", "slab"), route)


def halves(matrix):
    high = matrix.astype(np.float32).astype(jnp.bfloat16)
    low = (matrix - high.astype(np.float64)).astype(np.float32).astype(jnp.bfloat16)
    return [high, low]


def compact_tables(side):
    index = np.arange(side)
    fourier = np.exp(-2j * np.pi * (index[:, None] * index[None, :] % side) / side)
    wavenumber = np.where(index < side // 2, index, index - side)
    kernel = np.exp(-1j * np.pi * (wavenumber * wavenumber % (8 * side)) / (4 * side))
    line = np.fft.ifft(kernel)
    line = (line + line[-index % side]) / 2
    fresnel = line[(index[:, None] - index[None, :]) % side]
    scaled = fourier / math.sqrt(side)
    pieces = []
    for matrix in (fresnel, scaled):
        pieces += halves(matrix.real) + halves(matrix.imag)
    return np.stack(pieces)


def expand_kernel(pieces, *outs):
    side = pieces.shape[-1]
    for which in range(2):
        real_high, real_low, imag_high, imag_low = [pieces[4 * which + k] for k in range(4)]
        real = [real_high, real_low, real_high]
        imag = [imag_high, imag_low, imag_high]
        minus = [-imag_high, -imag_low, -imag_high]
        for column, blocks in enumerate((real + minus, imag + real)):
            for row, block in enumerate(blocks):
                outs[which][pl.ds(row * side, side), pl.ds(column * side, side)] = block


def expand(side, *gates):
    pieces = after(jnp.asarray(compact_tables(side)), *gates)
    return pl.pallas_call(
        expand_kernel,
        in_specs=[VMEM],
        out_specs=[VMEM] * 2,
        out_shape=[jax.ShapeDtypeStruct((6 * side, 2 * side), jnp.bfloat16)] * 2,
        compiler_params=params(16),
        name="expand",
    )(pieces)


def split(value):
    high = value.astype(jnp.bfloat16)
    low = (value - high.astype(jnp.float32)).astype(jnp.bfloat16)
    return high, low


def right_product(table, real, imag):
    side = real.shape[-1]
    real_high, real_low = split(real)
    imag_high, imag_low = split(imag)
    wide = jnp.concatenate([real_high, real_high, real_low, imag_high, imag_high, imag_low], axis=1)
    out = jnp.dot(wide, table[...], preferred_element_type=jnp.float32)
    return out[:, :side], out[:, side:]


def two_sided_transposed(table, real, imag):
    real, imag = right_product(table, real, imag)
    return right_product(table, real.T, imag.T)


def two_sided(table, real, imag):
    real, imag = two_sided_transposed(table, real, imag)
    return real.T, imag.T


def transmission(phase, absorption):
    square = phase * phase
    sine = jnp.full_like(phase, SIN[-1])
    cosine = jnp.full_like(phase, COS[-1])
    for a, b in zip(SIN[-2::-1], COS[-2::-1]):
        sine = sine * square + a
        cosine = cosine * square + b
    damping = jnp.exp(-absorption)
    return damping * cosine, damping * sine * phase


def is_lower(phase):
    if isinstance(phase, str):
        return phase == "lo"
    return lax.rem(lax.axis_index("tile"), 2) == phase


def pick(lower, first, second):
    if isinstance(lower, bool):
        return first if lower else second
    return jnp.where(lower, first, second)


def locate(spot, layout, tables, twin=0):
    which, phase, k, distance = spot
    sections, n_here, n_up, side = layout
    owner = lax.rem(lax.axis_index("slab") + distance, sections)
    here, up = owner * n_here + k, sections * n_here + owner * n_up + k
    width = len(tables) // 2 if len(tables) > 3 else len(tables)
    pairs = tables[width * twin]
    below = tables[width * twin + 1]
    lower = True if which == "last" else is_lower(phase)
    own, other = (here, up) if which == "slot" else (up, here)
    row = lax.rem(pick(lower, pairs[0, own], below[0, other]), side)
    col = pick(lower, pairs[1, own], below[1, other])
    low, high = pick(lower, row, jnp.int32(0)), pick(lower, jnp.int32(side), row)
    last = lax.axis_index("tile") == lax.axis_size("tile") - 1
    if which == "last":
        low = jnp.where(last, low, side)
    elif which == "swap":
        low = jnp.where(last & lower, side, low)
    return pick(lower, own, other), row, col, low, high


def slot_kernel(kind, *args):
    if kind == "last":

        @pl.when(lax.axis_index("tile") == lax.axis_size("tile") - 1)
        def _():
            slot_body(*args)
    else:
        slot_body(*args)


def slot_body(spot, layout, n_tables, *refs):
    tables, (probe, measured), refs = refs[:n_tables], refs[n_tables : n_tables + 2], refs[n_tables + 2 :]
    sections = layout[0]
    which, phase = spot[:2]
    pieces = 1 if which == "last" else 2
    own = refs[:pieces]
    others = refs[pieces : pieces + sections - 1]
    refs = refs[pieces + sections - 1 :]
    prop, dft = refs[:2]
    outs = refs[2 : 2 + sections]
    wave, trans, amplitude, sem = refs[2 + sections :]
    side = probe.shape[-1]
    slab = lax.axis_index("slab")
    index, row, col, low, high = locate(spot, layout, tables)
    col = lax.rem(col, side)
    lower = True if which == "last" else is_lower(phase)

    def fetch():
        return pltpu.make_async_copy(measured.at[index], amplitude, sem)

    if lower is True:
        fetch().start()
    elif lower is False:
        amplitude[...] = own[1][2]
    else:

        @pl.when(lower)
        def _():
            fetch().start()

        @pl.when(jnp.logical_not(lower))
        def _():
            amplitude[...] = own[1][2]

    rows = lax.broadcasted_iota(jnp.int32, (side, side), 0)
    patch = [own[0][0], own[0][1]]
    if pieces == 2:
        local_rows = (rows >= low) & (rows < high)
        patch = [jnp.where(local_rows, own[0][k], own[1][k]) for k in range(2)]
    trans[slab, 0], trans[slab, 1] = transmission(patch[0], patch[1])
    for distance in range(1, sections):
        owner = lax.rem(slab + (sections - distance), sections)
        real, imag = transmission(others[distance - 1][0], others[distance - 1][1])
        trans[owner, 0] = real
        trans[owner, 1] = imag
    for part in range(2):
        wave[0, part] = pltpu.roll(pltpu.roll(probe[part], row, 0), col, 1)
    for step in range(sections):
        a, b, c, d = wave[step, 0], wave[step, 1], trans[step, 0], trans[step, 1]
        real, imag = a * c - b * d, a * d + b * c
        if step < sections - 1:
            real, imag = two_sided(prop, real, imag)
            wave[step + 1, 0] = real
            wave[step + 1, 1] = imag
    real, imag = two_sided_transposed(dft, real, imag)
    if lower is True:
        fetch().wait()
    elif lower is not False:

        @pl.when(lower)
        def _():
            fetch().wait()

    factor = 1.0 - amplitude[...].T * lax.rsqrt(jnp.maximum(real * real + imag * imag, 0.25))
    real, minus = two_sided_transposed(dft, real * factor, -imag * factor)
    for step in range(sections - 1, -1, -1):
        a, b = wave[step, 0], wave[step, 1]
        wave[step, 0] = a * real - b * minus
        wave[step, 1] = -(a * minus + b * real)
        if step > 0:
            c, d = trans[step, 0], trans[step, 1]
            real, minus = c * real - d * minus, c * minus + d * real
            real, minus = two_sided(prop, real, minus)
    for distance in range(sections):
        outs[distance][...] = wave[lax.rem(slab + distance, sections)]


def run_slot(kind, spot, layout, tables, probe, measured, own, others, constants):
    sections, side = layout[0], layout[3]
    shape = jax.ShapeDtypeStruct((2, side, side), jnp.float32)
    return pl.pallas_call(
        lambda *refs: slot_kernel(kind, spot, layout, len(tables), *refs),
        in_specs=[SMEM] * len(tables) + [VMEM, HBM] + [VMEM] * (len(own) + len(others) + 2),
        out_specs=[VMEM] * sections,
        out_shape=[shape] * sections,
        scratch_shapes=[pltpu.VMEM((sections, 2, side, side), jnp.float32)] * 2
        + [pltpu.VMEM((side, side), jnp.float32), pltpu.SemaphoreType.DMA(())],
        compiler_params=params(32),
        name="slot_" + kind,
    )(*tables, probe, measured, *own, *others, *constants)


def cut_kernel(spots, layout, with_measured, n_tables, *refs):
    tables, (phase, absorption) = refs[:n_tables], refs[n_tables : n_tables + 2]
    refs = refs[n_tables + 2 :]
    count, side = len(spots), layout[3]
    blocks = phase.shape[2] // side
    extra = None
    if with_measured:
        sections, n_here, n_up, side = layout
        index = sections * n_here + lax.axis_index("slab") * n_up + spots[0][2]
        extra = pltpu.make_async_copy(refs[0].at[index], refs[1].at[2], refs[-3])
        refs = refs[1:]
    outs = refs[:count]
    buffer, sems = refs[-2], refs[-1]
    copies, columns = [], []
    for k in range(count):
        column = locate(spots[k], layout, tables)[2]
        first = lax.div(column, side)
        columns.append(lax.rem(column, side))
        for which, source in enumerate((phase, absorption)):
            for half in range(2):
                block = first if half == 0 else jnp.minimum(first + 1, blocks - 1)
                copies.append(
                    pltpu.make_async_copy(
                        source.at[0, :, pl.ds(pl.multiple_of(block * side, side), side)],
                        buffer.at[k, which, half],
                        sems.at[k, which, half],
                    )
                )
    for copy in copies:
        copy.start()
    if extra is not None:
        extra.start()
    lane = lax.broadcasted_iota(jnp.int32, (side, side), 1)
    for k in range(count):
        own = lane >= columns[k]
        for which in range(2):
            for half in range(2):
                copies[4 * k + 2 * which + half].wait()
            outs[k][which] = jnp.where(own, buffer[k, which, 0], buffer[k, which, 1])
    if extra is not None:
        extra.wait()


def cut(spots, layout, tables, phase, absorption, measured=None):
    side = layout[3]
    count = len(spots)
    shapes = [jax.ShapeDtypeStruct((2, side, side), jnp.float32)] * count
    scratch = [
        pltpu.VMEM((count, 2, 2, side, side), jnp.float32),
        pltpu.SemaphoreType.DMA((count, 2, 2)),
    ]
    inputs = [phase, absorption]
    if measured is not None:
        shapes = [jax.ShapeDtypeStruct((3, side, side), jnp.float32)] + shapes[1:]
        scratch = [pltpu.SemaphoreType.DMA(())] + scratch
        inputs.append(measured)
    return pl.pallas_call(
        lambda *refs: cut_kernel(spots, layout, measured is not None, len(tables), *refs),
        in_specs=[SMEM] * len(tables) + [HBM] * len(inputs),
        out_specs=[VMEM] * count,
        out_shape=shapes,
        scratch_shapes=scratch,
        compiler_params=params(16),
        name="cut",
    )(*tables, *inputs)


def join_kernel(spot, layout, *refs):
    tables, (here, there, out) = refs[:-3], refs[-3:]
    side = layout[3]
    low, high = locate(spot, layout, tables)[3:]
    rows = lax.broadcasted_iota(jnp.int32, (side, side), 0)
    keep = (rows >= low) & (rows < high)
    for part in range(2):
        out[part] = jnp.where(keep, here[part], there[part])


def join(spot, layout, tables, here, there):
    return pl.pallas_call(
        lambda *refs: join_kernel(spot, layout, *refs),
        in_specs=[SMEM] * len(tables) + [VMEM, VMEM],
        out_specs=VMEM,
        out_shape=jax.ShapeDtypeStruct(here.shape, jnp.float32),
        compiler_params=params(8),
        name="join",
    )(*tables, here, there)


def pack_kernel(*refs):
    out = refs[-1]
    for k, term in enumerate(refs[:-1]):
        out[k] = term[...]


def pack(terms):
    if len(terms) == 1:
        return terms[0][None]
    return pl.pallas_call(
        pack_kernel,
        in_specs=[VMEM] * len(terms),
        out_specs=VMEM,
        out_shape=jax.ShapeDtypeStruct((len(terms), *terms[0].shape), jnp.float32),
        compiler_params=params(8),
        name="pack",
    )(*terms)


def spread(metas, terms):
    views, kinds = [], []
    for kind, term in zip(metas, terms):
        if isinstance(kind, list):
            views += [term.at[i] for i in range(len(kind))]
            kinds += kind
        else:
            views.append(term)
            kinds.append(kind)
    return views, kinds


def spans(metas, tables, layout):
    side = layout[3]
    out = []
    for twin, spot in metas:
        index, row, col, low, high = locate(spot, layout, tables, twin)
        out.append((lax.div(col, side), lax.rem(col, side), low, high))
    return out


def early_kernel(metas, layout, *refs):
    out, copied, sem = refs[-3:]
    width = len(refs) - 3 - len(metas)
    tables, terms = refs[:width], refs[width:-3]
    terms, metas = spread(metas, terms)
    side = terms[0].shape[-1]
    blocks = out.shape[-1] // side
    rows = lax.broadcasted_iota(jnp.int32, (side, side), 0)
    lane = lax.broadcasted_iota(jnp.int32, (side, side), 1)

    @pl.loop(0, blocks)
    def _(block):
        out[:, :, pl.ds(pl.multiple_of(block * side, side), side)] = jnp.zeros((2, side, side), jnp.float32)

    for k, (first, col, low, high) in enumerate(spans(metas, tables, layout)):
        for half in range(2):
            block = first + half

            @pl.when((block < blocks) & (high > low))
            def _():
                keep = (rows >= low) & (rows < high)
                keep = keep & ((lane < col) if half else (lane >= col))
                place = pl.ds(pl.multiple_of(block * side, side), side)
                for part in range(2):
                    out[part, :, place] += jnp.where(keep, terms[k][part], 0.0)

    copy = pltpu.make_async_copy(out, copied.at[:, 0], sem)
    copy.start()
    copy.wait()


def early(metas, layout, tables, terms, cols_total):
    side = layout[3]
    return pl.pallas_call(
        lambda *refs: early_kernel(metas, layout, *refs),
        in_specs=[SMEM] * len(tables) + [VMEM] * len(terms),
        out_specs=[VMEM, HBM],
        out_shape=[
            jax.ShapeDtypeStruct((2, side, cols_total), jnp.float32),
            jax.ShapeDtypeStruct((2, 1, side, cols_total), jnp.float32),
        ],
        scratch_shapes=[pltpu.SemaphoreType.DMA(())],
        compiler_params=params(20),
        name="early",
    )(*tables, *terms)


def late_kernel(metas, layout, *refs):
    width = len(refs) - 5 - len(metas)
    tables, total, terms = refs[:width], refs[width], refs[width + 1 : -4]
    out, stage, sems = refs[-3:]
    side = terms[0].shape[-1]
    blocks = out.shape[-1] // side
    rows = lax.broadcasted_iota(jnp.int32, (side, side), 0)
    lane = lax.broadcasted_iota(jnp.int32, (side, side), 1)
    ranges = spans(metas, tables, layout)

    def place(block):
        return pl.ds(pl.multiple_of(block * side, side), side)

    def send(block):
        where = place(block)
        return pltpu.make_async_copy(stage.at[:, :, where], out.at[:, 0, :, where], sems.at[block])

    def touched(block):
        hit = jnp.bool_(False)
        for first, col, low, high in ranges:
            hit = hit | (((block == first) | (block == first + 1)) & (high > low))
        return hit

    @pl.loop(0, blocks)
    def _(block):
        @pl.when(touched(block))
        def _():
            where = place(block)
            stage[:, :, where] = total[:, :, where]
            for k, (first, col, low, high) in enumerate(ranges):
                for half in range(2):

                    @pl.when((first + half == block) & (high > low))
                    def _():
                        keep = (rows >= low) & (rows < high)
                        keep = keep & ((lane < col) if half else (lane >= col))
                        for part in range(2):
                            stage[part, :, where] += jnp.where(keep, terms[k][part], 0.0)

            send(block).start()

    @pl.loop(0, blocks)
    def _(block):
        @pl.when(touched(block))
        def _():
            send(block).wait()


def late(metas, layout, tables, total, copied, terms):
    side = layout[3]
    cols_total = total.shape[-1]
    return pl.pallas_call(
        lambda *refs: late_kernel(metas, layout, *refs),
        in_specs=[SMEM] * len(tables) + [VMEM] * (1 + len(terms)) + [HBM],
        out_specs=HBM,
        input_output_aliases={len(tables) + 1 + len(terms): 0},
        out_shape=jax.ShapeDtypeStruct((2, 1, side, cols_total), jnp.float32),
        scratch_shapes=[
            pltpu.VMEM((2, side, cols_total), jnp.float32),
            pltpu.SemaphoreType.DMA((cols_total // side,)),
        ],
        compiler_params=params(28),
        name="late",
    )(*tables, total, *terms, copied)


def local(phase, absorption, probe, measured, offsets):
    side = probe.shape[-1]
    cols_total = phase.shape[2]
    sections = lax.axis_size("slab")
    each = offsets.shape[0] // sections
    n_up = each // 2
    n_here = each - n_up
    distances = list(range(sections))

    layout = (sections, n_here, n_up, side)
    pairs = offsets.T
    tables = [pairs, move(pairs, "tile", 1)]
    back = lambda d: (sections - d) % sections
    far = distances[1:]
    phase = pltpu.with_memory_space_constraint(phase, pltpu.HBM)
    absorption = pltpu.with_memory_space_constraint(absorption, pltpu.HBM)
    measured = pltpu.with_memory_space_constraint(measured, pltpu.HBM)

    rounds, last_round = [], {}
    for k in range(n_here):
        if n_here == n_up:
            last_round[k] = 2 * k + (lax.axis_size("tile") - 1) % 2
            for parity in range(2):
                there = lambda value, parity=parity: swap(value, "tile", parity)
                rounds.append((k, parity, parity, there, there))
        else:
            rise = lambda value: move(value, "tile", 1)
            fall = lambda value: move(value, "tile", -1)
            if k < n_up:
                last_round[k] = len(rounds)
                rounds.append((k, "hi", "lo", rise, fall))
            rounds.append((k, "lo", "hi", fall, rise))
    count = len(rounds)
    done = [pairs]

    def step(kernel):
        out = kernel([after(pairs, *done)] + tables[1:])
        done[:] = [out[0] if isinstance(out, (list, tuple)) else out]
        return out

    spots = [("send", rounds[i][2], rounds[i][0], d) for i in range(count) for d in far]
    pieces = step(lambda p: cut(spots, layout, p, phase, absorption)) if spots else []
    sent, got = [], []
    for i, (k, role, send_role, there, home) in enumerate(rounds):
        sent.append([None, *pieces[i * len(far) : (i + 1) * len(far)]])
        got.append([None] + [there(piece) for piece in sent[i][1:]])
    for i, (k, role, send_role, there, home) in enumerate(rounds):
        extra_input = [] if role == "lo" else [measured]
        spots = [("send", send_role, k, 0)]
        sent[i][0] = step(lambda p: cut(spots, layout, p, phase, absorption, *extra_input))[0]
        got[i][0] = there(sent[i][0])
    ends = sorted(last_round)
    extra = [[rotate_last(sent[last_round[k]][d], d) for d in far] for k in ends]
    held = []
    for k, role, send_role, there, home in rounds:
        spots = [("slot", role, k, d) for d in distances]
        held.append(step(lambda p: cut(spots, layout, p, phase, absorption)))
    others = []
    for i, (k, role, send_role, there, home) in enumerate(rounds):
        joined = []
        for d in far:
            spot = ("slot", role, k, d)
            joined.append(step(lambda p: join(spot, layout, p, held[i][d], got[i][d])))
        others.append([rotate(joined[d - 1], "slab", d) for d in far])
        if i == 0:
            constants = expand(side, *done, *[value for row in extra for value in row])
            done[:] = [constants[0]]

    twin_tables = [rotate(table, "batch", 1) for table in tables]
    done += twin_tables

    def slot(kind, spot, own, rest):
        return step(
            lambda p: run_slot(kind, spot, layout, p, probe, measured, own, rest, constants)
        )

    outs, backs, homes = [], [], []
    for i, (k, role, send_role, there, home) in enumerate(rounds):
        outs.append(slot(f"{i}", ("slot", role, k, 0), [held[i][0], got[i][0]], others[i]))
        backs.append([rotate(outs[i][d], "slab", d) for d in far])
        homes.append(home(outs[i][0]))
    last_outs = [
        slot("last", ("last", "lo", k, 0), [sent[last_round[k]][0]], extra[n])
        for n, k in enumerate(ends)
    ]
    terms, kinds = [], []

    def group(items):
        values = [value for value, spot in items]
        twins = rotate(pack(values), "batch", 1)
        terms.extend(values + [twins])
        kinds.extend([(0, spot) for value, spot in items] + [[(1, spot) for value, spot in items]])
        return twins

    final, final_kinds = [], []
    ending = [
        [rotate_last(after(last_outs[n][d], *backs[-1]), d) for d in far] for n in range(len(ends))
    ]
    for n, k in enumerate(ends):
        final += [(ending[n][d - 1], ("last", "lo", k, back(d))) for d in far]
    last_items = [(last_outs[n][0], ("last", "lo", k, 0)) for n, k in enumerate(ends)]
    for i, (k, role, send_role, there, home) in enumerate(rounds):
        items = [(outs[i][0], ("slot", role, k, 0))]
        items += [(backs[i][d - 1], ("slot", role, k, back(d))) for d in far]
        items.append((homes[i], ("swap", send_role, k, 0)))
        if i == 0:
            items = last_items + items
        twins = group(items)
        for d in far:
            final.append((home(backs[i][d - 1]), ("swap", send_role, k, back(d))))
    total, copied = early(kinds, layout, tables + twin_tables, terms, cols_total)
    values = []
    for value, spot in final:
        values += [value, rotate(after(value, total), "batch", 1)]
        final_kinds += [(0, spot), (1, spot)]
    return late(final_kinds, layout, tables + twin_tables, total, copied, values)


def solution(mesh):
    in_specs = (
        P(("groups", "slab"), "tile", None),
        P(("groups", "slab"), "tile", None),
        P(),
        P(("groups", "tile", "batch"), None, None),
        P(("groups", "tile", "batch"), None),
    )
    out_specs = P(None, ("groups", "slab"), "tile", None)
    return jax.shard_map(local, mesh=mesh, in_specs=in_specs, out_specs=out_specs, check_vma=False)
```

```python
import math

import numpy as np
import jax
import jax.numpy as jnp
from jax import lax
from jax.experimental import pallas as pl
from jax.experimental.pallas import tpu as pltpu
from jax.sharding import PartitionSpec as P

SIN = [(-1.0) ** k / math.factorial(2 * k + 1) for k in range(8)]
COS = [(-1.0) ** k / math.factorial(2 * k) for k in range(8)]
VMEM = pl.BlockSpec(memory_space=pltpu.VMEM)
SMEM = pl.BlockSpec(memory_space=pltpu.SMEM)
HBM = pl.BlockSpec(memory_space=pltpu.HBM)


def params(mib):
    return pltpu.CompilerParams(vmem_limit_bytes=mib << 20)


def cost(microseconds):
    return pl.CostEstimate(flops=int(microseconds * 1e9), transcendentals=0, bytes_accessed=0)


def after(value, *others):
    return lax.optimization_barrier((value, *others))[0]


def move(block, axis, distance):
    size = lax.axis_size(axis)
    route = [(i, i + distance) for i in range(size) if 0 <= i + distance < size]
    return lax.ppermute(block, axis, route)


def rotate(block, axis, distance):
    size = lax.axis_size(axis)
    return lax.ppermute(block, axis, [(i, (i + distance) % size) for i in range(size)])


def swap(block, axis, phase):
    size = lax.axis_size(axis)
    route = []
    for lower in range(phase, size - 1, 2):
        route += [(lower, lower + 1), (lower + 1, lower)]
    return lax.ppermute(block, axis, route)


def rotate_last(block, distance):
    tiles, size = lax.axis_size("tile"), lax.axis_size("slab")
    base = (tiles - 1) * size
    route = [(base + i, base + (i + distance) % size) for i in range(size)]
    return lax.ppermute(block, ("tile", "slab"), route)


def halves(matrix):
    high = matrix.astype(np.float32).astype(jnp.bfloat16)
    low = (matrix - high.astype(np.float64)).astype(np.float32).astype(jnp.bfloat16)
    return [high, low]


def compact_tables(side):
    index = np.arange(side)
    fourier = np.exp(-2j * np.pi * (index[:, None] * index[None, :] % side) / side)
    wavenumber = np.where(index < side // 2, index, index - side)
    kernel = np.exp(-1j * np.pi * (wavenumber * wavenumber % (8 * side)) / (4 * side))
    line = np.fft.ifft(kernel)
    line = (line + line[-index % side]) / 2
    fresnel = line[(index[:, None] - index[None, :]) % side]
    scaled = fourier / math.sqrt(side)
    pieces = []
    for matrix in (fresnel, scaled):
        pieces += halves(matrix.real) + halves(matrix.imag)
    return np.stack(pieces)


def expand_kernel(pieces, *outs):
    side = pieces.shape[-1]
    for which in range(2):
        real_high, real_low, imag_high, imag_low = [pieces[4 * which + k] for k in range(4)]
        real = [real_high, real_low, real_high]
        imag = [imag_high, imag_low, imag_high]
        minus = [-imag_high, -imag_low, -imag_high]
        for column, blocks in enumerate((real + minus, imag + real)):
            for row, block in enumerate(blocks):
                outs[which][pl.ds(row * side, side), pl.ds(column * side, side)] = block


def expand(side, *gates):
    pieces = after(jnp.asarray(compact_tables(side)), *gates)
    return pl.pallas_call(
        expand_kernel,
        in_specs=[VMEM],
        out_specs=[VMEM] * 2,
        out_shape=[jax.ShapeDtypeStruct((6 * side, 2 * side), jnp.bfloat16)] * 2,
        compiler_params=params(16),
        name="expand",
    )(pieces)


def split(value):
    high = value.astype(jnp.bfloat16)
    low = (value - high.astype(jnp.float32)).astype(jnp.bfloat16)
    return high, low


def right_product(table, real, imag):
    side = real.shape[-1]
    real_high, real_low = split(real)
    imag_high, imag_low = split(imag)
    wide = jnp.concatenate([real_high, real_high, real_low, imag_high, imag_high, imag_low], axis=1)
    out = jnp.dot(wide, table[...], preferred_element_type=jnp.float32)
    return out[:, :side], out[:, side:]


def two_sided_transposed(table, real, imag):
    real, imag = right_product(table, real, imag)
    return right_product(table, real.T, imag.T)


def two_sided(table, real, imag):
    real, imag = two_sided_transposed(table, real, imag)
    return real.T, imag.T


def transmission(phase, absorption):
    square = phase * phase
    sine = jnp.full_like(phase, SIN[-1])
    cosine = jnp.full_like(phase, COS[-1])
    for a, b in zip(SIN[-2::-1], COS[-2::-1]):
        sine = sine * square + a
        cosine = cosine * square + b
    damping = jnp.exp(-absorption)
    return damping * cosine, damping * sine * phase


def is_lower(phase):
    if isinstance(phase, str):
        return phase == "lo"
    return lax.rem(lax.axis_index("tile"), 2) == phase


def pick(lower, first, second):
    if isinstance(lower, bool):
        return first if lower else second
    return jnp.where(lower, first, second)


def locate(spot, layout, tables, twin=0):
    which, phase, k, distance = spot
    sections, n_here, n_up, side = layout
    owner = lax.rem(lax.axis_index("slab") + distance, sections)
    here, up = owner * n_here + k, sections * n_here + owner * n_up + k
    width = len(tables) // 2 if len(tables) > 3 else len(tables)
    pairs = tables[width * twin]
    below = tables[width * twin + 1 + (0 if isinstance(phase, str) else phase)]
    lower = True if which == "last" else is_lower(phase)
    own, other = (here, up) if which == "slot" else (up, here)
    row = lax.rem(pick(lower, pairs[0, own], below[0, other]), side)
    col = pick(lower, pairs[1, own], below[1, other])
    low, high = pick(lower, row, jnp.int32(0)), pick(lower, jnp.int32(side), row)
    last = lax.axis_index("tile") == lax.axis_size("tile") - 1
    if which == "last":
        low = jnp.where(last, low, side)
    elif which == "swap":
        low = jnp.where(last & lower, side, low)
    return pick(lower, own, other), row, col, low, high


def slot_kernel(kind, *args):
    if kind == "last":

        @pl.when(lax.axis_index("tile") == lax.axis_size("tile") - 1)
        def _():
            slot_body(*args)
    else:
        slot_body(*args)


def slot_body(spot, layout, n_tables, *refs):
    tables, (probe, measured), refs = refs[:n_tables], refs[n_tables : n_tables + 2], refs[n_tables + 2 :]
    sections = layout[0]
    which, phase = spot[:2]
    pieces = 1 if which == "last" else 2
    own = refs[:pieces]
    others = refs[pieces : pieces + sections - 1]
    refs = refs[pieces + sections - 1 :]
    prop, dft = refs[:2]
    outs = refs[2 : 2 + sections]
    wave, trans, amplitude, sem = refs[2 + sections :]
    side = probe.shape[-1]
    slab = lax.axis_index("slab")
    index, row, col, low, high = locate(spot, layout, tables)
    col = lax.rem(col, side)
    lower = True if which == "last" else is_lower(phase)

    def fetch():
        return pltpu.make_async_copy(measured.at[index], amplitude, sem)

    if lower is True:
        fetch().start()
    elif lower is False:
        amplitude[...] = own[1][2]
    else:

        @pl.when(lower)
        def _():
            fetch().start()

        @pl.when(jnp.logical_not(lower))
        def _():
            amplitude[...] = own[1][2]

    rows = lax.broadcasted_iota(jnp.int32, (side, side), 0)
    patch = [own[0][0], own[0][1]]
    if pieces == 2:
        local_rows = (rows >= low) & (rows < high)
        patch = [jnp.where(local_rows, own[0][k], own[1][k]) for k in range(2)]
    trans[slab, 0], trans[slab, 1] = transmission(patch[0], patch[1])
    for distance in range(1, sections):
        owner = lax.rem(slab + (sections - distance), sections)
        real, imag = transmission(others[distance - 1][0], others[distance - 1][1])
        trans[owner, 0] = real
        trans[owner, 1] = imag
    for part in range(2):
        wave[0, part] = pltpu.roll(pltpu.roll(probe[part], row, 0), col, 1)
    for step in range(sections):
        a, b, c, d = wave[step, 0], wave[step, 1], trans[step, 0], trans[step, 1]
        real, imag = a * c - b * d, a * d + b * c
        if step < sections - 1:
            real, imag = two_sided(prop, real, imag)
            wave[step + 1, 0] = real
            wave[step + 1, 1] = imag
    real, imag = two_sided_transposed(dft, real, imag)
    if lower is True:
        fetch().wait()
    elif lower is not False:

        @pl.when(lower)
        def _():
            fetch().wait()

    factor = 1.0 - amplitude[...].T * lax.rsqrt(jnp.maximum(real * real + imag * imag, 0.25))
    real, minus = two_sided_transposed(dft, real * factor, -imag * factor)
    for step in range(sections - 1, -1, -1):
        a, b = wave[step, 0], wave[step, 1]
        wave[step, 0] = a * real - b * minus
        wave[step, 1] = -(a * minus + b * real)
        if step > 0:
            c, d = trans[step, 0], trans[step, 1]
            real, minus = c * real - d * minus, c * minus + d * real
            real, minus = two_sided(prop, real, minus)
    for distance in range(sections):
        outs[distance][...] = wave[lax.rem(slab + distance, sections)]


def run_slot(kind, spot, layout, tables, probe, measured, own, others, constants):
    sections, side = layout[0], layout[3]
    shape = jax.ShapeDtypeStruct((2, side, side), jnp.float32)
    return pl.pallas_call(
        lambda *refs: slot_kernel(kind, spot, layout, len(tables), *refs),
        in_specs=[SMEM] * len(tables) + [VMEM, HBM] + [VMEM] * (len(own) + len(others) + 2),
        out_specs=[VMEM] * sections,
        out_shape=[shape] * sections,
        scratch_shapes=[pltpu.VMEM((sections, 2, side, side), jnp.float32)] * 2
        + [pltpu.VMEM((side, side), jnp.float32), pltpu.SemaphoreType.DMA(())],
        compiler_params=params(32),
        name="slot_" + kind,
    )(*tables, probe, measured, *own, *others, *constants)


def cut_kernel(spots, layout, with_measured, n_tables, *refs):
    tables, (phase, absorption) = refs[:n_tables], refs[n_tables : n_tables + 2]
    refs = refs[n_tables + 2 :]
    count, side = len(spots), layout[3]
    blocks = phase.shape[2] // side
    extra = None
    if with_measured:
        sections, n_here, n_up, side = layout
        index = sections * n_here + lax.axis_index("slab") * n_up + spots[0][2]
        extra = pltpu.make_async_copy(refs[0].at[index], refs[1].at[2], refs[-3])
        refs = refs[1:]
    outs = refs[:count]
    buffer, sems = refs[-2], refs[-1]
    copies, columns = [], []
    for k in range(count):
        column = locate(spots[k], layout, tables)[2]
        first = lax.div(column, side)
        columns.append(lax.rem(column, side))
        for which, source in enumerate((phase, absorption)):
            for half in range(2):
                block = first if half == 0 else jnp.minimum(first + 1, blocks - 1)
                copies.append(
                    pltpu.make_async_copy(
                        source.at[0, :, pl.ds(pl.multiple_of(block * side, side), side)],
                        buffer.at[k, which, half],
                        sems.at[k, which, half],
                    )
                )
    for copy in copies:
        copy.start()
    if extra is not None:
        extra.start()
    lane = lax.broadcasted_iota(jnp.int32, (side, side), 1)
    for k in range(count):
        own = lane >= columns[k]
        for which in range(2):
            for half in range(2):
                copies[4 * k + 2 * which + half].wait()
            outs[k][which] = jnp.where(own, buffer[k, which, 0], buffer[k, which, 1])
    if extra is not None:
        extra.wait()


def cut(spots, layout, tables, phase, absorption, measured=None):
    side = layout[3]
    count = len(spots)
    shapes = [jax.ShapeDtypeStruct((2, side, side), jnp.float32)] * count
    scratch = [
        pltpu.VMEM((count, 2, 2, side, side), jnp.float32),
        pltpu.SemaphoreType.DMA((count, 2, 2)),
    ]
    inputs = [phase, absorption]
    if measured is not None:
        shapes = [jax.ShapeDtypeStruct((3, side, side), jnp.float32)] + shapes[1:]
        scratch = [pltpu.SemaphoreType.DMA(())] + scratch
        inputs.append(measured)
    return pl.pallas_call(
        lambda *refs: cut_kernel(spots, layout, measured is not None, len(tables), *refs),
        in_specs=[SMEM] * len(tables) + [HBM] * len(inputs),
        out_specs=[VMEM] * count,
        out_shape=shapes,
        scratch_shapes=scratch,
        compiler_params=params(16),
        name="cut",
    )(*tables, *inputs)


def join_kernel(spot, layout, *refs):
    tables, (here, there, out) = refs[:-3], refs[-3:]
    side = layout[3]
    low, high = locate(spot, layout, tables)[3:]
    rows = lax.broadcasted_iota(jnp.int32, (side, side), 0)
    keep = (rows >= low) & (rows < high)
    for part in range(2):
        out[part] = jnp.where(keep, here[part], there[part])


def join(spot, layout, tables, here, there):
    return pl.pallas_call(
        lambda *refs: join_kernel(spot, layout, *refs),
        in_specs=[SMEM] * len(tables) + [VMEM, VMEM],
        out_specs=VMEM,
        out_shape=jax.ShapeDtypeStruct(here.shape, jnp.float32),
        compiler_params=params(8),
        name="join",
    )(*tables, here, there)


def pack_kernel(*refs):
    out = refs[-1]
    for k, term in enumerate(refs[:-1]):
        out[k] = term[...]


def pack(terms):
    if len(terms) == 1:
        return terms[0][None]
    return pl.pallas_call(
        pack_kernel,
        in_specs=[VMEM] * len(terms),
        out_specs=VMEM,
        out_shape=jax.ShapeDtypeStruct((len(terms), *terms[0].shape), jnp.float32),
        compiler_params=params(8),
        name="pack",
    )(*terms)


def spread(metas, terms):
    views, kinds = [], []
    for kind, term in zip(metas, terms):
        if isinstance(kind, list):
            views += [term.at[i] for i in range(len(kind))]
            kinds += kind
        else:
            views.append(term)
            kinds.append(kind)
    return views, kinds


def spans(metas, tables, layout):
    side = layout[3]
    out = []
    for twin, spot in metas:
        index, row, col, low, high = locate(spot, layout, tables, twin)
        out.append((lax.div(col, side), lax.rem(col, side), low, high))
    return out


def early_kernel(metas, layout, *refs):
    out, copied, sem = refs[-3:]
    width = len(refs) - 3 - len(metas)
    tables, terms = refs[:width], refs[width:-3]
    terms, metas = spread(metas, terms)
    side = terms[0].shape[-1]
    blocks = out.shape[-1] // side
    rows = lax.broadcasted_iota(jnp.int32, (side, side), 0)
    lane = lax.broadcasted_iota(jnp.int32, (side, side), 1)

    @pl.loop(0, blocks)
    def _(block):
        out[:, :, pl.ds(pl.multiple_of(block * side, side), side)] = jnp.zeros((2, side, side), jnp.float32)

    for k, (first, col, low, high) in enumerate(spans(metas, tables, layout)):
        for half in range(2):
            block = first + half

            @pl.when((block < blocks) & (high > low))
            def _():
                keep = (rows >= low) & (rows < high)
                keep = keep & ((lane < col) if half else (lane >= col))
                place = pl.ds(pl.multiple_of(block * side, side), side)
                for part in range(2):
                    out[part, :, place] += jnp.where(keep, terms[k][part], 0.0)

    copy = pltpu.make_async_copy(out, copied.at[:, 0], sem)
    copy.start()
    copy.wait()


def early(metas, layout, tables, terms, cols_total):
    side = layout[3]
    return pl.pallas_call(
        lambda *refs: early_kernel(metas, layout, *refs),
        in_specs=[SMEM] * len(tables) + [VMEM] * len(terms),
        out_specs=[VMEM, HBM],
        out_shape=[
            jax.ShapeDtypeStruct((2, side, cols_total), jnp.float32),
            jax.ShapeDtypeStruct((2, 1, side, cols_total), jnp.float32),
        ],
        scratch_shapes=[pltpu.SemaphoreType.DMA(())],
        compiler_params=params(20),
        name="early",
    )(*tables, *terms)


def late_kernel(metas, layout, *refs):
    width = len(refs) - 5 - len(metas)
    tables, total, terms = refs[:width], refs[width], refs[width + 1 : -4]
    out, stage, sems = refs[-3:]
    side = terms[0].shape[-1]
    blocks = out.shape[-1] // side
    rows = lax.broadcasted_iota(jnp.int32, (side, side), 0)
    lane = lax.broadcasted_iota(jnp.int32, (side, side), 1)
    ranges = spans(metas, tables, layout)

    def place(block):
        return pl.ds(pl.multiple_of(block * side, side), side)

    def send(block):
        where = place(block)
        return pltpu.make_async_copy(stage.at[:, :, where], out.at[:, 0, :, where], sems.at[block])

    def touched(block):
        hit = jnp.bool_(False)
        for first, col, low, high in ranges:
            hit = hit | (((block == first) | (block == first + 1)) & (high > low))
        return hit

    @pl.loop(0, blocks)
    def _(block):
        @pl.when(touched(block))
        def _():
            where = place(block)
            stage[:, :, where] = total[:, :, where]
            for k, (first, col, low, high) in enumerate(ranges):
                for half in range(2):

                    @pl.when((first + half == block) & (high > low))
                    def _():
                        keep = (rows >= low) & (rows < high)
                        keep = keep & ((lane < col) if half else (lane >= col))
                        for part in range(2):
                            stage[part, :, where] += jnp.where(keep, terms[k][part], 0.0)

            send(block).start()

    @pl.loop(0, blocks)
    def _(block):
        @pl.when(touched(block))
        def _():
            send(block).wait()


def late(metas, layout, tables, total, copied, terms):
    side = layout[3]
    cols_total = total.shape[-1]
    return pl.pallas_call(
        lambda *refs: late_kernel(metas, layout, *refs),
        in_specs=[SMEM] * len(tables) + [VMEM] * (1 + len(terms)) + [HBM],
        out_specs=HBM,
        input_output_aliases={len(tables) + 1 + len(terms): 0},
        out_shape=jax.ShapeDtypeStruct((2, 1, side, cols_total), jnp.float32),
        scratch_shapes=[
            pltpu.VMEM((2, side, cols_total), jnp.float32),
            pltpu.SemaphoreType.DMA((cols_total // side,)),
        ],
        compiler_params=params(28),
        name="late",
    )(*tables, total, *terms, copied)


def local(phase, absorption, probe, measured, offsets):
    side = probe.shape[-1]
    cols_total = phase.shape[2]
    sections = lax.axis_size("slab")
    each = offsets.shape[0] // sections
    n_up = each // 2
    n_here = each - n_up
    distances = list(range(sections))

    layout = (sections, n_here, n_up, side)
    pairs = offsets.T
    if n_here == n_up:
        tables = [pairs] + [swap(pairs, "tile", parity) for parity in range(2)]
    else:
        tables = [pairs, move(pairs, "tile", 1)]
    back = lambda d: (sections - d) % sections
    far = distances[1:]
    phase = pltpu.with_memory_space_constraint(phase, pltpu.HBM)
    absorption = pltpu.with_memory_space_constraint(absorption, pltpu.HBM)
    measured = pltpu.with_memory_space_constraint(measured, pltpu.HBM)

    rounds, last_round = [], {}
    for k in range(n_here):
        if n_here == n_up:
            last_round[k] = 2 * k + (lax.axis_size("tile") - 1) % 2
            for parity in range(2):
                there = lambda value, parity=parity: swap(value, "tile", parity)
                rounds.append((k, parity, parity, there, there))
        else:
            rise = lambda value: move(value, "tile", 1)
            fall = lambda value: move(value, "tile", -1)
            if k < n_up:
                last_round[k] = len(rounds)
                rounds.append((k, "hi", "lo", rise, fall))
            rounds.append((k, "lo", "hi", fall, rise))
    count = len(rounds)
    done = [pairs]

    def step(kernel):
        out = kernel([after(pairs, *done)] + tables[1:])
        done[:] = [out[0] if isinstance(out, (list, tuple)) else out]
        return out

    spots = [("send", rounds[i][2], rounds[i][0], d) for i in range(count) for d in far]
    pieces = step(lambda p: cut(spots, layout, p, phase, absorption)) if spots else []
    sent, got = [], []
    for i, (k, role, send_role, there, home) in enumerate(rounds):
        sent.append([None, *pieces[i * len(far) : (i + 1) * len(far)]])
        got.append([None] + [there(piece) for piece in sent[i][1:]])
    for i, (k, role, send_role, there, home) in enumerate(rounds):
        extra_input = [] if role == "lo" else [measured]
        spots = [("send", send_role, k, 0)]
        sent[i][0] = step(lambda p: cut(spots, layout, p, phase, absorption, *extra_input))[0]
        got[i][0] = there(sent[i][0])
    ends = sorted(last_round)
    extra = [[rotate_last(sent[last_round[k]][d], d) for d in far] for k in ends]
    held = []
    for k, role, send_role, there, home in rounds:
        spots = [("slot", role, k, d) for d in distances]
        held.append(step(lambda p: cut(spots, layout, p, phase, absorption)))
    others = []
    for i, (k, role, send_role, there, home) in enumerate(rounds):
        joined = []
        for d in far:
            spot = ("slot", role, k, d)
            joined.append(step(lambda p: join(spot, layout, p, held[i][d], got[i][d])))
        others.append([rotate(joined[d - 1], "slab", d) for d in far])
        if i == 0:
            constants = expand(side, *done, *[value for row in extra for value in row])
            done[:] = [constants[0]]

    twin_tables = [rotate(table, "batch", 1) for table in tables]
    done += twin_tables

    def slot(kind, spot, own, rest):
        return step(
            lambda p: run_slot(kind, spot, layout, p, probe, measured, own, rest, constants)
        )

    outs, backs, homes = [], [], []
    for i, (k, role, send_role, there, home) in enumerate(rounds):
        outs.append(slot(f"{i}", ("slot", role, k, 0), [held[i][0], got[i][0]], others[i]))
        backs.append([rotate(outs[i][d], "slab", d) for d in far])
        homes.append(home(outs[i][0]))
    last_outs = [
        slot("last", ("last", "lo", k, 0), [sent[last_round[k]][0]], extra[n])
        for n, k in enumerate(ends)
    ]
    terms, kinds = [], []

    def group(items):
        values = [value for value, spot in items]
        twins = rotate(pack(values), "batch", 1)
        terms.extend(values + [twins])
        kinds.extend([(0, spot) for value, spot in items] + [[(1, spot) for value, spot in items]])
        return twins

    final, final_kinds = [], []
    ending = [
        [rotate_last(after(last_outs[n][d], *backs[-1]), d) for d in far] for n in range(len(ends))
    ]
    last_items = [(last_outs[n][0], ("last", "lo", k, 0)) for n, k in enumerate(ends)]
    for i, (k, role, send_role, there, home) in enumerate(rounds):
        items = [(outs[i][0], ("slot", role, k, 0))]
        items += [(backs[i][d - 1], ("slot", role, k, back(d))) for d in far]
        items.append((homes[i], ("swap", send_role, k, 0)))
        if i == 0:
            items = last_items + items
        twins = group(items)
        for d in far:
            final.append((home(backs[i][d - 1]), ("swap", send_role, k, back(d))))
        if i == 0:
            for n, k in enumerate(ends):
                final += [(ending[n][d - 1], ("last", "lo", k, back(d))) for d in far]
    total, copied = early(kinds, layout, tables + twin_tables, terms, cols_total)
    values = []
    for value, spot in final:
        values += [value, rotate(after(value, total), "batch", 1)]
        final_kinds += [(0, spot), (1, spot)]
    return late(final_kinds, layout, tables + twin_tables, total, copied, values)


def solution(mesh):
    in_specs = (
        P(("groups", "slab"), "tile", None),
        P(("groups", "slab"), "tile", None),
        P(),
        P(("groups", "tile", "batch"), None, None),
        P(("groups", "tile", "batch"), None),
    )
    out_specs = P(None, ("groups", "slab"), "tile", None)
    return jax.shard_map(local, mesh=mesh, in_specs=in_specs, out_specs=out_specs, check_vma=False)
```
